32 devices in a mesh: shard: 2 (over core), dp: 16 (over z, y, x).
Axes of the slice: x: 2, y: 2, z: 4, core: 2. Of those that a mesh axis runs over, the one named last changes fastest.
Arguments:
- content: bfloat16 [2, 2048, 768], P(None, ('shard', 'dp')), may hold values from -6 to 6
- query_state: bfloat16 [2, 2048, 768], P(None, ('shard', 'dp')), may hold values from -6 to 6
- token_seg: int32 [2, 2048], P(None, ('shard', 'dp')), may hold values from 0 to 12, as said below
- positions: int32 [2, 2048], P(None, ('shard', 'dp')), may hold values from 0 to 383, as said below
- parent: int32 [2, 2, 13], P(None, 'shard'), may hold values from 0 to 4, as said below
- w_query: bfloat16 [768, 768], P('shard'), may hold values from -0.21875 to 0.21875
- w_key: bfloat16 [768, 768], P('shard'), may hold values from -0.21875 to 0.21875
- w_value: bfloat16 [768, 768], P('shard'), may hold values from -0.21875 to 0.21875
- w_out: bfloat16 [768, 768], P('shard'), may hold values from -0.875 to 0.875
- w_inner: bfloat16 [768, 3072], P('shard'), may hold values from -0.21875 to 0.21875
- w_outer: bfloat16 [3072, 768], P('shard'), may hold values from -0.109375 to 0.109375
- b_inner: bfloat16 [3072], P('shard'), may hold values from -1.75 to 1.75
- b_outer: bfloat16 [768], P('shard'), may hold values from -1.75 to 1.75
- gain_attn: bfloat16 [768], P('shard'), may hold values from 0.5 to 1.5
- bias_attn: bfloat16 [768], P('shard'), may hold values from -1.75 to 1.75
- gain_ffn: bfloat16 [768], P('shard'), may hold values from 0.5 to 1.5
- bias_ffn: bfloat16 [768], P('shard'), may hold values from -1.75 to 1.75
- bias_content: bfloat16 [768], P('shard'), may hold values from -3 to 3
- bias_segment: bfloat16 [768], P('shard'), may hold values from -3 to 3
- seg_embed: bfloat16 [2, 768], P(None, 'shard'), may hold values from -6 to 6
- rel_table: bfloat16 [16, 12], P('shard'), may hold values from -4 to 4
- cot_content: bfloat16 [2, 2048, 768], P(None, ('shard', 'dp')), may hold values from -6 to 6
- cot_query: bfloat16 [2, 2048, 768], P(None, ('shard', 'dp')), may hold values from -6 to 6
Outputs:
- out_content: bfloat16 [2, 2048, 768], P(None, ('shard', 'dp'))
- out_query: bfloat16 [2, 2048, 768], P(None, ('shard', 'dp'))
- grad_content: float32 [2, 2048, 768], P(None, ('shard', 'dp'))
- grad_query: float32 [2, 2048, 768], P(None, ('shard', 'dp'))
- grad_w_query: float32 [768, 768], P('shard')
- grad_w_key: float32 [768, 768], P('shard')
- grad_w_value: float32 [768, 768], P('shard')
- grad_w_out: float32 [768, 768], P('shard')
- grad_w_inner: float32 [768, 3072], P('shard')
- grad_w_outer: float32 [3072, 768], P('shard')
- grad_b_inner: float32 [3072], P('shard')
- grad_b_outer: float32 [768], P('shard')
- grad_gain_attn: float32 [768], P('shard')
- grad_bias_attn: float32 [768], P('shard')
- grad_gain_ffn: float32 [768], P('shard')
- grad_bias_ffn: float32 [768], P('shard')
- grad_bias_content: float32 [768], P('shard')
- grad_bias_segment: float32 [768], P('shard')
- grad_seg_embed: float32 [2, 768], P(None, 'shard')
- grad_rel_table: float32 [16, 12], P('shard')
The draws below stay inside these ranges and needn't reach their ends.
Inputs may be any that keep to these rules, and one draw needn't show every extreme that they name: `token_seg`: each tree's 1024 tokens fall in 16 runs of 64 tokens; four runs carry segment 0 (the trunk), one run each carries segments 1 to 4 (branches) and 5 to 12 (leaves). Which run carries which segment is drawn for each tree. The trunk's runs hold positions 0 to 255, run after run in an order drawn for each tree; a branch's run holds 256 to 319 and a leaf's 5 * 64 to 383; positions rise by one along a run. Entry s is the parent segment of segment s: 0 for segment 0 and for the branches 1 to 4; each branch is the parent of exactly two leaves.
All inputs are finite; a program needn't handle non-finite values.
Results may differ from the reference program's by a relative error of at most 0.029.
Values may be sent and summed in bfloat16 or wider, within the bound.
No kernel may reach another device: no remote copies, remote signals or barrier semaphores. Data moves between devices by JAX's collectives and lax.ppermute only.
A program may use at most 192 MiB of HBM per device.

```python
import jax
import jax.numpy as jnp
from jax import lax

D = 768
HEADS = 12
HEAD = 64
FF = 3072
REL = 16
MICRO = 2
TREE = 1024
SEG = 64
TREES = 2
TOKENS = 2048


def tree_layout(key):
    tree_total = MICRO * TREES
    tree_keys = jax.random.split(jax.random.fold_in(key, 101), tree_total)
    unit_order = jax.vmap(lambda element: jax.random.permutation(element, 16))(tree_keys).astype(jnp.int32)
    segment = jnp.where(unit_order < 4, 0, unit_order - 3)
    start_pos = jnp.where(unit_order < 4, unit_order * SEG, jnp.where(unit_order < 8, 4 * SEG, 5 * SEG))
    offset = jnp.arange(SEG, dtype=jnp.int32)
    seg_tokens = jnp.repeat(segment, SEG, axis=1, total_repeat_length=TREE)
    pos_tokens = (start_pos[:, :, None] + offset[None, None, :]).reshape(tree_total, TREE)
    return (seg_tokens.reshape(MICRO, TOKENS), pos_tokens.reshape(MICRO, TOKENS))


def draw_token_seg(key, part):
    return tree_layout(key)[0]


def draw_positions(key, part):
    return tree_layout(key)[1]


def draw_parent(key, part):
    tree_total = MICRO * TREES
    tree_keys = jax.random.split(jax.random.fold_in(key, 202), tree_total)
    leaf_order = jax.vmap(lambda element: jax.random.permutation(element, 8))(tree_keys).astype(jnp.int32)
    leaves = 1 + leaf_order // 2
    joined = jnp.concatenate([jnp.zeros((tree_total, 5), jnp.int32), leaves], axis=1)
    return joined.reshape(MICRO, TREES, 13)


def block_scale(key, dims, cuts, least, top_value):
    gain = 1.0
    for axis_at, shards_of in cuts:
        draws = jax.random.uniform(jax.random.fold_in(jax.random.fold_in(key, 6), axis_at), (shards_of,), jnp.float32, least / len(cuts), top_value / len(cuts))
        gain = gain * jnp.repeat(jnp.exp(draws), dims[axis_at] // shards_of).reshape((-1,) + (1,) * (len(dims) - 1 - axis_at))
    return gain


def gaussian(key, extent, deviation, most, shards=(), kind=jnp.bfloat16):
    values = jax.random.normal(key, extent, jnp.float32) * deviation
    if len(shards) > 0:
        values = block_scale(key, extent, shards, -0.22, 0.18) * values
    return jnp.clip(values, min=-most, max=most).astype(kind)


def setup_inputs(seed: int = 0) -> dict:
    keys = jax.random.split(jax.random.key(seed), 24)
    return {
        "content": gaussian(keys[0], (MICRO, TOKENS, D), 1.0, 6.0, ((1, 32),)),
        "query_state": gaussian(keys[1], (MICRO, TOKENS, D), 1.0, 6.0, ((1, 32),)),
        "token_seg": draw_token_seg(jax.random.fold_in(keys[23], 71), 0),
        "positions": draw_positions(jax.random.fold_in(keys[23], 71), 0),
        "parent": draw_parent(jax.random.fold_in(keys[23], 71), 0),
        "w_query": gaussian(keys[5], (D, D), D ** -0.5, 0.21875, ((0, 2),)),
        "w_key": gaussian(keys[6], (D, D), D ** -0.5, 0.21875, ((0, 2),)),
        "w_value": gaussian(keys[7], (D, D), D ** -0.5, 0.21875, ((0, 2),)),
        "w_out": gaussian(keys[8], (D, D), (D // 16) ** -0.5, 0.875, ((0, 2),)),
        "w_inner": gaussian(keys[9], (D, FF), D ** -0.5, 0.21875, ((0, 2),)),
        "w_outer": gaussian(keys[10], (FF, D), FF ** -0.5, 0.109375, ((0, 2),)),
        "b_inner": gaussian(keys[11], (FF,), 0.3, 1.75, ((0, 2),)),
        "b_outer": gaussian(keys[12], (D,), 0.3, 1.75, ((0, 2),)),
        "gain_attn": jnp.clip(1.0 + 0.1 * jax.random.normal(keys[13], (D,), jnp.float32), 0.5, 1.5).astype(jnp.bfloat16),
        "bias_attn": gaussian(keys[14], (D,), 0.3, 1.75, ((0, 2),)),
        "gain_ffn": jnp.clip(1.0 + 0.1 * jax.random.normal(keys[15], (D,), jnp.float32), 0.5, 1.5).astype(jnp.bfloat16),
        "bias_ffn": gaussian(keys[16], (D,), 0.3, 1.75, ((0, 2),)),
        "bias_content": gaussian(keys[17], (D,), 0.5, 3.0, ((0, 2),)),
        "bias_segment": gaussian(keys[18], (D,), 0.5, 3.0, ((0, 2),)),
        "seg_embed": gaussian(keys[19], (2, D), 1.0, 6.0, ((1, 2),)),
        "rel_table": gaussian(keys[20], (REL, HEADS), 0.7, 4.0, ((0, 2),)),
        "cot_content": gaussian(keys[21], (MICRO, TOKENS, D), 1.0, 6.0, ((1, 32),)),
        "cot_query": gaussian(keys[22], (MICRO, TOKENS, D), 1.0, 6.0, ((1, 32),)),
    }


@jax.custom_vjp
def low(v):
    return lax.optimization_barrier(v.astype(jnp.bfloat16)).astype(jnp.float32)

@jax.custom_vjp
def low_back(v):
    return v

def low_keep(v):
    return (low(v), None)

def low_pass(kept, grad):
    return (grad,)

def back_keep(v):
    return (v, None)

def back_low(kept, grad):
    return (low(grad),)
low.defvjp(low_keep, low_pass)
low_back.defvjp(back_keep, back_low)
thresholds = (1, 2, 4, 8, 32, 128, 512)
norm_eps = 1e-05
masked_score = -1e+30
highest = lax.Precision.HIGHEST

def layer_norm(inputs, norm_gain, norm_shift):
    row_mean = lax.optimization_barrier(jnp.mean(inputs, axis=-1, keepdims=True))
    centred = inputs - row_mean
    spread = lax.optimization_barrier(jnp.mean(centred * centred, axis=-1, keepdims=True))
    return centred * lax.rsqrt(spread + norm_eps) * norm_gain + norm_shift

def gelu_tanh(inputs):
    return jax.nn.gelu(inputs, approximate=True)

def bucket_of(query_pos, key_pos):
    offset = query_pos[:, None] - key_pos[None, :]
    magnitude = jnp.abs(offset)
    bucket = jnp.zeros(offset.shape, jnp.int32)
    for threshold in thresholds:
        bucket = bucket + (magnitude >= threshold).astype(jnp.int32)
    return bucket + 8 * (offset < 0).astype(jnp.int32)

def tree_forward(params, content_rows, query_rows, segments, tree_pos, parent_row):
    w_query, w_key, w_value, w_out, w_inner, w_outer, b_inner, b_outer, gain_attn, bias_attn, gain_ffn, bias_ffn, bias_content, bias_segment, seg_embed, rel_table = params
    both_rows = jnp.concatenate([content_rows, query_rows], axis=0)
    tree_keys = low(low_back(jnp.dot(content_rows, w_key, precision=highest)))
    tree_values = low(low_back(jnp.dot(content_rows, w_value, precision=highest)))
    query_raw = low_back(jnp.dot(both_rows, w_query, precision=highest))
    query_content = low(query_raw + bias_content).reshape(2 * TREE, HEADS, HEAD)
    query_segment = (query_raw + bias_segment).reshape(2 * TREE, HEADS, HEAD)
    seg_score = jnp.einsum('qhd,chd->qhc', query_segment, seg_embed.reshape(2, HEADS, HEAD), precision=highest)
    key_heads = tree_keys.reshape(TREE, HEADS, HEAD)
    value_heads = tree_values.reshape(TREE, HEADS, HEAD)
    parent_one = parent_row[segments]
    parent_two = parent_row[parent_one]
    key_index = jnp.arange(TREE, dtype=jnp.int32)
    row_block = min(512, TREE)
    block_count = TREE // row_block

    def arrange(inputs):
        shaped = inputs.reshape((2, block_count, row_block) + inputs.shape[1:])
        return jnp.swapaxes(shaped, 0, 1).reshape((block_count, 2 * row_block) + inputs.shape[1:])

    def doubled(inputs):
        return jnp.concatenate([inputs, inputs], axis=0)
    row_kinds = jnp.concatenate([jnp.zeros(TREE, jnp.int32), jnp.ones(TREE, jnp.int32)])
    row_items = (arrange(query_content), arrange(seg_score), arrange(doubled(segments)), arrange(doubled(parent_one)), arrange(doubled(parent_two)), arrange(doubled(tree_pos)), arrange(doubled(key_index)), arrange(row_kinds))

    def attend(element):
        row_query, row_segscore, row_segment, row_parent, row_grand, row_pos, row_index, row_kind = element
        raw_scores = jnp.einsum('qhd,khd->hqk', row_query, key_heads, precision=highest)
        same_seg = row_segment[:, None] == segments[None, :]
        seg_term = jnp.where(same_seg[None], jnp.transpose(row_segscore[:, :, 1])[:, :, None], jnp.transpose(row_segscore[:, :, 0])[:, :, None])
        rel_bias = jnp.take(jnp.transpose(rel_table), bucket_of(row_pos, tree_pos), axis=1)
        scores = low_back((raw_scores + seg_term) * HEAD ** (-0.5) + rel_bias)
        visible = (segments[None, :] == row_segment[:, None]) | (segments[None, :] == row_parent[:, None])
        visible = visible | (segments[None, :] == row_grand[:, None])
        visible = visible & jnp.logical_not((row_kind[:, None] == 1) & (key_index[None, :] == row_index[:, None]))
        masked = jnp.where(visible[None], scores, masked_score)
        log_total = jax.nn.logsumexp(masked, axis=-1, keepdims=True)
        probs_low = low(jnp.exp(masked - log_total))
        attended_rows = jnp.einsum('hqk,khd->qhd', probs_low, value_heads, precision=highest)
        return attended_rows.reshape(2 * row_block, HEADS * HEAD)
    attended = lax.map(jax.checkpoint(attend), row_items)
    attended = jnp.swapaxes(attended.reshape(block_count, 2, row_block, D), 0, 1).reshape(2 * TREE, D)
    att_low = low(low_back(attended))
    branch = low_back(jnp.dot(att_low, w_out, precision=highest))
    middle = layer_norm(branch + both_rows, gain_attn, bias_attn)
    inner_pre = low_back(jnp.dot(low(middle), w_inner, precision=highest) + b_inner)
    outer_projection_output = low_back(jnp.dot(low(gelu_tanh(inner_pre)), w_outer, precision=highest) + b_outer)
    final_rows = layer_norm(outer_projection_output + middle, gain_ffn, bias_ffn)
    return (final_rows[:TREE], final_rows[TREE:])

def reference(content, query_state, token_seg, positions, parent, w_query, w_key, w_value, w_out, w_inner, w_outer, b_inner, b_outer, gain_attn, bias_attn, gain_ffn, bias_ffn, bias_content, bias_segment, seg_embed, rel_table, cot_content, cot_query):
    weights = (w_query, w_key, w_value, w_out, w_inner, w_outer, b_inner, b_outer, gain_attn, bias_attn, gain_ffn, bias_ffn, bias_content, bias_segment, seg_embed, rel_table)
    params = tuple((weight.astype(jnp.float32) for weight in weights))
    tree_total = MICRO * TREES
    seg_trees = token_seg.reshape(tree_total, TREE)
    pos_trees = positions.reshape(tree_total, TREE)
    parent_trees = parent.reshape(tree_total, 13)

    def forward(params_in, content_in, query_in):

        def per_tree(element):
            return tree_forward(params_in, element[0], element[1], element[2], element[3], element[4])
        results = lax.map(jax.checkpoint(per_tree), (content_in.reshape(tree_total, TREE, D), query_in.reshape(tree_total, TREE, D), seg_trees, pos_trees, parent_trees))
        return (results[0].reshape(MICRO, TOKENS, D), results[1].reshape(MICRO, TOKENS, D))
    layer_out, pullback = jax.vjp(forward, params, content.astype(jnp.float32), query_state.astype(jnp.float32))
    gradients, grad_content, grad_query = pullback((cot_content.astype(jnp.float32), cot_query.astype(jnp.float32)))
    return (layer_out[0].astype(jnp.bfloat16), layer_out[1].astype(jnp.bfloat16), grad_content, grad_query, gradients[0], gradients[1], gradients[2], gradients[3], gradients[4], gradients[5], gradients[6], gradients[7], gradients[8], gradients[9], gradients[10], gradients[11], gradients[12], gradients[13], gradients[14], gradients[15])
```

```python
import functools

import jax
import jax.numpy as jnp
from jax import lax
from jax.experimental import pallas as pl
from jax.experimental.pallas import tpu as pltpu
from jax.sharding import PartitionSpec as P

thresholds = (1, 2, 4, 8, 32, 128, 512)
norm_eps = 1e-05
masked_score = -1e30
path_runs = 6
trunk_runs = 4
tree_runs = 16
vmem_bytes = 60 * 1024 * 1024
low = jnp.bfloat16
f32 = jnp.float32
any_space = pl.BlockSpec(memory_space=pl.ANY)
smem_space = pl.BlockSpec(memory_space=pltpu.SMEM)
vmem_space = pl.BlockSpec(memory_space=pltpu.VMEM)


def mm(left, right):
    return lax.dot_general(left, right, (((1,), (0,)), ((), ())), preferred_element_type=f32)


def mm_nt(left, right):
    return lax.dot_general(left, right, (((1,), (1,)), ((), ())), preferred_element_type=f32)


def mm_tn(left, right):
    return lax.dot_general(left, right, (((0,), (0,)), ((), ())), preferred_element_type=f32)


def weight_copies(pieces, target, sems, first, shard):
    if len(pieces) == 1:
        return [pltpu.make_async_copy(pieces[0], target, sems.at[first])]
    half = pieces[0].shape[0]
    own = pl.multiple_of(shard * half, 16)
    other = pl.multiple_of((1 - shard) * half, 16)
    return [
        pltpu.make_async_copy(pieces[0], target.at[pl.ds(own, half)], sems.at[first]),
        pltpu.make_async_copy(pieces[1], target.at[pl.ds(other, half)], sems.at[first + 1]),
    ]


def scalar_at(scalars, slots, micro, entry):
    return scalars[2 + (3 + slots) * micro + entry]


def query_kernel(pieces, scalars, rows, vectors, *refs):
    weights = refs[:pieces]
    query_low, query_segment, full, sems = refs[pieces:]
    copies = weight_copies(weights, full, sems, 0, scalars[0])
    for copy in copies:
        copy.start()
    for copy in copies:
        copy.wait()
    raw = mm(rows[...], full[...])
    query_low[...] = (raw + vectors[9:10, :]).astype(low)
    query_segment[...] = (raw + vectors[10:11, :]).astype(low)


def keys_kernel(pieces, columns, run, slots, scalars, *refs):
    parts = refs[: len(columns)]
    refs = refs[len(columns) :]
    key_weights, value_weights = refs[:pieces], refs[pieces : 2 * pieces]
    path, keys, values, full_key, full_value, sems, path_sems = refs[2 * pieces :]
    shard = scalars[0]
    copies = weight_copies(key_weights, full_key, sems, 0, shard)
    copies = copies + weight_copies(value_weights, full_value, sems, pieces, shard)
    moves = []
    micro_count = path.shape[0]
    for micro in range(micro_count):
        for slot in range(slots):
            relative = scalar_at(scalars, slots, micro, 3 + slot)
            for part, (start, width) in enumerate(columns):
                index = (micro * slots + slot) * len(columns) + part
                moves.append(
                    pltpu.make_async_copy(
                        parts[part].at[relative, pl.ds(micro * run, run), :],
                        path.at[micro, pl.ds(slot * run, run), pl.ds(start, width)],
                        path_sems.at[index],
                    )
                )
    for copy in moves + copies:
        copy.start()
    for copy in moves + copies:
        copy.wait()
    for micro in range(micro_count):
        rows = path[micro]
        span = slots * run
        keys[micro * span : (micro + 1) * span, :] = mm(rows, full_key[...]).astype(low)
        values[micro * span : (micro + 1) * span, :] = mm(rows, full_value[...]).astype(low)


def head_masks():
    lane = lax.broadcasted_iota(jnp.int32, (1, 128), 1)
    first = lane < 64
    return first, first.astype(f32).astype(low), (1.0 - first.astype(f32)).astype(low)


def stack_query(query_low, query_segment, mask_a, mask_b):
    both = jnp.concatenate([query_low, query_segment], axis=1)
    wide_a = jnp.concatenate([mask_a, mask_a], axis=1)
    wide_b = jnp.concatenate([mask_b, mask_b], axis=1)
    return jnp.concatenate([both * wide_a, both * wide_b], axis=0)


def stack_keys(keys, vectors, lo):
    row = lax.broadcasted_iota(jnp.int32, (keys.shape[0], 1), 0)
    segment = jnp.where(row >= lo, vectors[12:13, :], vectors[11:12, :]).astype(low)
    return jnp.concatenate([keys, segment], axis=1)


def offsets_of(base, run, span):
    row = lax.broadcasted_iota(jnp.int32, (run, span), 0)
    column = lax.broadcasted_iota(jnp.int32, (run, span), 1)
    return base + row - column, column


def attend_kernel(run, slots, scalars, table, query_low, query_segment, keys, values, vectors, probs, attended):
    pair, micro = pl.program_id(0), pl.program_id(1)
    base, lo, hi = (scalar_at(scalars, slots, micro, entry) for entry in range(3))
    span = slots * run
    first, mask_a, mask_b = head_masks()
    left = stack_query(query_low[...], query_segment[...], mask_a, mask_b)
    right = stack_keys(keys[...], vectors[...], lo)
    raw = mm_nt(left, right)
    delta, column = offsets_of(base, run, span)
    visible = column < hi
    biases = []
    for head in range(2):
        at = 2 * pair + head
        bias = jnp.full((run, span), table[0, at], f32)
        for step, threshold in enumerate(thresholds):
            if threshold < span:
                bias = jnp.where(delta >= threshold, table[1 + step, at], bias)
                bias = jnp.where(delta <= -threshold, table[9 + step, at], bias)
        bias = jnp.where(visible, bias, masked_score)
        biases.append(bias)
        biases.append(jnp.where(delta == 0, masked_score, bias))
    scores = raw * 0.125 + jnp.concatenate(biases, axis=0)
    peak = jnp.max(scores, axis=-1, keepdims=True)
    mass = jnp.exp(scores - peak)
    total = jnp.sum(mass, axis=-1, keepdims=True)
    probs_low = (mass * (1.0 / total)).astype(low)
    probs[0] = probs_low
    heads = mm(probs_low, values[...])
    attended[...] = jnp.where(first, heads[: 2 * run], heads[2 * run :])


def norm_forward(inputs):
    centred = inputs - jnp.mean(inputs, axis=-1, keepdims=True)
    scale = lax.rsqrt(jnp.mean(centred * centred, axis=-1, keepdims=True) + norm_eps)
    return centred * scale, scale


def norm_backward(gradient, gain, normal, scale):
    d_normal = gradient * gain
    mean_first = jnp.mean(d_normal, axis=-1, keepdims=True)
    mean_second = jnp.mean(d_normal * normal, axis=-1, keepdims=True)
    return scale * (d_normal - mean_first - normal * mean_second)


def column_sum(inputs):
    return jnp.sum(inputs, axis=0, keepdims=True)


def feed_kernel(pieces, run, scalars, rows, attended, cotangent, vectors, inner_bias, *refs):
    out_weights, inner_weights, outer_weights = (refs[i * pieces : (i + 1) * pieces] for i in range(3))
    refs = refs[3 * pieces :]
    out_content, out_query, d_mid_in, d_branch_out, d_att, small = refs[:6]
    outputs = 4 if pieces == 2 else 2
    grads = refs[6 : 6 + outputs]
    full_out, full_inner, full_outer, act_low, slope = refs[6 + outputs : 11 + outputs]
    if pieces == 2:
        held_outer, held_inner, sems, grad_sems = refs[11 + outputs :]
    else:
        (sems,) = refs[11 + outputs :]
    shard, place = scalars[0], scalars[1]
    copies = [
        weight_copies(out_weights, full_out, sems, 0, shard),
        weight_copies(inner_weights, full_inner, sems, pieces, shard),
        weight_copies(outer_weights, full_outer, sems, 2 * pieces, shard),
    ]
    for group in copies:
        for copy in group:
            copy.start()
    model = rows.shape[1]
    hidden = full_inner.shape[1]
    att_low = attended[...].astype(low)
    for copy in copies[0]:
        copy.wait()
    normal_first, scale_first = norm_forward(mm(att_low, full_out[...]) + rows[...].astype(f32))
    middle = normal_first * vectors[5:6, :] + vectors[6:7, :]
    middle_low = middle.astype(low)
    for copy in copies[1]:
        copy.wait()
    for copy in copies[2]:
        copy.wait()
    wide = model
    total = None
    for start in range(0, hidden, wide):
        at = slice(start, start + wide)
        pre = mm(middle_low, full_inner[:, at]) + inner_bias[:, at]
        squared = pre * pre
        bent = jnp.tanh(0.7978845608028654 * pre * (1.0 + 0.044715 * squared))
        half = 0.5 * (1.0 + bent)
        act = (pre * half).astype(low)
        act_low[:, at] = act
        slope[:, at] = half + (0.5 * 0.7978845608028654) * pre * (1.0 - bent * bent) * (
            1.0 + (3 * 0.044715) * squared
        )
        share = mm(act, full_outer[at, :])
        total = share if total is None else total + share
    normal_second, scale_second = norm_forward(total + vectors[4:5, :] + middle)
    final = (normal_second * vectors[7:8, :] + vectors[8:9, :]).astype(low)
    for micro in range(out_content.shape[0]):
        start = 2 * run * micro
        out_content[micro] = final[start : start + run]
        out_query[micro] = final[start + run : start + 2 * run]
    d_final = cotangent[...].astype(f32)
    small[7:8, :] = column_sum(d_final * normal_second)
    small[8:9, :] = column_sum(d_final)
    d_final_in = norm_backward(d_final, vectors[7:8, :], normal_second, scale_second)
    d_outer = d_final_in.astype(low)
    small[4:5, :] = column_sum(d_outer.astype(f32))
    block = model // 2

    def hold_outer(start, value):
        if pieces == 1:
            grads[0][start : start + block, :] = value.astype(low)
            return
        half = hidden // 2
        target = (start // half) ^ shard
        for down in range(2):
            for across in range(2):
                chunk = ((start % half) // (block // 2) + down) * 2 + across
                held_outer[target, chunk ^ place] = value[
                    down * (block // 2) : (down + 1) * (block // 2), across * block : (across + 1) * block
                ].astype(low)

    def hold_inner(start, value):
        if pieces == 1:
            grads[1][:, start : start + block] = value.astype(low)
            return
        for quarter in range(4):
            chunk = (quarter % 2) * 8 + start // block
            held_inner[(quarter // 2) ^ shard, chunk ^ place] = value[
                quarter * (block // 2) : (quarter + 1) * (block // 2), :
            ].astype(low)

    for start in range(0, hidden, block):
        hold_outer(start, mm_tn(act_low[:, start : start + block], d_outer))
    sent = []
    if pieces == 2:
        sent = [
            pltpu.make_async_copy(held_outer.at[0], grads[0], grad_sems.at[0]),
            pltpu.make_async_copy(held_outer.at[1], grads[1], grad_sems.at[1]),
        ]
        for copy in sent:
            copy.start()
    d_middle = d_final_in
    for start in range(0, hidden, block):
        at = slice(start, start + block)
        d_inner = (mm_nt(d_outer, full_outer[at, :]) * slope[:, at]).astype(low)
        summed = column_sum(d_inner.astype(f32))
        row, lane = start // model, start % model
        small[row : row + 1, lane : lane + block] = summed
        hold_inner(start, mm_tn(middle_low, d_inner))
        d_middle = d_middle + mm_nt(d_inner, full_inner[:, at])
    if pieces == 2:
        late = [
            pltpu.make_async_copy(held_inner.at[0], grads[2], grad_sems.at[2]),
            pltpu.make_async_copy(held_inner.at[1], grads[3], grad_sems.at[3]),
        ]
        for copy in late:
            copy.start()
        sent = sent + late
    small[5:6, :] = column_sum(d_middle * normal_first)
    small[6:7, :] = column_sum(d_middle)
    small[9:16, :] = jnp.zeros((7, model), f32)
    d_mid = norm_backward(d_middle, vectors[5:6, :], normal_first, scale_first)
    d_mid_in[...] = d_mid
    d_branch = d_mid.astype(low)
    d_branch_out[...] = d_branch
    d_att[...] = mm_nt(d_branch, full_out[...]).astype(low)
    for copy in sent:
        copy.wait()


def back_kernel(
    run,
    slots,
    scalars,
    query_low,
    query_segment,
    keys,
    values,
    probs,
    d_att,
    attended,
    vectors,
    d_query,
    d_keys,
    d_values,
    small,
    buckets,
):
    micro = pl.program_id(1)
    base, lo = scalar_at(scalars, slots, micro, 0), scalar_at(scalars, slots, micro, 1)
    span = slots * run
    first, mask_a, mask_b = head_masks()
    gradient = d_att[...]
    stacked = jnp.concatenate([gradient * mask_a, gradient * mask_b], axis=0)
    product = gradient.astype(f32) * attended[...]
    delta_a = jnp.sum(jnp.where(first, product, 0.0), axis=-1, keepdims=True)
    delta_b = jnp.sum(jnp.where(first, 0.0, product), axis=-1, keepdims=True)
    delta_row = jnp.concatenate([delta_a, delta_b], axis=0)
    probs_low = probs[0]
    d_probs = mm_nt(stacked, values[...])
    d_scores = (probs_low.astype(f32) * (d_probs - delta_row)).astype(low)
    left = stack_query(query_low[...], query_segment[...], mask_a, mask_b)
    right = stack_keys(keys[...], vectors[...], lo)
    d_left = mm(d_scores, right) * 0.125
    mine = jnp.concatenate([first, first], axis=1)
    d_left = jnp.where(mine, d_left[: 2 * run], d_left[2 * run :])
    d_content, d_segment = d_left[:, :128], d_left[:, 128:]
    d_query[...] = (d_content + d_segment).astype(low)
    d_right = mm_tn(d_scores, left) * 0.125
    d_keys[...] = d_right[:, :128].astype(low)
    d_values[...] = mm_tn(probs_low, stacked).astype(low)
    row = lax.broadcasted_iota(jnp.int32, (span, 1), 0)
    d_embed = d_right[:, 128:]
    shares = jnp.concatenate(
        [
            column_sum(d_content),
            column_sum(d_segment),
            column_sum(jnp.where(row >= lo, 0.0, d_embed)),
            column_sum(jnp.where(row >= lo, d_embed, 0.0)),
            jnp.zeros((4, 128), f32),
        ],
        axis=0,
    )
    delta, _ = offsets_of(base, run, span)
    exact = d_scores.astype(f32)
    tallies = []
    for head in range(2):
        at = 2 * run * head
        both = exact[at : at + run] + exact[at + run : at + 2 * run]
        rows = [None] * 16
        rows[0] = column_sum(jnp.where(delta == 0, both, 0.0))
        for step, threshold in enumerate(thresholds):
            if threshold < span:
                later = thresholds[step + 1] if step + 1 < len(thresholds) else span
                above = (delta >= threshold) & (delta < later)
                below = (delta <= -threshold) & (delta > -later)
                rows[1 + step] = column_sum(jnp.where(above, both, 0.0))
                rows[9 + step] = column_sum(jnp.where(below, both, 0.0))
        blank = jnp.zeros((1, span), f32)
        tallies.append(jnp.concatenate([blank if entry is None else entry for entry in rows], axis=0))

    @pl.when(micro == 0)
    def _():
        small[...] = shares
        for head in range(2):
            buckets[head] = tallies[head]

    @pl.when(micro != 0)
    def _():
        small[...] += shares
        for head in range(2):
            buckets[head] += tallies[head]


def weights_kernel(pieces, columns, run, slots, scalars, rows, path, attended, d_branch, d_query, d_keys, d_values, d_mid_in, *refs):
    weights = [refs[i * pieces : (i + 1) * pieces] for i in range(3)]
    refs = refs[3 * pieces :]
    d_content, d_state = refs[:2]
    parts = refs[2 : 2 + len(columns)]
    refs = refs[2 + len(columns) :]
    if pieces == 2:
        kept, sent, full, held, sems, grad_sems = refs
    else:
        natural, full, sems = refs[:4], refs[4], refs[5]
    shard, place = scalars[0], scalars[1]
    copies = [weight_copies(weights[i], full.at[i], sems, i * pieces, shard) for i in range(3)]
    for group in copies:
        for copy in group:
            copy.start()
    model = rows.shape[1]
    block = model // 2
    small_rows = block // 8

    def hold(which, value):
        if pieces == 1:
            natural[which][...] = value.astype(low)
            return
        for half in range(2):
            for down in range(8):
                for across in range(2):
                    start = half * block + down * small_rows
                    held[half ^ shard, (down * 2 + across) ^ place, which * small_rows : (which + 1) * small_rows, :] = value[
                        start : start + small_rows, across * block : (across + 1) * block
                    ].astype(low)

    hold(0, mm_tn(rows[...], d_query[...]))
    hold(1, mm_tn(path[...], d_keys[...]))
    hold(2, mm_tn(path[...], d_values[...]))
    hold(3, mm_tn(attended[...].astype(low), d_branch[...]))
    leaving = []
    if pieces == 2:
        leaving = [
            pltpu.make_async_copy(held.at[0], kept, grad_sems.at[0]),
            pltpu.make_async_copy(held.at[1], sent, grad_sems.at[1]),
        ]
        for copy in leaving:
            copy.start()
    for group in copies:
        for copy in group:
            copy.wait()
    for part in parts:
        part[...] = jnp.zeros(part.shape, part.dtype)
    span = slots * run
    for micro in range(rows.shape[0] // (2 * run)):
        at = slice(micro * span, (micro + 1) * span)
        shares = mm_nt(d_keys[at, :], full[1]) + mm_nt(d_values[at, :], full[2])
        for slot in range(slots):
            relative = scalar_at(scalars, slots, micro, 3 + slot)
            for part, (start, width) in enumerate(columns):
                piece = shares[slot * run : (slot + 1) * run, start : start + width]
                spot = (relative, slice(micro * run, (micro + 1) * run), slice(None))
                parts[part][spot] = (parts[part][spot].astype(f32) + piece).astype(low)
    d_both = d_mid_in[...] + mm_nt(d_query[...], full[0])
    for micro in range(rows.shape[0] // (2 * run)):
        start = 2 * run * micro
        d_content[micro] = d_both[start : start + run]
        d_state[micro] = d_both[start + run : start + 2 * run]
    for copy in leaving:
        copy.wait()


def spread_kernel(layout, scalars, *refs):
    source, targets = refs[0], refs[1:]
    for which, target in enumerate(targets):
        rows = target.shape[0]
        target[...] = source[0, which * rows : (which + 1) * rows, :].astype(f32)


def send(inputs, mask):
    return lax.ppermute(inputs, "dp", [(i, i ^ mask) for i in range(lax.axis_size("dp"))])


def bits_of(order):
    named = {"x": (0,), "y": (1,), "z": (2, 3)}
    total = lax.axis_size("dp").bit_length() - 1
    return [named[axis] for axis in order] + [(bit,) for bit in range(4, total)], total


def gather_blocks(block, order):
    stages, total = bits_of(order)
    held = block.reshape((1,) * total + block.shape)
    for bits in stages:
        if len(bits) == 2:
            near, far, both = send(held, 4), send(held, 8), send(held, 12)
            at = total - 1 - bits[0]
            held = jnp.concatenate(
                [jnp.concatenate([held, near], axis=at), jnp.concatenate([far, both], axis=at)], axis=at - 1
            )
        else:
            held = jnp.concatenate([held, send(held, 1 << bits[0])], axis=total - 1 - bits[0])
    return held.reshape((1 << total,) + block.shape)


def scatter_blocks(blocks, order):
    stages, total = bits_of(order[::-1])
    held = blocks.reshape((2,) * total + blocks.shape[1:])

    def part(inputs, bit, which):
        return lax.slice_in_dim(inputs, which, which + 1, axis=total - 1 - bit)

    for bits in stages[::-1]:
        if len(bits) == 2:
            lower, upper = part(held, 3, 0), part(held, 3, 1)
            near, far, both = send(part(lower, 2, 1), 4), send(part(upper, 2, 0), 8), send(part(upper, 2, 1), 12)
            held = (part(lower, 2, 0).astype(f32) + near + far + both).astype(low)
        else:
            held = part(held, bits[0], 0) + send(part(held, bits[0], 1), 1 << bits[0])
    return held.reshape(blocks.shape[1:])


def all_sum(blocks):
    rows = blocks.shape[1]
    cuts = (0, rows // 2, rows * 3 // 4, rows)
    orders = ("yxz", "zxy", "xzy")
    pieces = []
    for part, order in enumerate(orders):
        share = scatter_blocks(blocks[:, cuts[part] : cuts[part + 1]], order)
        pieces.append(gather_blocks(share, order[::-1]))
    return jnp.concatenate(pieces, axis=1)


def shards(
    content,
    query_state,
    token_seg,
    positions,
    parent,
    w_query,
    w_key,
    w_value,
    w_out,
    w_inner,
    w_outer,
    b_inner,
    b_outer,
    gain_attn,
    bias_attn,
    gain_ffn,
    bias_ffn,
    bias_content,
    bias_segment,
    seg_embed,
    rel_table,
    cot_content,
    cot_query,
):
    micro_count, run, model = content.shape
    shard_count, dp_count = lax.axis_size("shard"), lax.axis_size("dp")
    shard, place = lax.axis_index("shard"), lax.axis_index("dp")
    heads = rel_table.shape[1]
    bucket_total = rel_table.shape[0] * shard_count
    hidden = w_inner.shape[1]
    pairs = heads // 2
    per_run = dp_count // tree_runs
    slots = path_runs * per_run
    span = slots * run
    rows_total = 2 * run * micro_count
    pieces = 2 if shard_count == 2 and dp_count == tree_runs else 1
    part_width = model // shard_count

    def fetch(weight):
        if pieces == 2:
            return [weight, lax.ppermute(weight, "shard", [(0, 1), (1, 0)])]
        return [lax.all_gather(weight, "shard", axis=0, tiled=True)]

    own_seg = token_seg[:, 0]
    own_slot = positions[:, 0] // run
    facts = jnp.stack([own_seg, own_slot], axis=1).reshape(2 * micro_count).astype(low)
    columns = ((0, model // 2), (model // 2, model // 6), (model // 2 + model // 6, model // 3))
    orders = ("zxy", "xyz", "yzx")
    flat_content = content.reshape(micro_count * run, model)
    fact_rows = jnp.broadcast_to(
        jnp.pad(facts, (0, 16 - 2 * micro_count))[:, None], (16, columns[1][1])
    )
    tree_parts = []
    for part, (start, width) in enumerate(columns):
        block = flat_content[:, start : start + width]
        if part == 1:
            block = jnp.concatenate([block, fact_rows], axis=0)
        tree_parts.append(gather_blocks(block, orders[part]))

    small_parts = jnp.concatenate(
        [
            b_inner.reshape(-1, part_width),
            jnp.stack([b_outer, gain_attn, bias_attn, gain_ffn, bias_ffn, bias_content, bias_segment]),
            seg_embed,
            jnp.pad(rel_table.reshape(1, -1), ((0, 0), (0, part_width - rel_table.size))),
        ],
        axis=0,
    )
    inner_rows = b_inner.shape[0] // part_width
    fill = 16 - small_parts.shape[0]
    small_parts = jnp.pad(small_parts, ((0, fill), (0, 0)))
    if pieces == 2:
        other = lax.ppermute(small_parts, "shard", [(0, 1), (1, 0)])
        gathered = jnp.where(shard == 0, jnp.stack([small_parts, other]), jnp.stack([other, small_parts]))
    else:
        gathered = lax.all_gather(small_parts, "shard", axis=0, tiled=False)
    gathered = gathered.astype(f32)
    inner_bias = gathered[:, :inner_rows].reshape(1, hidden)
    vectors = jnp.transpose(gathered, (1, 0, 2)).reshape(16, model)
    table = gathered[:, 13, : rel_table.size].reshape(bucket_total, heads)

    query_weights, key_weights, value_weights = fetch(w_query), fetch(w_key), fetch(w_value)
    out_weights, inner_weights, outer_weights = fetch(w_out), fetch(w_inner), fetch(w_outer)

    every = jnp.transpose(
        tree_parts[1][:, micro_count * run : micro_count * run + 2 * micro_count, 0].astype(jnp.int32)
    ).reshape(micro_count, 2, dp_count)
    blocks = jnp.arange(dp_count, dtype=jnp.int32)
    entries = [shard, place]
    for micro in range(micro_count):
        segs, slots_of = every[micro, 0], every[micro, 1]
        mine = own_seg[micro]
        above = jnp.sum(jnp.where(jnp.arange(parent.shape[2]) == mine, parent[micro, 0], 0))
        trunk = mine == 0
        leaf = mine > 4
        branch = jnp.where(leaf, above, mine)
        base = own_slot[micro] * run
        first_branch, first_leaf = trunk_runs * per_run, (trunk_runs + 1) * per_run
        lo = jnp.where(trunk, 0, jnp.where(leaf, first_leaf, first_branch)) * run
        hi = jnp.where(trunk, first_branch, jnp.where(leaf, slots, first_leaf)) * run
        entries += [base, lo, hi]
        for slot in range(slots):
            wanted = 0 if slot < first_branch else branch if slot < first_leaf else mine
            shown = (segs == wanted) & (slots_of == slot)
            entries.append(jnp.sum(jnp.where(shown, blocks, 0)))
    scalars = jnp.stack([jnp.asarray(entry, jnp.int32) for entry in entries])
    early = jnp.stack([jnp.asarray(entry, jnp.int32) for entry in entries[:2]])

    rows = jnp.concatenate([content, query_state], axis=1).reshape(rows_total, model)
    cotangent = jnp.concatenate([cot_content, cot_query], axis=1).reshape(rows_total, model)
    grown = pltpu.CompilerParams(vmem_limit_bytes=vmem_bytes)

    def shape(dims, kind):
        return jax.ShapeDtypeStruct(dims, kind)

    dma = pltpu.SemaphoreType.DMA
    query_low, query_segment = pl.pallas_call(
        functools.partial(query_kernel, pieces),
        out_shape=(shape((rows_total, model), low),) * 2,
        in_specs=[smem_space, vmem_space, vmem_space] + [any_space] * pieces,
        out_specs=(vmem_space,) * 2,
        scratch_shapes=[pltpu.VMEM((model, model), low), dma((pieces,))],
        compiler_params=grown,
        name="query_projection",
    )(early, rows, vectors, *query_weights)

    path, keys, values = pl.pallas_call(
        functools.partial(keys_kernel, pieces, columns, run, slots),
        out_shape=(
            shape((micro_count, span, model), low),
            shape((micro_count * span, model), low),
            shape((micro_count * span, model), low),
        ),
        in_specs=[smem_space] + [any_space] * (len(columns) + 2 * pieces),
        out_specs=(vmem_space,) * 3,
        scratch_shapes=[
            pltpu.VMEM((model, model), low),
            pltpu.VMEM((model, model), low),
            dma((2 * pieces,)),
            dma((micro_count * slots * len(columns),)),
        ],
        compiler_params=grown,
        name="path_keys",
    )(scalars, *tree_parts, *key_weights, *value_weights)
    path = path.reshape(micro_count * span, model)

    row_block = pl.BlockSpec((2 * run, 128), lambda pair, micro: (micro, pair))
    key_block = pl.BlockSpec((span, 128), lambda pair, micro: (micro, pair))
    vector_block = pl.BlockSpec((16, 128), lambda pair, micro: (0, pair))
    prob_block = pl.BlockSpec((1, 4 * run, span), lambda pair, micro: (pair * micro_count + micro, 0, 0))
    probs, attended = pl.pallas_call(
        functools.partial(attend_kernel, run, slots),
        grid=(pairs, micro_count),
        out_shape=(
            shape((pairs * micro_count, 4 * run, span), low),
            shape((rows_total, model), f32),
        ),
        in_specs=[smem_space, smem_space, row_block, row_block, key_block, key_block, vector_block],
        out_specs=(prob_block, row_block),
        compiler_params=grown,
        name="attend",
    )(scalars, table, query_low, query_segment, keys, values, vectors)

    chunk = (dp_count, hidden // (8 * shard_count), model // 2)
    if pieces == 2:
        grad_shapes = [shape(chunk, low)] * 4
        grad_specs = [any_space] * 4
        grad_scratch = [pltpu.VMEM((2,) + chunk, low)] * 2
    else:
        grad_shapes = [shape((hidden, model), low), shape((model, hidden), low)]
        grad_specs = [vmem_space] * 2
        grad_scratch = []
    results = pl.pallas_call(
        functools.partial(feed_kernel, pieces, run),
        out_shape=[
            shape((micro_count, run, model), low),
            shape((micro_count, run, model), low),
            shape((rows_total, model), f32),
            shape((rows_total, model), low),
            shape((rows_total, model), low),
            shape((16, model), f32),
        ]
        + grad_shapes,
        in_specs=[smem_space] + [vmem_space] * 5 + [any_space] * (3 * pieces),
        out_specs=[vmem_space] * 6 + grad_specs,
        scratch_shapes=[
            pltpu.VMEM((model, model), low),
            pltpu.VMEM((model, hidden), low),
            pltpu.VMEM((hidden, model), low),
            pltpu.VMEM((rows_total, hidden), low),
            pltpu.VMEM((rows_total, hidden), f32),
        ]
        + grad_scratch
        + [dma((3 * pieces,))]
        + ([dma((4,))] if pieces == 2 else []),
        compiler_params=grown,
        name="feed_forward",
    )(scalars, rows, attended, cotangent, vectors, inner_bias, *out_weights, *inner_weights, *outer_weights)
    out_content, out_query, d_mid_in, d_branch, d_att, small_first = results[:6]

    d_query, d_keys, d_values, small_second, tallies = pl.pallas_call(
        functools.partial(back_kernel, run, slots),
        grid=(pairs, micro_count),
        out_shape=(
            shape((rows_total, model), low),
            shape((micro_count * span, model), low),
            shape((micro_count * span, model), low),
            shape((8, model), f32),
            shape((heads, 16, span), f32),
        ),
        in_specs=[smem_space, row_block, row_block, key_block, key_block, prob_block, row_block, row_block, vector_block],
        out_specs=(
            row_block,
            key_block,
            key_block,
            pl.BlockSpec((8, 128), lambda pair, micro: (0, pair)),
            pl.BlockSpec((2, 16, span), lambda pair, micro: (pair, 0, 0)),
        ),
        compiler_params=grown,
        name="attend_back",
    )(scalars, query_low, query_segment, keys, values, probs, d_att, attended, vectors)

    if pieces == 2:
        grad_shapes = [shape(chunk, low)] * 2
        grad_specs = [any_space] * 2
    else:
        grad_shapes = [shape((model, model), low)] * 4
        grad_specs = [vmem_space] * 4
    later = pl.pallas_call(
        functools.partial(weights_kernel, pieces, columns, run, slots),
        out_shape=[shape((micro_count, run, model), f32)] * 2
        + [shape((dp_count, micro_count * run, width), low) for _, width in columns]
        + grad_shapes,
        in_specs=[smem_space] + [vmem_space] * 8 + [any_space] * (3 * pieces),
        out_specs=[vmem_space] * (2 + len(columns)) + grad_specs,
        scratch_shapes=[pltpu.VMEM((3, model, model), low)]
        + ([pltpu.VMEM((2,) + chunk, low)] if pieces == 2 else [])
        + [dma((3 * pieces,))]
        + ([dma((2,))] if pieces == 2 else []),
        compiler_params=grown,
        name="weight_gradients",
    )(scalars, rows, path, attended, d_branch, d_query, d_keys, d_values, d_mid_in, *query_weights, *key_weights, *value_weights)
    d_content, grad_query = later[:2]
    tree_grads = later[2 : 2 + len(columns)]
    later = later[2 + len(columns) :]

    arrived = [scatter_blocks(part, order[::-1]) for part, order in zip(tree_grads, orders)]
    grad_content = d_content + jnp.concatenate(arrived, axis=1).astype(f32).reshape(content.shape)

    def spread(blocks_in, shapes, dims, place_of):
        return pl.pallas_call(
            functools.partial(spread_kernel, None),
            grid_spec=pltpu.PrefetchScalarGridSpec(
                num_scalar_prefetch=1,
                grid=(dp_count,),
                in_specs=[pl.BlockSpec((1,) + blocks_in.shape[1:], lambda i, s: (i ^ s[1], 0, 0))],
                out_specs=[pl.BlockSpec(dims, place_of)] * len(shapes),
            ),
            out_shape=[shape(entry, f32) for entry in shapes],
            compiler_params=grown,
            name="spread",
        )(early, blocks_in)

    half = model // 2
    if pieces == 2:
        swap = [(0, 1), (1, 0)]
        outer_sum = all_sum(results[6] + lax.ppermute(results[7], "shard", swap))
        inner_sum = all_sum(results[8] + lax.ppermute(results[9], "shard", swap))
        later_sum = all_sum(later[0] + lax.ppermute(later[1], "shard", swap))
        (grad_w_outer,) = spread(outer_sum, [w_outer.shape], (chunk[1], half), lambda i, s: (i // 2, i % 2))
        (grad_w_inner,) = spread(inner_sum, [w_inner.shape], (chunk[1], half), lambda i, s: (i // 8, i % 8))
        grad_w_query, grad_w_key, grad_w_value, grad_w_out = spread(
            later_sum, [w_query.shape] * 4, (half // 8, half), lambda i, s: (i // 2, i % 2)
        )
    else:
        totals = []
        for entry in (*results[6:8], *later):
            share = lax.psum_scatter(entry, "shard", scatter_dimension=0, tiled=True)
            totals.append(lax.psum(share, "dp").astype(f32))
        grad_w_outer, grad_w_inner, grad_w_query, grad_w_key, grad_w_value, grad_w_out = totals

    bucket_grads = jnp.transpose(jnp.sum(tallies, axis=-1)).reshape(1, -1)
    small = jnp.concatenate(
        [
            small_first[:9],
            small_second[:4],
            jnp.pad(bucket_grads, ((0, 0), (0, model - bucket_grads.shape[1]))),
        ],
        axis=0,
    )
    small = lax.psum(small, ("shard", "dp"))
    grad_b_inner = lax.dynamic_slice_in_dim(small[:4].reshape(-1), shard * b_inner.shape[0], b_inner.shape[0])
    narrow = lax.dynamic_slice_in_dim(small[4:13], shard * part_width, part_width, axis=1)
    grad_rel_table = lax.dynamic_slice_in_dim(
        small[13, : bucket_total * heads].reshape(bucket_total, heads),
        shard * rel_table.shape[0],
        rel_table.shape[0],
        axis=0,
    )
    return (
        out_content,
        out_query,
        grad_content,
        grad_query,
        grad_w_query,
        grad_w_key,
        grad_w_value,
        grad_w_out,
        grad_w_inner,
        grad_w_outer,
        grad_b_inner,
        narrow[0],
        narrow[1],
        narrow[2],
        narrow[3],
        narrow[4],
        narrow[5],
        narrow[6],
        narrow[7:9],
        grad_rel_table,
    )


def solution(mesh):
    rows = P(None, ("shard", "dp"), None)
    tokens = P(None, ("shard", "dp"))
    matrix = P("shard", None)
    vector = P("shard")
    return jax.shard_map(
        shards,
        mesh=mesh,
        in_specs=(rows, rows, tokens, tokens, P(None, "shard", None))
        + (matrix,) * 6
        + (vector,) * 8
        + (P(None, "shard"), matrix, rows, rows),
        out_specs=(rows,) * 4 + (matrix,) * 6 + (vector,) * 8 + (P(None, "shard"), matrix),
        check_vma=False,
    )
```

```python
import functools

import jax
import jax.numpy as jnp
from jax import lax
from jax.experimental import pallas as pl
from jax.experimental.pallas import tpu as pltpu
from jax.sharding import PartitionSpec as P

thresholds = (1, 2, 4, 8, 32, 128, 512)
norm_eps = 1e-05
masked_score = -1e30
path_runs = 6
trunk_runs = 4
tree_runs = 16
vmem_bytes = 60 * 1024 * 1024
low = jnp.bfloat16
f32 = jnp.float32
def cost(microseconds):
    return pl.CostEstimate(flops=int(microseconds * 1e9), bytes_accessed=0, transcendentals=0)


any_space = pl.BlockSpec(memory_space=pl.ANY)
smem_space = pl.BlockSpec(memory_space=pltpu.SMEM)
vmem_space = pl.BlockSpec(memory_space=pltpu.VMEM)


def mm(left, right):
    return lax.dot_general(left, right, (((1,), (0,)), ((), ())), preferred_element_type=f32)


def mm_nt(left, right):
    return lax.dot_general(left, right, (((1,), (1,)), ((), ())), preferred_element_type=f32)


def mm_tn(left, right):
    return lax.dot_general(left, right, (((0,), (0,)), ((), ())), preferred_element_type=f32)


def weight_copies(pieces, target, sems, first, shard):
    if len(pieces) == 1:
        return [pltpu.make_async_copy(pieces[0], target, sems.at[first])]
    half = pieces[0].shape[0]
    own = pl.multiple_of(shard * half, 16)
    other = pl.multiple_of((1 - shard) * half, 16)
    return [
        pltpu.make_async_copy(pieces[0], target.at[pl.ds(own, half)], sems.at[first]),
        pltpu.make_async_copy(pieces[1], target.at[pl.ds(other, half)], sems.at[first + 1]),
    ]


def scalar_at(scalars, micro, entry):
    return scalars[2 + 5 * micro + entry]


def block_index(at, total):
    return tuple((at >> (total - 1 - i)) & 1 for i in range(total))


def half_index(bit, which, total):
    everything = [slice(None)] * total
    everything[total - 1 - bit] = pl.ds(which, 1)
    return tuple(everything)


def half_at(bit, which, total):
    everything = [slice(None)] * total
    everything[total - 1 - bit] = which
    return tuple(everything)


def query_kernel(pieces, scalars, rows, vectors, *refs):
    weights = refs[:pieces]
    query_low, query_segment, full, sems = refs[pieces:]
    copies = weight_copies(weights, full, sems, 0, scalars[0])
    for copy in copies:
        copy.start()
    for copy in copies:
        copy.wait()
    raw = mm(rows[...], full[...])
    query_low[...] = (raw + vectors[9:10, :]).astype(low)
    query_segment[...] = (raw + vectors[10:11, :]).astype(low)


def keys_kernel(pieces, columns, lasts, run, slots, scalars, *refs):
    parts = refs[: 2 * len(columns)]
    refs = refs[2 * len(columns) :]
    key_weights, value_weights = refs[:pieces], refs[pieces : 2 * pieces]
    path, keys, values, found, full_key, full_value, tree, sems, tree_sems = refs[2 * pieces :]
    shard = scalars[0]
    total = len(tree.shape) - 2
    moves = []
    for part, (start, width) in enumerate(columns):
        for which in range(2):
            source = parts[2 * part + which]
            target = tree.at[
                (*half_index(lasts[part], which, total), pl.ds(0, source.shape[-2]), pl.ds(start, width))
            ]
            moves.append(pltpu.make_async_copy(source, target, tree_sems.at[2 * part + which]))
    copies = weight_copies(key_weights, full_key, sems, 0, shard)
    copies = copies + weight_copies(value_weights, full_value, sems, pieces, shard)
    for copy in moves + copies:
        copy.start()
    for copy in moves:
        copy.wait()
    micro_count = path.shape[0]
    content_rows = micro_count * run
    facts = [
        tree[(*block_index(block, total), slice(content_rows, content_rows + 16), slice(0, 128))].astype(f32)
        for block in range(1 << total)
    ]
    numbers = lax.broadcasted_iota(jnp.int32, (1 << total, 128), 0)
    for micro in range(micro_count):
        segs = jnp.concatenate([entry[2 * micro : 2 * micro + 1] for entry in facts], axis=0).astype(jnp.int32)
        places = jnp.concatenate([entry[2 * micro + 1 : 2 * micro + 2] for entry in facts], axis=0).astype(jnp.int32)
        for slot in range(slots):
            if slot < slots // path_runs * trunk_runs:
                wanted = 0
            else:
                wanted = scalar_at(scalars, micro, 4 if slot < slots // path_runs * (trunk_runs + 1) else 3)
            shown = (segs == wanted) & (places == slot)
            relative = jnp.max(jnp.where(shown, numbers, 0))
            found[micro * slots + slot] = relative
            at = block_index(relative, total)
            path[micro, slot * run : (slot + 1) * run, :] = tree[(*at, slice(micro * run, (micro + 1) * run), slice(None))]
    for copy in copies:
        copy.wait()
    for micro in range(micro_count):
        rows = path[micro]
        span = slots * run
        keys[micro * span : (micro + 1) * span, :] = mm(rows, full_key[...]).astype(low)
        values[micro * span : (micro + 1) * span, :] = mm(rows, full_value[...]).astype(low)


def head_masks():
    lane = lax.broadcasted_iota(jnp.int32, (1, 128), 1)
    first = lane < 64
    return first, first.astype(f32).astype(low), (1.0 - first.astype(f32)).astype(low)


def stack_query(query_low, query_segment, mask_a, mask_b):
    both = jnp.concatenate([query_low, query_segment], axis=1)
    wide_a = jnp.concatenate([mask_a, mask_a], axis=1)
    wide_b = jnp.concatenate([mask_b, mask_b], axis=1)
    return jnp.concatenate([both * wide_a, both * wide_b], axis=0)


def stack_keys(keys, vectors, lo):
    row = lax.broadcasted_iota(jnp.int32, (keys.shape[0], 1), 0)
    segment = jnp.where(row >= lo, vectors[12:13, :], vectors[11:12, :]).astype(low)
    return jnp.concatenate([keys, segment], axis=1)


def offsets_of(base, run, span):
    row = lax.broadcasted_iota(jnp.int32, (run, span), 0)
    column = lax.broadcasted_iota(jnp.int32, (run, span), 1)
    return base + row - column, column


def attend_kernel(run, slots, scalars, table, query_low, query_segment, keys, values, vectors, probs, attended):
    pair, micro = pl.program_id(0), pl.program_id(1)
    base, lo, hi = (scalar_at(scalars, micro, entry) for entry in range(3))
    span = slots * run
    first, mask_a, mask_b = head_masks()
    left = stack_query(query_low[...], query_segment[...], mask_a, mask_b)
    right = stack_keys(keys[...], vectors[...], lo)
    raw = mm_nt(left, right)
    delta, column = offsets_of(base, run, span)
    visible = column < hi
    biases = []
    for head in range(2):
        at = 2 * pair + head
        bias = jnp.full((run, span), table[0, at], f32)
        for step, threshold in enumerate(thresholds):
            if threshold < span:
                bias = jnp.where(delta >= threshold, table[1 + step, at], bias)
                bias = jnp.where(delta <= -threshold, table[9 + step, at], bias)
        bias = jnp.where(visible, bias, masked_score)
        biases.append(bias)
        biases.append(jnp.where(delta == 0, masked_score, bias))
    scores = raw * 0.125 + jnp.concatenate(biases, axis=0)
    peak = jnp.max(scores, axis=-1, keepdims=True)
    mass = jnp.exp(scores - peak)
    total = jnp.sum(mass, axis=-1, keepdims=True)
    probs_low = (mass * (1.0 / total)).astype(low)
    probs[0] = probs_low
    heads = mm(probs_low, values[...])
    attended[...] = jnp.where(first, heads[: 2 * run], heads[2 * run :])


def norm_forward(inputs):
    centred = inputs - jnp.mean(inputs, axis=-1, keepdims=True)
    scale = lax.rsqrt(jnp.mean(centred * centred, axis=-1, keepdims=True) + norm_eps)
    return centred * scale, scale


def norm_backward(gradient, gain, normal, scale):
    d_normal = gradient * gain
    mean_first = jnp.mean(d_normal, axis=-1, keepdims=True)
    mean_second = jnp.mean(d_normal * normal, axis=-1, keepdims=True)
    return scale * (d_normal - mean_first - normal * mean_second)


def column_sum(inputs):
    return jnp.sum(inputs, axis=0, keepdims=True)


def feed_cuts(pieces, model):
    if pieces == 1:
        return ()
    step = model // 6
    return ((0, step), (step, step), (2 * step, step))


def later_cuts(model):
    whole = model // 4 + 16
    step = whole // 48 * 16
    return ((0, step), (step, step), (2 * step, whole - 2 * step))


def tree_cuts(height):
    step = height // 48 * 16 + 16
    return ((0, step), (step, step), (2 * step, height - 2 * step))


def feed_kernel(pieces, run, scalars, rows, attended, cotangent, vectors, inner_bias, *refs):
    out_weights, inner_weights, outer_weights = (refs[i * pieces : (i + 1) * pieces] for i in range(3))
    refs = refs[3 * pieces :]
    out_content, out_query, d_mid_in, d_branch_out, d_att, small = refs[:6]
    routes = feed_cuts(pieces, rows.shape[1])
    outputs = 4 if pieces == 2 else 2
    grads = refs[6 : 6 + outputs]
    full_out, full_inner, full_outer, act_low, slope = refs[6 + outputs : 11 + outputs]
    if pieces == 2:
        held, sems, grad_sems = refs[11 + outputs :]
    else:
        (sems,) = refs[11 + outputs :]
    shard, place = scalars[0], scalars[1]
    copies = [
        weight_copies(out_weights, full_out, sems, 0, shard),
        weight_copies(inner_weights, full_inner, sems, pieces, shard),
        weight_copies(outer_weights, full_outer, sems, 2 * pieces, shard),
    ]
    for group in copies:
        for copy in group:
            copy.start()
    model = rows.shape[1]
    hidden = full_inner.shape[1]
    att_low = attended[...].astype(low)
    for copy in copies[0]:
        copy.wait()
    normal_first, scale_first = norm_forward(mm(att_low, full_out[...]) + rows[...].astype(f32))
    middle = normal_first * vectors[5:6, :] + vectors[6:7, :]
    middle_low = middle.astype(low)
    for copy in copies[1]:
        copy.wait()
    for copy in copies[2]:
        copy.wait()
    wide = model
    total = None
    for start in range(0, hidden, wide):
        at = slice(start, start + wide)
        pre = mm(middle_low, full_inner[:, at]) + inner_bias[:, at]
        squared = pre * pre
        bent = jnp.tanh(0.7978845608028654 * pre * (1.0 + 0.044715 * squared))
        half = 0.5 * (1.0 + bent)
        act = (pre * half).astype(low)
        act_low[:, at] = act
        slope[:, at] = half + (0.5 * 0.7978845608028654) * pre * (1.0 - bent * bent) * (
            1.0 + (3 * 0.044715) * squared
        )
        share = mm(act, full_outer[at, :])
        total = share if total is None else total + share
    normal_second, scale_second = norm_forward(total + vectors[4:5, :] + middle)
    final = (normal_second * vectors[7:8, :] + vectors[8:9, :]).astype(low)
    for micro in range(out_content.shape[0]):
        start = 2 * run * micro
        out_content[micro] = final[start : start + run]
        out_query[micro] = final[start + run : start + 2 * run]
    d_final = cotangent[...].astype(f32)
    small[7:8, :] = column_sum(d_final * normal_second)
    small[8:9, :] = column_sum(d_final)
    d_final_in = norm_backward(d_final, vectors[7:8, :], normal_second, scale_second)
    d_outer = d_final_in.astype(low)
    small[4:5, :] = column_sum(d_outer.astype(f32))
    block = model // 2

    def hold_outer(start, value):
        if pieces == 1:
            grads[0][start : start + block, :] = value.astype(low)
            return
        half = hidden // 2
        target = (start // half) ^ shard
        for down in range(2):
            for across in range(2):
                chunk = ((start % half) // (block // 2) + down) * 2 + across
                held[(target, *block_index(chunk ^ place, 4), slice(0, block // 2), slice(None))] = value[
                    down * (block // 2) : (down + 1) * (block // 2), across * block : (across + 1) * block
                ].astype(low)

    def hold_inner(start, value):
        if pieces == 1:
            grads[1][:, start : start + block] = value.astype(low)
            return
        for quarter in range(4):
            chunk = (quarter % 2) * 8 + start // block
            held[
                ((quarter // 2) ^ shard, *block_index(chunk ^ place, 4), slice(block // 2, block), slice(None))
            ] = value[
                quarter * (block // 2) : (quarter + 1) * (block // 2), :
            ].astype(low)

    for start in range(0, hidden, block):
        hold_outer(start, mm_tn(act_low[:, start : start + block], d_outer))
    d_middle = d_final_in
    for start in range(0, hidden, block):
        at = slice(start, start + block)
        d_inner = (mm_nt(d_outer, full_outer[at, :]) * slope[:, at]).astype(low)
        summed = column_sum(d_inner.astype(f32))
        row, lane = start // model, start % model
        small[row : row + 1, lane : lane + block] = summed
        hold_inner(start, mm_tn(middle_low, d_inner))
        d_middle = d_middle + mm_nt(d_inner, full_inner[:, at])
    sent = []
    for part, (start, height) in enumerate(routes):
        for side in range(2):
            for which in range(2):
                rows_at = (pl.ds(start, height), slice(None))
                source = held.at[(side, *half_at(routes_out[part][0], which, 4), *rows_at)]
                target = grads[2 * side + which].at[(*(slice(None),) * 3, *rows_at)]
                sent.append(pltpu.make_async_copy(source, target, grad_sems.at[4 * part + 2 * side + which]))
    for copy in sent:
        copy.start()
    small[5:6, :] = column_sum(d_middle * normal_first)
    small[6:7, :] = column_sum(d_middle)
    small[9:16, :] = jnp.zeros((7, model), f32)
    d_mid = norm_backward(d_middle, vectors[5:6, :], normal_first, scale_first)
    d_mid_in[...] = d_mid
    d_branch = d_mid.astype(low)
    d_branch_out[...] = d_branch
    d_att[...] = mm_nt(d_branch, full_out[...]).astype(low)
    for copy in sent:
        copy.wait()


def back_kernel(
    run,
    slots,
    scalars,
    query_low,
    query_segment,
    keys,
    values,
    probs,
    d_att,
    attended,
    vectors,
    d_query,
    d_keys,
    d_values,
    small,
    buckets,
):
    micro = pl.program_id(1)
    base, lo = scalar_at(scalars, micro, 0), scalar_at(scalars, micro, 1)
    span = slots * run
    first, mask_a, mask_b = head_masks()
    gradient = d_att[...]
    stacked = jnp.concatenate([gradient * mask_a, gradient * mask_b], axis=0)
    product = gradient.astype(f32) * attended[...]
    delta_a = jnp.sum(jnp.where(first, product, 0.0), axis=-1, keepdims=True)
    delta_b = jnp.sum(jnp.where(first, 0.0, product), axis=-1, keepdims=True)
    delta_row = jnp.concatenate([delta_a, delta_b], axis=0)
    probs_low = probs[0]
    d_probs = mm_nt(stacked, values[...])
    d_scores = (probs_low.astype(f32) * (d_probs - delta_row)).astype(low)
    left = stack_query(query_low[...], query_segment[...], mask_a, mask_b)
    right = stack_keys(keys[...], vectors[...], lo)
    d_left = mm(d_scores, right) * 0.125
    mine = jnp.concatenate([first, first], axis=1)
    d_left = jnp.where(mine, d_left[: 2 * run], d_left[2 * run :])
    d_content, d_segment = d_left[:, :128], d_left[:, 128:]
    d_query[...] = (d_content + d_segment).astype(low)
    d_right = mm_tn(d_scores, left) * 0.125
    d_keys[...] = d_right[:, :128].astype(low)
    d_values[...] = mm_tn(probs_low, stacked).astype(low)
    row = lax.broadcasted_iota(jnp.int32, (span, 1), 0)
    d_embed = d_right[:, 128:]
    shares = jnp.concatenate(
        [
            column_sum(d_content),
            column_sum(d_segment),
            column_sum(jnp.where(row >= lo, 0.0, d_embed)),
            column_sum(jnp.where(row >= lo, d_embed, 0.0)),
            jnp.zeros((4, 128), f32),
        ],
        axis=0,
    )
    delta, _ = offsets_of(base, run, span)
    exact = d_scores.astype(f32)
    tallies = []
    for head in range(2):
        at = 2 * run * head
        both = exact[at : at + run] + exact[at + run : at + 2 * run]
        rows = [None] * 16
        rows[0] = column_sum(jnp.where(delta == 0, both, 0.0))
        for step, threshold in enumerate(thresholds):
            if threshold < span:
                later = thresholds[step + 1] if step + 1 < len(thresholds) else span
                above = (delta >= threshold) & (delta < later)
                below = (delta <= -threshold) & (delta > -later)
                rows[1 + step] = column_sum(jnp.where(above, both, 0.0))
                rows[9 + step] = column_sum(jnp.where(below, both, 0.0))
        blank = jnp.zeros((1, span), f32)
        tallies.append(jnp.concatenate([blank if entry is None else entry for entry in rows], axis=0))

    @pl.when(micro == 0)
    def _():
        small[...] = shares
        for head in range(2):
            buckets[head] = tallies[head]

    @pl.when(micro != 0)
    def _():
        small[...] += shares
        for head in range(2):
            buckets[head] += tallies[head]


def weights_kernel(
    pieces,
    run,
    slots,
    scalars,
    found,
    rows,
    path,
    attended,
    d_branch,
    d_query,
    d_keys,
    d_values,
    d_mid_in,
    small_first,
    small_second,
    tallies,
    *refs,
):
    weights = [refs[i * pieces : (i + 1) * pieces] for i in range(3)]
    refs = refs[3 * pieces :]
    d_content, d_state = refs[:2]
    model = rows.shape[1]
    block = model // 2
    if pieces == 2:
        kept, sent, full, tree, held, sems, grad_sems = refs[2:4], refs[4:6], *refs[6:]
    else:
        natural, tree_out, small_out, full, tree, sems, grad_sems = refs[2:6], *refs[6:]
    shard, place = scalars[0], scalars[1]
    copies = [weight_copies(weights[i], full.at[i], sems, i * pieces, shard) for i in range(3)]
    for group in copies:
        for copy in group:
            copy.start()
    small_rows = block // 8

    def hold(which, value):
        if pieces == 1:
            natural[which][...] = value.astype(low)
            return
        for half in range(2):
            for down in range(8):
                for across in range(2):
                    start = half * block + down * small_rows
                    spot = slice(which * small_rows, (which + 1) * small_rows)
                    held[(half ^ shard, *block_index((down * 2 + across) ^ place, 4), spot, slice(None))] = value[
                        start : start + small_rows, across * block : (across + 1) * block
                    ].astype(low)

    hold(0, mm_tn(rows[...], d_query[...]))
    hold(1, mm_tn(path[...], d_keys[...]))
    hold(2, mm_tn(path[...], d_values[...]))
    hold(3, mm_tn(attended[...].astype(low), d_branch[...]))
    ones = jnp.ones((8, tallies.shape[2]), f32)
    sums = []
    for head in range(tallies.shape[0]):
        sums.append(
            lax.dot_general(
                ones,
                tallies[head],
                (((1,), (1,)), ((), ())),
                precision=lax.Precision.HIGHEST,
                preferred_element_type=f32,
            )[:1]
        )
    buckets = jnp.concatenate(sums, axis=0)
    if pieces == 1:
        small_out[:9, :] = small_first[:9, :]
        small_out[9:13, :] = small_second[:4, :]
        small_out[13:, :] = jnp.zeros((small_out.shape[0] - 13, model), f32)
        small_out[16 : 16 + buckets.shape[0], :16] = buckets
    else:
        last = model // 4
        for half in range(2):
            at = slice(half * block, (half + 1) * block)
            lines = [
                small_first[2 * half + i // 2 : 2 * half + i // 2 + 1, (i % 2) * block : (i % 2 + 1) * block]
                for i in range(4)
            ]
            lines += [small_first[i : i + 1, at] for i in range(4, 9)]
            lines += [small_second[i : i + 1, at] for i in range(4)]
            for chunk in range(16):
                line = lines[chunk].astype(low) if chunk < 13 else jnp.zeros((1, block), low)
                spread_line = jnp.concatenate([line.astype(f32), jnp.zeros((15, block), f32)], axis=0)
                held[(half ^ shard, *block_index(chunk ^ place, 4), slice(last, last + 16), slice(None))] = spread_line.astype(low)
            wide = jnp.concatenate(
                [buckets[:, 8 * half : 8 * half + 8], jnp.zeros((buckets.shape[0], block - 8), f32)], axis=1
            )
            wide = jnp.concatenate([wide, jnp.zeros((16 - buckets.shape[0], block), f32)], axis=0)
            held[(half ^ shard, *block_index(13 ^ place, 4), slice(last, last + 16), slice(None))] = wide.astype(low)
    leaving = []
    if pieces == 2:
        for part, (start, height) in enumerate(later_cuts(model)):
            for which in range(2):
                at = 2 * part + which
                rows_at = (pl.ds(start, height), slice(None))
                for side in range(2):
                    source = held.at[(side, *half_at(routes_out[part][0], which, 4), *rows_at)]
                    target = (kept, sent)[side][which].at[(*(slice(None),) * 3, *rows_at)]
                    leaving.append(pltpu.make_async_copy(source, target, grad_sems.at[6 * side + at]))
        for copy in leaving:
            copy.start()
    for group in copies:
        for copy in group:
            copy.wait()
    tree[...] = jnp.zeros(tree.shape, tree.dtype)
    span = slots * run
    micro_count = rows.shape[0] // (2 * run)
    for micro in range(micro_count):
        at = slice(micro * span, (micro + 1) * span)
        shares = mm_nt(d_keys[at, :], full[1]) + mm_nt(d_values[at, :], full[2])
        for slot in range(slots):
            relative = found[micro * slots + slot]
            for half in range(2):
                piece = shares[slot * run : (slot + 1) * run, half * block : (half + 1) * block]
                start = (half * micro_count + micro) * run
                spot = (*block_index(relative, len(tree.shape) - 2), slice(start, start + run), slice(None))
                tree[spot] = (tree[spot].astype(f32) + piece).astype(low)
    if pieces == 2:
        last_copies = []
        skip = model // 4 + 16
        for part, (start, height) in enumerate(tree_cuts(tree.shape[-2])):
            for which in range(2):
                source = tree.at[(*half_at(routes_out[part][0], which, 4), pl.ds(start, height), slice(None))]
                target = kept[which].at[(*(slice(None),) * 3, pl.ds(skip + start, height), slice(None))]
                last_copies.append(pltpu.make_async_copy(source, target, grad_sems.at[12 + 2 * part + which]))
    else:
        last_copies = [pltpu.make_async_copy(tree, tree_out, grad_sems.at[0])]
    for copy in last_copies:
        copy.start()
    d_both = d_mid_in[...] + mm_nt(d_query[...], full[0])
    for micro in range(micro_count):
        start = 2 * run * micro
        d_content[micro] = d_both[start : start + run]
        d_state[micro] = d_both[start + run : start + 2 * run]
    for copy in leaving + last_copies:
        copy.wait()


def collect_pieces(refs, held, sems):
    copies = []
    for part, route in enumerate(routes_out):
        for which in range(2):
            at = 2 * part + which
            target = held[part].at[(*half_index(route[0], which, 4), slice(None), slice(None))]
            copies.append(pltpu.make_async_copy(refs[at], target, sems.at[at]))
    for copy in copies:
        copy.start()
    for copy in copies:
        copy.wait()


def feed_spread_kernel(scalars, *refs):
    outer, inner, first, second, third, sems = refs[6:]
    collect_pieces(refs[:6], (first, second, third), sems)
    place = scalars[1]
    height, side = first.shape[-2:]
    total = 3 * height // 2
    for chunk in range(16):
        at = block_index(chunk ^ place, 4)
        down, across = (chunk // 2) * total, (chunk % 2) * side
        outer[down : down + height, across : across + side] = first[at].astype(f32)
        middle = second[at].astype(f32)
        outer[down + height : down + total, across : across + side] = middle[: total - height]
        down, across = (chunk // 8) * total, (chunk % 8) * side
        inner[down : down + total - height, across : across + side] = middle[total - height :]
        inner[down + total - height : down + total, across : across + side] = third[at].astype(f32)


def later_spread_kernel(scalars, *refs):
    weights, small, sources, sems = refs[6:10], refs[10], refs[11:14], refs[14]
    collect_pieces(refs[:6], sources, sems)
    place = scalars[1]
    side = sources[0].shape[-1]
    rows = weights[0].shape[0] // 8
    cuts = later_cuts(2 * side)
    for chunk in range(16):
        at = block_index(chunk ^ place, 4)
        down, across = (chunk // 2) * rows, (chunk % 2) * side
        for source, (start, height) in zip(sources, cuts):
            value = source[at].astype(f32)
            for which in range(4):
                begin, end = max(start, which * rows), min(start + height, (which + 1) * rows)
                if begin < end:
                    top = down + begin - which * rows
                    weights[which][top : top + end - begin, across : across + side] = value[begin - start : end - start]
            begin = 4 * rows
            if start <= begin < start + height:
                small[chunk] = value[begin - start : begin - start + 16]


routes_out = ((0, 1, 2), (1, 2, 0), (2, 0, 1))


def send(inputs, bit):
    count = lax.axis_size("dp")
    return lax.ppermute(inputs, "dp", [(i, i ^ (1 << bit)) for i in range(count)])


def half_dims(bit):
    return tuple(1 if i == bit_total() - 1 - bit else 2 for i in range(bit_total()))


def bit_total():
    return lax.axis_size("dp").bit_length() - 1


def extra_bits():
    return tuple(range(3, bit_total()))


def grow(held, bit):
    return jnp.concatenate([held, send(held, bit)], axis=bit_total() - 1 - bit)


def part_of(held, bit, which):
    total = bit_total()
    if held.ndim == 3:
        held = held.reshape((2,) * total + held.shape[1:])
    return lax.slice_in_dim(held, which, which + 1, axis=total - 1 - bit)


def scatter_rest(held, route):
    for bit in route + extra_bits()[::-1]:
        held = part_of(held, bit, 0) + send(part_of(held, bit, 1), bit)
    return held.reshape(held.shape[-2:])


def scatter_blocks(blocks, route):
    held = part_of(blocks, route[0], 0) + send(part_of(blocks, route[0], 1), route[0])
    return scatter_rest(held, route[1:])


def axis_of(bit):
    return bit_total() - 1 - bit


def sum_rounds(lower, upper, keep):
    ready = yield list(upper)
    held = [own + send(entry, route[0]) for own, entry, route in zip(lower, ready, routes_out)]
    for step in (1, 2):
        ready = yield [part_of(entry, route[step], 1) for entry, route in zip(held, routes_out)]
        held = [
            part_of(entry, route[step], 0) + send(other, route[step])
            for entry, other, route in zip(held, ready, routes_out)
        ]
    for bit in extra_bits()[::-1]:
        (ready,) = yield [jnp.concatenate([part_of(entry, bit, 1) for entry in held], axis=-2)]
        arrived = send(ready, bit)
        start, later = 0, []
        for entry in held:
            height = entry.shape[-2]
            later.append(part_of(entry, bit, 0) + arrived[..., start : start + height, :])
            start += height
        held = later
    shares = held
    joined = jnp.concatenate([entry[..., :rows, :] for entry, rows in zip(held, keep)], axis=-2)
    for bit in extra_bits():
        (ready,) = yield [joined]
        joined = jnp.concatenate([joined, send(ready, bit)], axis=axis_of(bit))
    start, held = 0, []
    for rows in keep:
        held.append(joined[..., start : start + rows, :])
        start += rows
    for step in (2, 1):
        ready = yield held
        held = [
            jnp.concatenate([entry, send(entry, route[step])], axis=axis_of(route[step]))
            for entry, route in zip(ready, routes_out)
        ]
    ready = yield held
    arrived = [send(entry, route[0]) for entry, route in zip(ready, routes_out)]
    return [piece for pair in zip(ready, arrived) for piece in pair], shares


class Rounds:
    def __init__(self, steps):
        self.steps = steps
        self.pending = next(steps)
        self.result = None

    def advance(self, ready):
        try:
            self.pending = self.steps.send(ready)
        except StopIteration as stop:
            self.pending, self.result = [], stop.value


def advance_after(group, other):
    joined = lax.optimization_barrier(list(group.pending) + list(other.pending))
    group.advance(joined[: len(group.pending)])


def advance_free(pending, others):
    joined = lax.optimization_barrier(list(pending) + list(others))
    return joined[: len(pending)], joined[len(pending) :]


def spread_dims(held, route):
    return jnp.expand_dims(held, axis_of(route[0]))


def advance_together(groups, others=()):
    joined = [entry for group in groups for entry in group.pending] + list(others)
    joined = lax.optimization_barrier(joined)
    for group in groups:
        count = len(group.pending)
        ready, joined = joined[:count], joined[count:]
        group.advance(ready)
    return joined


def shards(
    content,
    query_state,
    token_seg,
    positions,
    parent,
    w_query,
    w_key,
    w_value,
    w_out,
    w_inner,
    w_outer,
    b_inner,
    b_outer,
    gain_attn,
    bias_attn,
    gain_ffn,
    bias_ffn,
    bias_content,
    bias_segment,
    seg_embed,
    rel_table,
    cot_content,
    cot_query,
):
    micro_count, run, model = content.shape
    shard_count, dp_count = lax.axis_size("shard"), lax.axis_size("dp")
    shard, place = lax.axis_index("shard"), lax.axis_index("dp")
    heads = rel_table.shape[1]
    bucket_total = rel_table.shape[0] * shard_count
    hidden = w_inner.shape[1]
    pairs = heads // 2
    per_run = dp_count // tree_runs
    slots = path_runs * per_run
    span = slots * run
    rows_total = 2 * run * micro_count
    pieces = 2 if shard_count == 2 and dp_count == tree_runs else 1
    part_width = model // shard_count

    def fetch(weight):
        if pieces == 2:
            return [weight, lax.ppermute(weight, "shard", [(0, 1), (1, 0)])]
        return [lax.all_gather(weight, "shard", axis=0, tiled=True)]

    own_seg = token_seg[:, 0]
    own_slot = positions[:, 0] // run
    facts = jnp.stack([own_seg, own_slot], axis=1).reshape(2 * micro_count, 1).astype(low)
    fact_rows = jnp.broadcast_to(jnp.pad(facts, ((0, 16 - 2 * micro_count), (0, 0))), (16, model))
    third = model // 3
    columns = ((0, third), (third, third), (2 * third, third))
    content_rows = micro_count * run
    block = jnp.concatenate([content.reshape(content_rows, model), fact_rows], axis=0)
    total_bits = bit_total()
    block, b_inner, b_outer, parent, w_query, w_key = lax.optimization_barrier(
        (block, b_inner, b_outer, parent, w_query, w_key)
    )
    held = block.reshape((1,) * total_bits + block.shape)
    for bit in extra_bits():
        held = grow(held, bit)
    query_weights, key_weights = fetch(w_query), fetch(w_key)
    parts = []
    for part, (start, width) in enumerate(columns):
        height = block.shape[0] if part == 0 else content_rows
        parts.append(held[..., :height, start : start + width])
    parts, (query_weights[-1], key_weights[-1], w_value, w_out) = advance_free(
        parts, [query_weights[-1], key_weights[-1], w_value, w_out]
    )
    value_weights, out_weights = fetch(w_value), fetch(w_out)
    parts = [grow(piece, route[2]) for piece, route in zip(parts, routes_out)]
    parts, (value_weights[-1], out_weights[-1], w_inner) = advance_free(
        parts, [value_weights[-1], out_weights[-1], w_inner]
    )
    inner_weights = fetch(w_inner)
    parts = [grow(piece, route[1]) for piece, route in zip(parts, routes_out)]
    parts, (inner_weights[-1], w_outer) = advance_free(parts, [inner_weights[-1], w_outer])
    outer_weights = fetch(w_outer)
    tree_parts = [entry for piece, route in zip(parts, routes_out) for entry in (piece, send(piece, route[0]))]
    tree_parts, (outer_weights[-1],) = advance_free(tree_parts, [outer_weights[-1]])

    first_branch, first_leaf = trunk_runs * per_run, (trunk_runs + 1) * per_run
    mine = own_seg
    above = jnp.sum(jnp.where(jnp.arange(parent.shape[2]) == mine[:, None], parent[:, 0], 0), axis=1)
    trunk, leaf = mine == 0, mine > trunk_runs
    branch = jnp.where(leaf, above, mine)
    lo = jnp.where(trunk, 0, jnp.where(leaf, first_leaf, first_branch)) * run
    hi = jnp.where(trunk, first_branch, jnp.where(leaf, slots, first_leaf)) * run
    early = jnp.stack([shard, place]).astype(jnp.int32)
    facts_own = jnp.stack([own_slot * run, lo, hi, mine, branch], axis=1)
    scalars = jnp.concatenate([early, facts_own.reshape(-1)]).astype(jnp.int32)

    small_parts = jnp.concatenate(
        [
            b_inner.reshape(-1, part_width),
            jnp.stack([b_outer, gain_attn, bias_attn, gain_ffn, bias_ffn, bias_content, bias_segment]),
            seg_embed,
            jnp.pad(rel_table.reshape(1, -1), ((0, 0), (0, part_width - rel_table.size))),
        ],
        axis=0,
    )
    inner_rows = b_inner.shape[0] // part_width
    fill = 16 - small_parts.shape[0]
    small_parts = jnp.pad(small_parts, ((0, fill), (0, 0)))
    if pieces == 2:
        other = lax.ppermute(small_parts, "shard", [(0, 1), (1, 0)])
        gathered = jnp.where(shard == 0, jnp.stack([small_parts, other]), jnp.stack([other, small_parts]))
    else:
        gathered = lax.all_gather(small_parts, "shard", axis=0, tiled=False)
    gathered = gathered.astype(f32)
    inner_bias = gathered[:, :inner_rows].reshape(1, hidden)
    vectors = jnp.transpose(gathered, (1, 0, 2)).reshape(16, model)
    table = gathered[:, 13, : rel_table.size].reshape(bucket_total, heads)

    rows = jnp.concatenate([content, query_state], axis=1).reshape(rows_total, model)
    cotangent = jnp.concatenate([cot_content, cot_query], axis=1).reshape(rows_total, model)
    grown = pltpu.CompilerParams(vmem_limit_bytes=vmem_bytes)

    def shape(dims, kind):
        return jax.ShapeDtypeStruct(dims, kind)

    dma = pltpu.SemaphoreType.DMA
    query_low, query_segment = pl.pallas_call(
        functools.partial(query_kernel, pieces),
        out_shape=(shape((rows_total, model), low),) * 2,
        in_specs=[smem_space, vmem_space, vmem_space] + [any_space] * pieces,
        out_specs=(vmem_space,) * 2,
        scratch_shapes=[pltpu.VMEM((model, model), low), dma((pieces,))],
        compiler_params=grown,
        name="query_projection",
        cost_estimate=cost(4),
    )(early, rows, vectors, *query_weights)

    path, keys, values, found = pl.pallas_call(
        functools.partial(keys_kernel, pieces, columns, [route[0] for route in routes_out], run, slots),
        out_shape=(
            shape((micro_count, span, model), low),
            shape((micro_count * span, model), low),
            shape((micro_count * span, model), low),
            shape((micro_count * slots,), jnp.int32),
        ),
        in_specs=[smem_space] + [any_space] * (2 * len(columns) + 2 * pieces),
        out_specs=(vmem_space,) * 3 + (smem_space,),
        scratch_shapes=[
            pltpu.VMEM((model, model), low),
            pltpu.VMEM((model, model), low),
            pltpu.VMEM((2,) * total_bits + (content_rows + 16, model), low),
            dma((2 * pieces,)),
            dma((2 * len(columns),)),
        ],
        compiler_params=grown,
        name="path_keys",
        cost_estimate=cost(6),
    )(scalars, *tree_parts, *key_weights, *value_weights)
    path = path.reshape(micro_count * span, model)

    row_block = pl.BlockSpec((2 * run, 128), lambda pair, micro: (micro, pair))
    key_block = pl.BlockSpec((span, 128), lambda pair, micro: (micro, pair))
    vector_block = pl.BlockSpec((16, 128), lambda pair, micro: (0, pair))
    prob_block = pl.BlockSpec((1, 4 * run, span), lambda pair, micro: (pair * micro_count + micro, 0, 0))
    probs, attended = pl.pallas_call(
        functools.partial(attend_kernel, run, slots),
        grid=(pairs, micro_count),
        out_shape=(
            shape((pairs * micro_count, 4 * run, span), low),
            shape((rows_total, model), f32),
        ),
        in_specs=[smem_space, smem_space, row_block, row_block, key_block, key_block, vector_block],
        out_specs=(prob_block, row_block),
        compiler_params=grown,
        name="attend",
        cost_estimate=cost(11),
    )(scalars, table, query_low, query_segment, keys, values, vectors)

    half = model // 2
    if pieces == 2:
        grad_shapes = [shape((2,) * (total_bits - 1) + (half, half), low)] * 4
        grad_specs = [any_space] * len(grad_shapes)
        grad_scratch = [pltpu.VMEM((2,) * (1 + total_bits) + (half, half), low)]
    else:
        grad_shapes = [shape((hidden, model), low), shape((model, hidden), low)]
        grad_specs = [vmem_space] * 2
        grad_scratch = []
    results = pl.pallas_call(
        functools.partial(feed_kernel, pieces, run),
        out_shape=[
            shape((micro_count, run, model), low),
            shape((micro_count, run, model), low),
            shape((rows_total, model), f32),
            shape((rows_total, model), low),
            shape((rows_total, model), low),
            shape((16, model), f32),
        ]
        + grad_shapes,
        in_specs=[smem_space] + [vmem_space] * 5 + [any_space] * (3 * pieces),
        out_specs=[vmem_space] * 6 + grad_specs,
        scratch_shapes=[
            pltpu.VMEM((model, model), low),
            pltpu.VMEM((model, hidden), low),
            pltpu.VMEM((hidden, model), low),
            pltpu.VMEM((rows_total, hidden), low),
            pltpu.VMEM((rows_total, hidden), f32),
        ]
        + grad_scratch
        + [dma((3 * pieces,))]
        + ([dma((12,))] if pieces == 2 else []),
        compiler_params=grown,
        name="feed_forward",
        cost_estimate=cost(21),
    )(scalars, rows, attended, cotangent, vectors, inner_bias, *out_weights, *inner_weights, *outer_weights)
    out_content, out_query, d_mid_in, d_branch, d_att, small_first = results[:6]

    swap = [(0, 1), (1, 0)]
    if pieces == 2:
        feed_grads = results[6:]
        feed_other = [lax.ppermute(entry, "shard", swap) for entry in (feed_grads[3], feed_grads[2])]

    d_query, d_keys, d_values, small_second, tallies = pl.pallas_call(
        functools.partial(back_kernel, run, slots),
        grid=(pairs, micro_count),
        out_shape=(
            shape((rows_total, model), low),
            shape((micro_count * span, model), low),
            shape((micro_count * span, model), low),
            shape((8, model), f32),
            shape((heads, 16, span), f32),
        ),
        in_specs=[smem_space, row_block, row_block, key_block, key_block, prob_block, row_block, row_block, vector_block],
        out_specs=(
            row_block,
            key_block,
            key_block,
            pl.BlockSpec((8, 128), lambda pair, micro: (0, pair)),
            pl.BlockSpec((2, 16, span), lambda pair, micro: (pair, 0, 0)),
        ),
        compiler_params=grown,
        name="attend_back",
        cost_estimate=cost(14),
    )(scalars, query_low, query_segment, keys, values, probs, d_att, attended, vectors)

    if pieces == 2:
        sizes = [height for _, height in feed_cuts(pieces, model)]
        upper = [
            spread_dims(feed_grads[1][..., start : start + height, :] + feed_other[0][..., start : start + height, :], route)
            for (start, height), route in zip(feed_cuts(pieces, model), routes_out)
        ]
        feed_lower = feed_other[1]
        *upper, feed_lower, d_query = lax.optimization_barrier((*upper, feed_lower, d_query))
        lower = [
            spread_dims(feed_grads[0][..., start : start + height, :] + feed_lower[..., start : start + height, :], route)
            for (start, height), route in zip(feed_cuts(pieces, model), routes_out)
        ]
        feed_rounds = Rounds(sum_rounds(lower, upper, sizes))
        feed_rounds.advance(feed_rounds.pending)
    tree_height = 2 * micro_count * run
    if pieces == 2:
        whole = later_cuts(model)[-1][0] + later_cuts(model)[-1][1]
        heights = [entry[1] for entry in later_cuts(model)]
        grad_shapes = [shape((2,) * (total_bits - 1) + (whole + tree_height, half), low)] * 2
        grad_shapes += [shape((2,) * (total_bits - 1) + (whole, half), low)] * 2
        grad_specs = [any_space] * 4
        extra = [pltpu.VMEM((2,) * (1 + total_bits) + (whole, half), low)]
    else:
        grad_shapes = [shape((model, model), low)] * 4 + [
            shape((2,) * total_bits + (tree_height, half), low),
            shape((32, model), f32),
        ]
        grad_specs = [vmem_space] * 4 + [any_space, vmem_space]
        extra = []
    later = pl.pallas_call(
        functools.partial(weights_kernel, pieces, run, slots),
        out_shape=[shape((micro_count, run, model), f32)] * 2 + grad_shapes,
        in_specs=[smem_space] * 2 + [vmem_space] * 11 + [any_space] * (3 * pieces),
        out_specs=[vmem_space] * 2 + grad_specs,
        scratch_shapes=[pltpu.VMEM((3, model, model), low), pltpu.VMEM((2,) * total_bits + (tree_height, half), low)]
        + extra
        + [dma((3 * pieces,)), dma((18,))],
        compiler_params=grown,
        name="weight_gradients",
        cost_estimate=cost(15),
    )(
        scalars,
        found,
        rows,
        path,
        attended,
        d_branch,
        d_query,
        d_keys,
        d_values,
        d_mid_in,
        small_first,
        small_second,
        tallies,
        *query_weights,
        *key_weights,
        *value_weights,
    )
    d_content, grad_query = later[:2]

    if pieces == 2:
        feed_rounds.pending, others = advance_free(feed_rounds.pending, [later[5], later[4]])
        others = [lax.ppermute(entry, "shard", swap) for entry in others]
        feed_rounds.advance(feed_rounds.pending)
        feed_rounds.pending, others = advance_free(feed_rounds.pending, others)
        feed_rounds.advance(feed_rounds.pending)

        def route_sum(mine, other, part):
            start, height = later_cuts(model)[part]
            more, tall = tree_cuts(tree_height)[part]
            summed = mine[..., start : start + height, :] + other[..., start : start + height, :]
            more_rows = mine[..., whole + more : whole + more + tall, :]
            return spread_dims(jnp.concatenate([summed, more_rows], axis=-2), routes_out[part])

        lower = [route_sum(later[2], others[1], part) for part in range(3)]
        upper = [route_sum(later[3], others[0], part) for part in range(3)]
        later_rounds = Rounds(sum_rounds(lower, upper, heights))
        for _ in range(5):
            advance_after(later_rounds, feed_rounds)
            feed_rounds.advance(feed_rounds.pending)
        advance_together([later_rounds])
        feed_done = advance_together([later_rounds], feed_rounds.result[0])
        advance_together([later_rounds])

        def pieces_scratch(sizes):
            return [pltpu.VMEM((2,) * total_bits + (height, half), low) for height in sizes] + [dma((6,))]

        grad_w_outer, grad_w_inner = pl.pallas_call(
            feed_spread_kernel,
            out_shape=(shape(w_outer.shape, f32), shape(w_inner.shape, f32)),
            in_specs=[smem_space] + [any_space] * 6,
            out_specs=(vmem_space,) * 2,
            scratch_shapes=pieces_scratch([height for _, height in feed_cuts(pieces, model)]),
            compiler_params=grown,
            name="feed_spread",
            cost_estimate=cost(7),
        )(early, *feed_done)
        later_done, shares = later_rounds.result
        arrived = [share.reshape(share.shape[-2:])[rows:] for share, rows in zip(shares, heights)]
        tree_grad = jnp.concatenate(arrived, axis=0)
        *squares, small = pl.pallas_call(
            later_spread_kernel,
            out_shape=[shape(w_query.shape, f32)] * 4 + [shape((dp_count, 16, half), f32)],
            in_specs=[smem_space] + [any_space] * 6,
            out_specs=[vmem_space] * 5,
            scratch_shapes=pieces_scratch(heights),
            compiler_params=grown,
            name="later_spread",
            cost_estimate=cost(4),
        )(early, *later_done)
        grad_w_query, grad_w_key, grad_w_value, grad_w_out = squares
        grad_b_inner = small[:4, 0].reshape(-1)
        narrow = small[4:13, 0]
        grad_rel_table = jnp.transpose(small[13, :heads, : rel_table.shape[0]])
    else:
        totals = []
        for entry in (*results[6:8], *later[2:6]):
            share = lax.psum_scatter(entry, "shard", scatter_dimension=0, tiled=True)
            totals.append(lax.psum(share, "dp").astype(f32))
        grad_w_outer, grad_w_inner, grad_w_query, grad_w_key, grad_w_value, grad_w_out = totals
        tree_grad = scatter_blocks(later[6], routes_out[0])
        small = lax.psum(later[7], ("shard", "dp"))
        grad_b_inner = lax.dynamic_slice_in_dim(small[:4].reshape(-1), shard * b_inner.shape[0], b_inner.shape[0])
        narrow = lax.dynamic_slice_in_dim(small[4:13], shard * part_width, part_width, axis=1)
        grad_rel_table = lax.dynamic_slice_in_dim(
            jnp.transpose(small[16 : 16 + heads, :bucket_total]), shard * rel_table.shape[0], rel_table.shape[0], axis=0
        )
    halves = tree_grad.astype(f32).reshape(2, micro_count, run, half)
    grad_content = d_content + jnp.concatenate([halves[0], halves[1]], axis=-1)
    return (
        out_content,
        out_query,
        grad_content,
        grad_query,
        grad_w_query,
        grad_w_key,
        grad_w_value,
        grad_w_out,
        grad_w_inner,
        grad_w_outer,
        grad_b_inner,
        narrow[0],
        narrow[1],
        narrow[2],
        narrow[3],
        narrow[4],
        narrow[5],
        narrow[6],
        narrow[7:9],
        grad_rel_table,
    )


def solution(mesh):
    rows = P(None, ("shard", "dp"), None)
    tokens = P(None, ("shard", "dp"))
    matrix = P("shard", None)
    vector = P("shard")
    return jax.shard_map(
        shards,
        mesh=mesh,
        in_specs=(rows, rows, tokens, tokens, P(None, "shard", None))
        + (matrix,) * 6
        + (vector,) * 8
        + (P(None, "shard"), matrix, rows, rows),
        out_specs=(rows,) * 4 + (matrix,) * 6 + (vector,) * 8 + (P(None, "shard"), matrix),
        check_vma=False,
    )
```

```python
import functools

import jax
import jax.numpy as jnp
from jax import lax
from jax.experimental import pallas as pl
from jax.experimental.pallas import tpu as pltpu
from jax.sharding import PartitionSpec as P

thresholds = (1, 2, 4, 8, 32, 128, 512)
norm_eps = 1e-05
masked_score = -1e30
path_runs = 6
trunk_runs = 4
tree_runs = 16
vmem_bytes = 60 * 1024 * 1024
low = jnp.bfloat16
f32 = jnp.float32
def cost(microseconds):
    return pl.CostEstimate(flops=int(microseconds * 1e9), bytes_accessed=0, transcendentals=0)


any_space = pl.BlockSpec(memory_space=pl.ANY)
smem_space = pl.BlockSpec(memory_space=pltpu.SMEM)
vmem_space = pl.BlockSpec(memory_space=pltpu.VMEM)


def mm(left, right):
    return lax.dot_general(left, right, (((1,), (0,)), ((), ())), preferred_element_type=f32)


def mm_nt(left, right):
    return lax.dot_general(left, right, (((1,), (1,)), ((), ())), preferred_element_type=f32)


def mm_tn(left, right):
    return lax.dot_general(left, right, (((0,), (0,)), ((), ())), preferred_element_type=f32)


def weight_copies(pieces, target, sems, first, shard):
    if len(pieces) == 1:
        return [pltpu.make_async_copy(pieces[0], target, sems.at[first])]
    half = pieces[0].shape[0]
    own = pl.multiple_of(shard * half, 16)
    other = pl.multiple_of((1 - shard) * half, 16)
    return [
        pltpu.make_async_copy(pieces[0], target.at[pl.ds(own, half)], sems.at[first]),
        pltpu.make_async_copy(pieces[1], target.at[pl.ds(other, half)], sems.at[first + 1]),
    ]


def scalar_at(scalars, micro, entry):
    return scalars[2 + 5 * micro + entry]


def block_index(at, total):
    return tuple((at >> (total - 1 - i)) & 1 for i in range(total))


def half_index(bit, which, total):
    everything = [slice(None)] * total
    everything[total - 1 - bit] = pl.ds(which, 1)
    return tuple(everything)


def half_at(bit, which, total):
    everything = [slice(None)] * total
    everything[total - 1 - bit] = which
    return tuple(everything)


def query_kernel(pieces, scalars, rows, vectors, *refs):
    weights = refs[:pieces]
    query_low, query_segment, full, sems = refs[pieces:]
    copies = weight_copies(weights, full, sems, 0, scalars[0])
    for copy in copies:
        copy.start()
    for copy in copies:
        copy.wait()
    raw = mm(rows[...], full[...])
    query_low[...] = (raw + vectors[9:10, :]).astype(low)
    query_segment[...] = (raw + vectors[10:11, :]).astype(low)


def keys_kernel(pieces, columns, lasts, run, slots, scalars, *refs):
    parts = refs[: 2 * len(columns)]
    refs = refs[2 * len(columns) :]
    key_weights, value_weights = refs[:pieces], refs[pieces : 2 * pieces]
    path, keys, values, found, full_key, full_value, tree, sems, tree_sems = refs[2 * pieces :]
    shard = scalars[0]
    total = len(tree.shape) - 2
    moves = []
    for part, (start, width) in enumerate(columns):
        for which in range(2):
            source = parts[2 * part + which]
            target = tree.at[
                (*half_index(lasts[part], which, total), pl.ds(0, source.shape[-2]), pl.ds(start, width))
            ]
            moves.append(pltpu.make_async_copy(source, target, tree_sems.at[2 * part + which]))
    copies = weight_copies(key_weights, full_key, sems, 0, shard)
    copies = copies + weight_copies(value_weights, full_value, sems, pieces, shard)
    for copy in moves + copies:
        copy.start()
    for copy in moves:
        copy.wait()
    micro_count = path.shape[0]
    content_rows = micro_count * run
    facts = [
        tree[(*block_index(block, total), slice(content_rows, content_rows + 16), slice(0, 128))].astype(f32)
        for block in range(1 << total)
    ]
    numbers = lax.broadcasted_iota(jnp.int32, (1 << total, 128), 0)
    for micro in range(micro_count):
        segs = jnp.concatenate([entry[2 * micro : 2 * micro + 1] for entry in facts], axis=0).astype(jnp.int32)
        places = jnp.concatenate([entry[2 * micro + 1 : 2 * micro + 2] for entry in facts], axis=0).astype(jnp.int32)
        for slot in range(slots):
            if slot < slots // path_runs * trunk_runs:
                wanted = 0
            else:
                wanted = scalar_at(scalars, micro, 4 if slot < slots // path_runs * (trunk_runs + 1) else 3)
            shown = (segs == wanted) & (places == slot)
            relative = jnp.max(jnp.where(shown, numbers, 0))
            found[micro * slots + slot] = relative
            at = block_index(relative, total)
            path[micro, slot * run : (slot + 1) * run, :] = tree[(*at, slice(micro * run, (micro + 1) * run), slice(None))]
    for copy in copies:
        copy.wait()
    for micro in range(micro_count):
        rows = path[micro]
        span = slots * run
        keys[micro * span : (micro + 1) * span, :] = mm(rows, full_key[...]).astype(low)
        values[micro * span : (micro + 1) * span, :] = mm(rows, full_value[...]).astype(low)


def head_masks():
    lane = lax.broadcasted_iota(jnp.int32, (1, 128), 1)
    first = lane < 64
    return first, first.astype(f32).astype(low), (1.0 - first.astype(f32)).astype(low)


def stack_query(query_low, query_segment, mask_a, mask_b):
    both = jnp.concatenate([query_low, query_segment], axis=1)
    wide_a = jnp.concatenate([mask_a, mask_a], axis=1)
    wide_b = jnp.concatenate([mask_b, mask_b], axis=1)
    return jnp.concatenate([both * wide_a, both * wide_b], axis=0)


def stack_keys(keys, vectors, lo):
    row = lax.broadcasted_iota(jnp.int32, (keys.shape[0], 1), 0)
    segment = jnp.where(row >= lo, vectors[12:13, :], vectors[11:12, :]).astype(low)
    return jnp.concatenate([keys, segment], axis=1)


def offsets_of(base, run, span):
    row = lax.broadcasted_iota(jnp.int32, (run, span), 0)
    column = lax.broadcasted_iota(jnp.int32, (run, span), 1)
    return base + row - column, column


def attend_kernel(run, slots, scalars, table, query_low, query_segment, keys, values, vectors, probs, attended):
    pair = pl.program_id(0)
    span = slots * run
    first, mask_a, mask_b = head_masks()
    for micro in range(probs.shape[0]):
        base, lo, hi = (scalar_at(scalars, micro, entry) for entry in range(3))
        rows = slice(micro * 2 * run, (micro + 1) * 2 * run)
        columns = slice(micro * span, (micro + 1) * span)
        left = stack_query(query_low[rows, :], query_segment[rows, :], mask_a, mask_b)
        right = stack_keys(keys[columns, :], vectors[...], lo)
        raw = mm_nt(left, right)
        delta, column = offsets_of(base, run, span)
        visible = column < hi
        biases = []
        for head in range(2):
            at = 2 * pair + head
            bias = jnp.full((run, span), table[0, at], f32)
            for step, threshold in enumerate(thresholds):
                if threshold < span:
                    bias = jnp.where(delta >= threshold, table[1 + step, at], bias)
                    bias = jnp.where(delta <= -threshold, table[9 + step, at], bias)
            bias = jnp.where(visible, bias, masked_score)
            biases.append(bias)
            biases.append(jnp.where(delta == 0, masked_score, bias))
        scores = raw * 0.125 + jnp.concatenate(biases, axis=0)
        peak = jnp.max(scores, axis=-1, keepdims=True)
        mass = jnp.exp(scores - peak)
        total = jnp.sum(mass, axis=-1, keepdims=True)
        probs_low = (mass * (1.0 / total)).astype(low)
        probs[micro] = probs_low
        heads = mm(probs_low, values[columns, :])
        attended[rows, :] = jnp.where(first, heads[: 2 * run], heads[2 * run :])


def norm_forward(inputs):
    centred = inputs - jnp.mean(inputs, axis=-1, keepdims=True)
    scale = lax.rsqrt(jnp.mean(centred * centred, axis=-1, keepdims=True) + norm_eps)
    return centred * scale, scale


def norm_backward(gradient, gain, normal, scale):
    d_normal = gradient * gain
    mean_first = jnp.mean(d_normal, axis=-1, keepdims=True)
    mean_second = jnp.mean(d_normal * normal, axis=-1, keepdims=True)
    return scale * (d_normal - mean_first - normal * mean_second)


def column_sum(inputs):
    return jnp.sum(inputs, axis=0, keepdims=True)


def feed_cuts(pieces, model):
    if pieces == 1:
        return ()
    step = model // 6
    return ((0, step), (step, step), (2 * step, step))


def later_cuts(model):
    whole = model // 4 + 16
    step = whole // 40 * 16
    return ((0, step), (step, step), (2 * step, whole - 2 * step))


def tree_cuts(height):
    step = height // 48 * 16 + 16
    return ((0, step), (step, step), (2 * step, height - 2 * step))


def feed_kernel(pieces, run, scalars, rows, attended, cotangent, vectors, inner_bias, *refs):
    out_weights, inner_weights, outer_weights = (refs[i * pieces : (i + 1) * pieces] for i in range(3))
    refs = refs[3 * pieces :]
    out_content, out_query, d_mid_in, d_branch_out, d_att, small = refs[:6]
    routes = feed_cuts(pieces, rows.shape[1])
    outputs = 4 if pieces == 2 else 2
    grads = refs[6 : 6 + outputs]
    full_out, full_inner, full_outer, act_low, slope = refs[6 + outputs : 11 + outputs]
    if pieces == 2:
        held, sems, grad_sems = refs[11 + outputs :]
    else:
        (sems,) = refs[11 + outputs :]
    shard, place = scalars[0], scalars[1]
    copies = [
        weight_copies(out_weights, full_out, sems, 0, shard),
        weight_copies(inner_weights, full_inner, sems, pieces, shard),
        weight_copies(outer_weights, full_outer, sems, 2 * pieces, shard),
    ]
    for group in copies:
        for copy in group:
            copy.start()
    model = rows.shape[1]
    hidden = full_inner.shape[1]
    att_low = attended[...].astype(low)
    for copy in copies[0]:
        copy.wait()
    normal_first, scale_first = norm_forward(mm(att_low, full_out[...]) + rows[...].astype(f32))
    middle = normal_first * vectors[5:6, :] + vectors[6:7, :]
    middle_low = middle.astype(low)
    for copy in copies[1]:
        copy.wait()
    wide = model
    total = None
    for start in range(0, hidden, wide):
        at = slice(start, start + wide)
        pre = mm(middle_low, full_inner[:, at]) + inner_bias[:, at]
        squared = pre * pre
        bent = jnp.tanh(0.7978845608028654 * pre * (1.0 + 0.044715 * squared))
        half = 0.5 * (1.0 + bent)
        act = (pre * half).astype(low)
        act_low[:, at] = act
        slope[:, at] = half + (0.5 * 0.7978845608028654) * pre * (1.0 - bent * bent) * (
            1.0 + (3 * 0.044715) * squared
        )
        if start == 0:
            for copy in copies[2]:
                copy.wait()
        share = mm(act, full_outer[at, :])
        total = share if total is None else total + share
    normal_second, scale_second = norm_forward(total + vectors[4:5, :] + middle)
    final = (normal_second * vectors[7:8, :] + vectors[8:9, :]).astype(low)
    for micro in range(out_content.shape[0]):
        start = 2 * run * micro
        out_content[micro] = final[start : start + run]
        out_query[micro] = final[start + run : start + 2 * run]
    d_final = cotangent[...].astype(f32)
    small[7:8, :] = column_sum(d_final * normal_second)
    small[8:9, :] = column_sum(d_final)
    d_final_in = norm_backward(d_final, vectors[7:8, :], normal_second, scale_second)
    d_outer = d_final_in.astype(low)
    small[4:5, :] = column_sum(d_outer.astype(f32))
    block = model // 2

    def hold_outer(start, value):
        if pieces == 1:
            grads[0][start : start + block, :] = value.astype(low)
            return
        half = hidden // 2
        target = (start // half) ^ shard
        for down in range(2):
            for across in range(2):
                chunk = ((start % half) // (block // 2) + down) * 2 + across
                held[(target, *block_index(chunk ^ place, 4), slice(0, block // 2), slice(None))] = value[
                    down * (block // 2) : (down + 1) * (block // 2), across * block : (across + 1) * block
                ].astype(low)

    def hold_inner(start, value):
        if pieces == 1:
            grads[1][:, start : start + block] = value.astype(low)
            return
        for quarter in range(4):
            chunk = (quarter % 2) * 8 + start // block
            held[
                ((quarter // 2) ^ shard, *block_index(chunk ^ place, 4), slice(block // 2, block), slice(None))
            ] = value[
                quarter * (block // 2) : (quarter + 1) * (block // 2), :
            ].astype(low)

    for start in range(0, hidden, block):
        hold_outer(start, mm_tn(act_low[:, start : start + block], d_outer))
    sent = []
    for part, (start, height) in enumerate(routes):
        for side in range(2):
            for which in range(2):
                rows_at = (pl.ds(start, height), slice(None))
                source = held.at[(side, *half_at(routes_out[part][0], which, 4), *rows_at)]
                target = grads[2 * side + which].at[(*(slice(None),) * 3, *rows_at)]
                sent.append(pltpu.make_async_copy(source, target, grad_sems.at[4 * part + 2 * side + which]))
    for copy in sent[:4]:
        copy.start()
    d_middle = d_final_in
    for start in range(0, hidden, block):
        at = slice(start, start + block)
        d_inner = (mm_nt(d_outer, full_outer[at, :]) * slope[:, at]).astype(low)
        summed = column_sum(d_inner.astype(f32))
        row, lane = start // model, start % model
        small[row : row + 1, lane : lane + block] = summed
        hold_inner(start, mm_tn(middle_low, d_inner))
        d_middle = d_middle + mm_nt(d_inner, full_inner[:, at])
    for copy in sent[4:]:
        copy.start()
    small[5:6, :] = column_sum(d_middle * normal_first)
    small[6:7, :] = column_sum(d_middle)
    small[9:16, :] = jnp.zeros((7, model), f32)
    d_mid = norm_backward(d_middle, vectors[5:6, :], normal_first, scale_first)
    d_mid_in[...] = d_mid
    d_branch = d_mid.astype(low)
    d_branch_out[...] = d_branch
    d_att[...] = mm_nt(d_branch, full_out[...]).astype(low)
    for copy in sent:
        copy.wait()


def back_kernel(
    run,
    slots,
    scalars,
    query_low,
    query_segment,
    keys,
    values,
    probs,
    d_att,
    attended,
    vectors,
    d_query,
    d_keys,
    d_values,
    small,
    buckets,
):
    span = slots * run
    first, mask_a, mask_b = head_masks()
    shares = jnp.zeros((8, 128), f32)
    tallies = [jnp.zeros((16, span), f32)] * 2
    for micro in range(probs.shape[0]):
        base, lo = scalar_at(scalars, micro, 0), scalar_at(scalars, micro, 1)
        rows = slice(micro * 2 * run, (micro + 1) * 2 * run)
        columns = slice(micro * span, (micro + 1) * span)
        gradient = d_att[rows, :]
        stacked = jnp.concatenate([gradient * mask_a, gradient * mask_b], axis=0)
        product = gradient.astype(f32) * attended[rows, :]
        delta_a = jnp.sum(jnp.where(first, product, 0.0), axis=-1, keepdims=True)
        delta_b = jnp.sum(jnp.where(first, 0.0, product), axis=-1, keepdims=True)
        delta_row = jnp.concatenate([delta_a, delta_b], axis=0)
        probs_low = probs[micro]
        d_probs = mm_nt(stacked, values[columns, :])
        d_scores = (probs_low.astype(f32) * (d_probs - delta_row)).astype(low)
        left = stack_query(query_low[rows, :], query_segment[rows, :], mask_a, mask_b)
        right = stack_keys(keys[columns, :], vectors[...], lo)
        d_left = mm(d_scores, right) * 0.125
        mine = jnp.concatenate([first, first], axis=1)
        d_left = jnp.where(mine, d_left[: 2 * run], d_left[2 * run :])
        d_content, d_segment = d_left[:, :128], d_left[:, 128:]
        d_query[rows, :] = (d_content + d_segment).astype(low)
        d_right = mm_tn(d_scores, left) * 0.125
        d_keys[columns, :] = d_right[:, :128].astype(low)
        d_values[columns, :] = mm_tn(probs_low, stacked).astype(low)
        row = lax.broadcasted_iota(jnp.int32, (span, 1), 0)
        d_embed = d_right[:, 128:]
        shares = shares + jnp.concatenate(
            [
                column_sum(d_content),
                column_sum(d_segment),
                column_sum(jnp.where(row >= lo, 0.0, d_embed)),
                column_sum(jnp.where(row >= lo, d_embed, 0.0)),
                jnp.zeros((4, 128), f32),
            ],
            axis=0,
        )
        delta, _ = offsets_of(base, run, span)
        exact = d_scores.astype(f32)
        for head in range(2):
            at = 2 * run * head
            both = exact[at : at + run] + exact[at + run : at + 2 * run]
            lines = [None] * 16
            lines[0] = column_sum(jnp.where(delta == 0, both, 0.0))
            for step, threshold in enumerate(thresholds):
                if threshold < span:
                    later = thresholds[step + 1] if step + 1 < len(thresholds) else span
                    above = (delta >= threshold) & (delta < later)
                    below = (delta <= -threshold) & (delta > -later)
                    lines[1 + step] = column_sum(jnp.where(above, both, 0.0))
                    lines[9 + step] = column_sum(jnp.where(below, both, 0.0))
            blank = jnp.zeros((1, span), f32)
            tallies[head] = tallies[head] + jnp.concatenate(
                [blank if entry is None else entry for entry in lines], axis=0
            )
    small[...] = shares
    for head in range(2):
        buckets[head] = tallies[head]


def columns_of(parts, at):
    pieces, start = [], 0
    for part in parts:
        low_end, high_end = max(at.start, start), min(at.stop, start + part.shape[1])
        if low_end < high_end:
            pieces.append(part[:, low_end - start : high_end - start])
        start += part.shape[1]
    return pieces[0] if len(pieces) == 1 else jnp.concatenate(pieces, axis=1)


def weights_kernel(
    pieces,
    scalars,
    rows,
    path,
    attended,
    d_branch,
    small_first,
    *refs,
):
    d_query, d_keys, d_values, small_second, tallies = (refs[i : 10 : 5] for i in range(5))
    refs = refs[10:]
    model = rows.shape[1]
    block = model // 2
    if pieces == 2:
        kept, sent, held, grad_sems = refs[:2], refs[2:4], *refs[4:]
    else:
        natural, small_out = refs[:4], refs[4]
    shard, place = scalars[0], scalars[1]
    small_rows = block // 8

    def hold(which, across, value):
        if pieces == 1:
            natural[which][:, across * block : (across + 1) * block] = value.astype(low)
            return
        spot = (slice(which * small_rows, (which + 1) * small_rows), slice(None))
        for half in range(2):
            for down in range(8):
                start = half * block + down * small_rows
                held[(half ^ shard, *block_index((down * 2 + across) ^ place, 4), *spot)] = value[
                    start : start + small_rows, :
                ].astype(low)

    for across in range(2):
        at = slice(across * block, (across + 1) * block)
        hold(0, across, mm_tn(rows[...], columns_of(d_query, at)))
        hold(1, across, mm_tn(path[...], columns_of(d_keys, at)))
        hold(2, across, mm_tn(path[...], columns_of(d_values, at)))
        hold(3, across, mm_tn(attended[...].astype(low), d_branch[:, at]))
    buckets = jnp.zeros((16, 16), f32)
    every_head = [part[head] for part in tallies for head in range(part.shape[0])]
    line = lax.broadcasted_iota(jnp.int32, every_head[0].shape, 0)
    for head, tally in enumerate(every_head):
        buckets = buckets + lax.dot_general(
            tally,
            (line == head).astype(f32),
            (((1,), (1,)), ((), ())),
            precision=lax.Precision.HIGHEST,
            preferred_element_type=f32,
        )
    if pieces == 1:
        small_out[:9, :] = small_first[:9, :]
        for across in range(2):
            small_out[9:13, across * block : (across + 1) * block] = columns_of(small_second, slice(across * block, (across + 1) * block))[:4]
        small_out[13:, :] = jnp.zeros((small_out.shape[0] - 13, model), f32)
        small_out[16:32, :16] = buckets
    else:
        last = model // 4
        for half in range(2):
            at = slice(half * block, (half + 1) * block)
            lines = [
                small_first[2 * half + i // 2 : 2 * half + i // 2 + 1, (i % 2) * block : (i % 2 + 1) * block]
                for i in range(4)
            ]
            lines += [small_first[i : i + 1, at] for i in range(4, 9)]
            late_lines = columns_of(small_second, at)
            lines += [late_lines[i : i + 1, :] for i in range(4)]
            for chunk in range(16):
                line = lines[chunk].astype(low) if chunk < 13 else jnp.zeros((1, block), low)
                spread_line = jnp.concatenate([line.astype(f32), jnp.zeros((15, block), f32)], axis=0)
                held[(half ^ shard, *block_index(chunk ^ place, 4), slice(last, last + 16), slice(None))] = spread_line.astype(low)
            wide = jnp.concatenate([buckets[8 * half : 8 * half + 8], jnp.zeros((8, 16), f32)], axis=0)
            wide = jnp.concatenate([wide, jnp.zeros((16, block - 16), f32)], axis=1)
            held[(half ^ shard, *block_index(13 ^ place, 4), slice(last, last + 16), slice(None))] = wide.astype(low)
    leaving = []
    if pieces == 2:
        for part, (start, height) in enumerate(later_cuts(model)):
            for which in range(2):
                at = 2 * part + which
                rows_at = (pl.ds(start, height), slice(None))
                for side in range(2):
                    source = held.at[(side, *half_at(routes_out[part][0], which, 4), *rows_at)]
                    target = (kept, sent)[side][which].at[(*(slice(None),) * 3, *rows_at)]
                    leaving.append(pltpu.make_async_copy(source, target, grad_sems.at[6 * side + at]))
        for copy in leaving:
            copy.start()
    for copy in leaving:
        copy.wait()


def tree_kernel(pieces, run, slots, scalars, found, d_mid_in, *refs):
    d_query, d_keys, d_values = (refs[i : 6 : 3] for i in range(3))
    refs = refs[6:]
    weights = [refs[i * pieces : (i + 1) * pieces] for i in range(3)]
    refs = refs[3 * pieces :]
    d_content, d_state = refs[:2]
    if pieces == 2:
        kept, full, tree, sems, grad_sems = refs[2:4], *refs[4:]
    else:
        tree_out, full, tree, sems, grad_sems = refs[2:]
    copies = [weight_copies(weights[i], full.at[i], sems, i * pieces, scalars[0]) for i in range(3)]
    for group in copies:
        for copy in group:
            copy.start()
    block = d_mid_in.shape[1] // 2
    tree[...] = jnp.zeros(tree.shape, tree.dtype)
    for group in copies[1:]:
        for copy in group:
            copy.wait()
    span = slots * run
    micro_count = d_mid_in.shape[0] // (2 * run)
    for micro in range(micro_count):
        at = slice(micro * span, (micro + 1) * span)
        shares = mm_nt(jnp.concatenate([entry[at, :] for entry in d_keys], axis=1), full[1])
        shares = shares + mm_nt(jnp.concatenate([entry[at, :] for entry in d_values], axis=1), full[2])
        for slot in range(slots):
            relative = found[micro * slots + slot]
            for half in range(2):
                piece = shares[slot * run : (slot + 1) * run, half * block : (half + 1) * block]
                start = (half * micro_count + micro) * run
                spot = (*block_index(relative, len(tree.shape) - 2), slice(start, start + run), slice(None))
                tree[spot] = (tree[spot].astype(f32) + piece).astype(low)
    if pieces == 2:
        last_copies = []
        for part, (start, height) in enumerate(tree_cuts(tree.shape[-2])):
            for which in range(2):
                source = tree.at[(*half_at(routes_out[part][0], which, 4), pl.ds(start, height), slice(None))]
                target = kept[which].at[(*(slice(None),) * 3, pl.ds(start, height), slice(None))]
                last_copies.append(pltpu.make_async_copy(source, target, grad_sems.at[2 * part + which]))
    else:
        last_copies = [pltpu.make_async_copy(tree, tree_out, grad_sems.at[0])]
    for copy in last_copies:
        copy.start()
    for copy in copies[0]:
        copy.wait()
    d_both = d_mid_in[...] + mm_nt(jnp.concatenate([entry[...] for entry in d_query], axis=1), full[0])
    for micro in range(micro_count):
        start = 2 * run * micro
        d_content[micro] = d_both[start : start + run]
        d_state[micro] = d_both[start + run : start + 2 * run]
    for copy in last_copies:
        copy.wait()


def collect_pieces(refs, held, sems):
    copies = []
    for part, route in enumerate(routes_out):
        for which in range(2):
            at = 2 * part + which
            target = held[part].at[(*half_index(route[0], which, 4), slice(None), slice(None))]
            copies.append(pltpu.make_async_copy(refs[at], target, sems.at[at]))
    for copy in copies:
        copy.start()
    for copy in copies:
        copy.wait()


def feed_spread_kernel(scalars, *refs):
    outer, inner, first, second, third, sems = refs[6:]
    collect_pieces(refs[:6], (first, second, third), sems)
    place = scalars[1]
    height, side = first.shape[-2:]
    total = 3 * height // 2
    for chunk in range(16):
        at = block_index(chunk ^ place, 4)
        down, across = (chunk // 2) * total, (chunk % 2) * side
        outer[down : down + height, across : across + side] = first[at].astype(f32)
        middle = second[at].astype(f32)
        outer[down + height : down + total, across : across + side] = middle[: total - height]
        down, across = (chunk // 8) * total, (chunk % 8) * side
        inner[down : down + total - height, across : across + side] = middle[total - height :]
        inner[down + total - height : down + total, across : across + side] = third[at].astype(f32)


def later_spread_kernel(scalars, *refs):
    weights, inner_bias, vectors, embed, table, sources, sems = refs[6:10], refs[10], refs[11:18], *refs[18:20], refs[20:23], refs[23]
    collect_pieces(refs[:6], sources, sems)
    place = scalars[1]
    side = sources[0].shape[-1]
    rows = weights[0].shape[0] // 8
    cuts = later_cuts(2 * side)
    for chunk in range(16):
        at = block_index(chunk ^ place, 4)
        down, across = (chunk // 2) * rows, (chunk % 2) * side
        for source, (start, height) in zip(sources, cuts):
            value = source[at].astype(f32)
            for which in range(4):
                begin, end = max(start, which * rows), min(start + height, (which + 1) * rows)
                if begin < end:
                    top = down + begin - which * rows
                    weights[which][top : top + end - begin, across : across + side] = value[begin - start : end - start]
            begin = 4 * rows
            if start <= begin < start + height:
                line = value[begin - start : begin - start + 1]
                if chunk < 4:
                    inner_bias[chunk * side : (chunk + 1) * side] = line.reshape(side)
                elif chunk < 11:
                    vectors[chunk - 4][...] = line.reshape(side)
                elif chunk < 13:
                    embed[chunk - 11 : chunk - 10, :] = line
                elif chunk == 13:
                    table[...] = value[begin - start : begin - start + table.shape[0], : table.shape[1]]


routes_out = ((0, 1, 2), (1, 2, 0), (2, 0, 1))


def send(inputs, bit):
    count = lax.axis_size("dp")
    return lax.ppermute(inputs, "dp", [(i, i ^ (1 << bit)) for i in range(count)])


def half_dims(bit):
    return tuple(1 if i == bit_total() - 1 - bit else 2 for i in range(bit_total()))


def bit_total():
    return lax.axis_size("dp").bit_length() - 1


def extra_bits():
    return tuple(range(3, bit_total()))


def grow(held, bit):
    return jnp.concatenate([held, send(held, bit)], axis=bit_total() - 1 - bit)


def part_of(held, bit, which):
    total = bit_total()
    if held.ndim == 3:
        held = held.reshape((2,) * total + held.shape[1:])
    return lax.slice_in_dim(held, which, which + 1, axis=total - 1 - bit)


def scatter_rest(held, route):
    for bit in route + extra_bits()[::-1]:
        held = part_of(held, bit, 0) + send(part_of(held, bit, 1), bit)
    return held.reshape(held.shape[-2:])


def scatter_blocks(blocks, route):
    held = part_of(blocks, route[0], 0) + send(part_of(blocks, route[0], 1), route[0])
    return scatter_rest(held, route[1:])


def axis_of(bit):
    return bit_total() - 1 - bit


def sum_rounds(lower, upper, keep):
    ready = yield list(upper)
    held = [own + send(entry, route[0]) for own, entry, route in zip(lower, ready, routes_out)]
    for step in (1, 2):
        ready = yield [part_of(entry, route[step], 1) for entry, route in zip(held, routes_out)]
        held = [
            part_of(entry, route[step], 0) + send(other, route[step])
            for entry, other, route in zip(held, ready, routes_out)
        ]
    for bit in extra_bits()[::-1]:
        (ready,) = yield [jnp.concatenate([part_of(entry, bit, 1) for entry in held], axis=-2)]
        arrived = send(ready, bit)
        start, later = 0, []
        for entry in held:
            height = entry.shape[-2]
            later.append(part_of(entry, bit, 0) + arrived[..., start : start + height, :])
            start += height
        held = later
    shares = held
    joined = jnp.concatenate([entry[..., :rows, :] for entry, rows in zip(held, keep)], axis=-2)
    for bit in extra_bits():
        (ready,) = yield [joined]
        joined = jnp.concatenate([joined, send(ready, bit)], axis=axis_of(bit))
    start, held = 0, []
    for rows in keep:
        held.append(joined[..., start : start + rows, :])
        start += rows
    for step in (2, 1):
        ready = yield held
        held = [
            jnp.concatenate([entry, send(entry, route[step])], axis=axis_of(route[step]))
            for entry, route in zip(ready, routes_out)
        ]
    ready = yield held
    arrived = [send(entry, route[0]) for entry, route in zip(ready, routes_out)]
    return [piece for pair in zip(ready, arrived) for piece in pair], shares


class Rounds:
    def __init__(self, steps):
        self.steps = steps
        self.pending = next(steps)
        self.result = None

    def advance(self, ready):
        try:
            self.pending = self.steps.send(ready)
        except StopIteration as stop:
            self.pending, self.result = [], stop.value


def advance_after(group, other):
    joined = lax.optimization_barrier(list(group.pending) + list(other.pending))
    group.advance(joined[: len(group.pending)])


def advance_free(pending, others):
    joined = lax.optimization_barrier(list(pending) + list(others))
    return joined[: len(pending)], joined[len(pending) :]


def spread_dims(held, route):
    return jnp.expand_dims(held, axis_of(route[0]))


def advance_together(groups, others=()):
    joined = [entry for group in groups for entry in group.pending] + list(others)
    joined = lax.optimization_barrier(joined)
    for group in groups:
        count = len(group.pending)
        ready, joined = joined[:count], joined[count:]
        group.advance(ready)
    return joined


def shards(
    content,
    query_state,
    token_seg,
    positions,
    parent,
    w_query,
    w_key,
    w_value,
    w_out,
    w_inner,
    w_outer,
    b_inner,
    b_outer,
    gain_attn,
    bias_attn,
    gain_ffn,
    bias_ffn,
    bias_content,
    bias_segment,
    seg_embed,
    rel_table,
    cot_content,
    cot_query,
):
    micro_count, run, model = content.shape
    shard_count, dp_count = lax.axis_size("shard"), lax.axis_size("dp")
    shard, place = lax.axis_index("shard"), lax.axis_index("dp")
    heads = rel_table.shape[1]
    bucket_total = rel_table.shape[0] * shard_count
    hidden = w_inner.shape[1]
    pairs = heads // 2
    per_run = dp_count // tree_runs
    slots = path_runs * per_run
    span = slots * run
    rows_total = 2 * run * micro_count
    pieces = 2 if shard_count == 2 and dp_count == tree_runs else 1
    part_width = model // shard_count

    def fetch(weight):
        if pieces == 2:
            return [weight, lax.ppermute(weight, "shard", [(0, 1), (1, 0)])]
        return [lax.all_gather(weight, "shard", axis=0, tiled=True)]

    own_seg = token_seg[:, 0]
    own_slot = positions[:, 0] // run
    facts = jnp.stack([own_seg, own_slot], axis=1).reshape(2 * micro_count, 1).astype(low)
    fact_rows = jnp.broadcast_to(jnp.pad(facts, ((0, 16 - 2 * micro_count), (0, 0))), (16, model))
    third = model // 3
    columns = ((0, third), (third, third), (2 * third, third))
    content_rows = micro_count * run
    block = jnp.concatenate([content.reshape(content_rows, model), fact_rows], axis=0)
    total_bits = bit_total()
    block, b_inner, b_outer, parent, seg_embed, w_query, w_key, cot_content = lax.optimization_barrier(
        (block, b_inner, b_outer, parent, seg_embed, w_query, w_key, cot_content)
    )
    held = block.reshape((1,) * total_bits + block.shape)
    for bit in extra_bits():
        held = grow(held, bit)
    query_weights, key_weights = fetch(w_query), fetch(w_key)
    inner_rows = b_inner.shape[0] // part_width
    flat = [b_inner, b_outer, gain_attn, bias_attn, gain_ffn, bias_ffn, bias_content, bias_segment]
    flat += [seg_embed.reshape(-1), rel_table.reshape(-1)]
    fill = 16 * part_width - sum(entry.size for entry in flat)
    small_parts = jnp.concatenate(flat + [jnp.zeros((fill,), low)]).reshape(16, part_width)
    parts = []
    for part, (start, width) in enumerate(columns):
        height = block.shape[0] if part == 0 else content_rows
        parts.append(held[..., :height, start : start + width])
    parts, (query_weights[-1], key_weights[-1], w_value, small_parts, parent, content, cot_query) = advance_free(
        parts, [query_weights[-1], key_weights[-1], w_value, small_parts, parent, content, cot_query]
    )
    value_weights = fetch(w_value)
    first_branch, first_leaf = trunk_runs * per_run, (trunk_runs + 1) * per_run
    mine = own_seg
    above = jnp.sum(jnp.where(jnp.arange(parent.shape[2]) == mine[:, None], parent[:, 0], 0), axis=1)
    trunk, leaf = mine == 0, mine > trunk_runs
    branch = jnp.where(leaf, above, mine)
    lo = jnp.where(trunk, 0, jnp.where(leaf, first_leaf, first_branch)) * run
    hi = jnp.where(trunk, first_branch, jnp.where(leaf, slots, first_leaf)) * run
    early = jnp.stack([shard, place]).astype(jnp.int32)
    facts_own = jnp.stack([own_slot * run, lo, hi, mine, branch], axis=1)
    scalars = jnp.concatenate([early, facts_own.reshape(-1)]).astype(jnp.int32)

    rows = jnp.concatenate([content, query_state], axis=1).reshape(rows_total, model)
    cotangent = jnp.concatenate([cot_content, cot_query], axis=1).reshape(rows_total, model)
    if pieces == 2:
        other = lax.ppermute(small_parts, "shard", [(0, 1), (1, 0)])
        gathered = jnp.where(shard == 0, jnp.stack([small_parts, other]), jnp.stack([other, small_parts]))
    else:
        gathered = lax.all_gather(small_parts, "shard", axis=0, tiled=False)
    gathered = gathered.astype(f32)
    parts = [grow(piece, route[2]) for piece, route in zip(parts, routes_out)]
    parts, (value_weights[-1], w_out, w_inner, gathered, scalars, rows, cotangent) = advance_free(
        parts, [value_weights[-1], w_out, w_inner, gathered, scalars, rows, cotangent]
    )
    inner_weights, out_weights = fetch(w_inner), fetch(w_out)
    inner_bias = gathered[:, :inner_rows].reshape(1, hidden)
    vectors = jnp.transpose(gathered, (1, 0, 2)).reshape(16, model)
    table = gathered[:, 13, : rel_table.size].reshape(bucket_total, heads)

    parts = [grow(piece, route[1]) for piece, route in zip(parts, routes_out)]
    parts, (out_weights[-1], inner_weights[-1], w_outer, vectors, inner_bias, table) = advance_free(
        parts, [out_weights[-1], inner_weights[-1], w_outer, vectors, inner_bias, table]
    )
    outer_weights = fetch(w_outer)
    tree_parts = [entry for piece, route in zip(parts, routes_out) for entry in (piece, send(piece, route[0]))]
    tree_parts, (outer_weights[-1],) = advance_free(tree_parts, [outer_weights[-1]])

    grown = pltpu.CompilerParams(vmem_limit_bytes=vmem_bytes)

    def shape(dims, kind):
        return jax.ShapeDtypeStruct(dims, kind)

    dma = pltpu.SemaphoreType.DMA
    query_low, query_segment = pl.pallas_call(
        functools.partial(query_kernel, pieces),
        out_shape=(shape((rows_total, model), low),) * 2,
        in_specs=[smem_space, vmem_space, vmem_space] + [any_space] * pieces,
        out_specs=(vmem_space,) * 2,
        scratch_shapes=[pltpu.VMEM((model, model), low), dma((pieces,))],
        compiler_params=grown,
        name="query_projection",
        cost_estimate=cost(1),
    )(early, rows, vectors, *query_weights)

    path, keys, values, found = pl.pallas_call(
        functools.partial(keys_kernel, pieces, columns, [route[0] for route in routes_out], run, slots),
        out_shape=(
            shape((micro_count, span, model), low),
            shape((micro_count * span, model), low),
            shape((micro_count * span, model), low),
            shape((micro_count * slots,), jnp.int32),
        ),
        in_specs=[smem_space] + [any_space] * (2 * len(columns) + 2 * pieces),
        out_specs=(vmem_space,) * 3 + (smem_space,),
        scratch_shapes=[
            pltpu.VMEM((model, model), low),
            pltpu.VMEM((model, model), low),
            pltpu.VMEM((2,) * total_bits + (content_rows + 16, model), low),
            dma((2 * pieces,)),
            dma((2 * len(columns),)),
        ],
        compiler_params=grown,
        name="path_keys",
        cost_estimate=cost(6),
    )(scalars, *tree_parts, *key_weights, *value_weights)
    path = path.reshape(micro_count * span, model)

    def blocks_at(first):
        return (
            pl.BlockSpec((rows_total, 128), lambda pair: (0, pair + first)),
            pl.BlockSpec((micro_count * span, 128), lambda pair: (0, pair + first)),
            pl.BlockSpec((micro_count, 4 * run, span), lambda pair: (pair + first, 0, 0)),
            pl.BlockSpec((16, 128), lambda pair: (0, pair + first)),
        )

    row_block, key_block, prob_block, vector_block = blocks_at(0)
    probs, attended = pl.pallas_call(
        functools.partial(attend_kernel, run, slots),
        grid=(pairs,),
        out_shape=(
            shape((pairs * micro_count, 4 * run, span), low),
            shape((rows_total, model), f32),
        ),
        in_specs=[smem_space, smem_space, row_block, row_block, key_block, key_block, vector_block],
        out_specs=(prob_block, row_block),
        compiler_params=grown,
        name="attend",
        cost_estimate=cost(11),
    )(scalars, table, query_low, query_segment, keys, values, vectors)

    half = model // 2
    if pieces == 2:
        grad_shapes = [shape((2,) * (total_bits - 1) + (half, half), low)] * 4
        grad_specs = [any_space] * len(grad_shapes)
        grad_scratch = [pltpu.VMEM((2,) * (1 + total_bits) + (half, half), low)]
    else:
        grad_shapes = [shape((hidden, model), low), shape((model, hidden), low)]
        grad_specs = [vmem_space] * 2
        grad_scratch = []
    results = pl.pallas_call(
        functools.partial(feed_kernel, pieces, run),
        out_shape=[
            shape((micro_count, run, model), low),
            shape((micro_count, run, model), low),
            shape((rows_total, model), f32),
            shape((rows_total, model), low),
            shape((rows_total, model), low),
            shape((16, model), f32),
        ]
        + grad_shapes,
        in_specs=[smem_space] + [vmem_space] * 5 + [any_space] * (3 * pieces),
        out_specs=[vmem_space] * 6 + grad_specs,
        scratch_shapes=[
            pltpu.VMEM((model, model), low),
            pltpu.VMEM((model, hidden), low),
            pltpu.VMEM((hidden, model), low),
            pltpu.VMEM((rows_total, hidden), low),
            pltpu.VMEM((rows_total, hidden), f32),
        ]
        + grad_scratch
        + [dma((3 * pieces,))]
        + ([dma((12,))] if pieces == 2 else []),
        compiler_params=grown,
        name="feed_forward",
        cost_estimate=cost(21),
    )(scalars, rows, attended, cotangent, vectors, inner_bias, *out_weights, *inner_weights, *outer_weights)
    out_content, out_query, d_mid_in, d_branch, d_att, small_first = results[:6]

    swap = [(0, 1), (1, 0)]
    if pieces == 2:
        feed_grads = results[6:]
        feed_other = [lax.ppermute(entry, "shard", swap) for entry in (feed_grads[3], feed_grads[2])]

    def attend_back(first, pair_count, gradient):
        rows_in, keys_in, probs_in, vector_in = blocks_at(first)
        return pl.pallas_call(
            functools.partial(back_kernel, run, slots),
            grid=(pair_count,),
            out_shape=(
                shape((rows_total, 128 * pair_count), low),
                shape((micro_count * span, 128 * pair_count), low),
                shape((micro_count * span, 128 * pair_count), low),
                shape((8, 128 * pair_count), f32),
                shape((2 * pair_count, 16, span), f32),
            ),
            in_specs=[smem_space, rows_in, rows_in, keys_in, keys_in, probs_in, rows_in, rows_in, vector_in],
            out_specs=(
                row_block,
                key_block,
                key_block,
                pl.BlockSpec((8, 128), lambda pair: (0, pair)),
                pl.BlockSpec((2, 16, span), lambda pair: (pair, 0, 0)),
            ),
            compiler_params=grown,
            name="attend_back",
            cost_estimate=cost(3),
        )(scalars, query_low, query_segment, keys, values, probs, gradient, attended, vectors)

    back_first = attend_back(0, pairs // 3, d_att)
    if pieces == 2:
        sizes = [height for _, height in feed_cuts(pieces, model)]
        upper = [
            spread_dims(feed_grads[1][..., start : start + height, :] + feed_other[0][..., start : start + height, :], route)
            for (start, height), route in zip(feed_cuts(pieces, model), routes_out)
        ]
        feed_lower = feed_other[1]
        *upper, feed_lower, d_att, _ = lax.optimization_barrier((*upper, feed_lower, d_att, back_first[0]))
        lower = [
            spread_dims(feed_grads[0][..., start : start + height, :] + feed_lower[..., start : start + height, :], route)
            for (start, height), route in zip(feed_cuts(pieces, model), routes_out)
        ]
        feed_rounds = Rounds(sum_rounds(lower, upper, sizes))
        feed_rounds.advance(feed_rounds.pending)
    back_second = attend_back(pairs // 3, pairs - pairs // 3, d_att)
    tree_height = 2 * micro_count * run
    if pieces == 2:
        whole = later_cuts(model)[-1][0] + later_cuts(model)[-1][1]
        heights = [entry[1] for entry in later_cuts(model)]
        cube = (2,) * (total_bits - 1)
        grad_shapes = [shape(cube + (whole, half), low)] * 4
        grad_specs = [any_space] * 4
        extra = [pltpu.VMEM((2,) * (1 + total_bits) + (whole, half), low), dma((12,))]
        tree_shapes = [shape(cube + (tree_height, half), low)] * 2
    else:
        grad_shapes = [shape((model, model), low)] * 4 + [shape((32, model), f32)]
        grad_specs = [vmem_space] * 5
        extra = []
        tree_shapes = [shape((2,) * total_bits + (tree_height, half), low)]
    later = pl.pallas_call(
        functools.partial(weights_kernel, pieces),
        out_shape=grad_shapes,
        in_specs=[smem_space] + [vmem_space] * 15,
        out_specs=grad_specs,
        scratch_shapes=extra,
        compiler_params=grown,
        name="weight_gradients",
        cost_estimate=cost(3),
    )(scalars, rows, path, attended, d_branch, small_first, *back_first, *back_second)
    if pieces == 2:
        feed_rounds.pending, later = advance_free(feed_rounds.pending, later)
        feed_rounds.pending, (d_mid_in,) = advance_free(feed_rounds.pending, [d_mid_in])
        feed_rounds.advance(feed_rounds.pending)
    d_content, grad_query, *tree_grads = pl.pallas_call(
        functools.partial(tree_kernel, pieces, run, slots),
        out_shape=[shape((micro_count, run, model), f32)] * 2 + tree_shapes,
        in_specs=[smem_space] * 2 + [vmem_space] * 7 + [any_space] * (3 * pieces),
        out_specs=[vmem_space] * 2 + [any_space] * len(tree_shapes),
        scratch_shapes=[
            pltpu.VMEM((3, model, model), low),
            pltpu.VMEM((2,) * total_bits + (tree_height, half), low),
            dma((3 * pieces,)),
            dma((6,)),
        ],
        compiler_params=grown,
        name="tree_gradients",
        cost_estimate=cost(3),
    )(scalars, found, d_mid_in, *back_first[:3], *back_second[:3], *query_weights, *key_weights, *value_weights)

    if pieces == 2:
        others = [lax.ppermute(entry, "shard", swap) for entry in (later[3], later[2])]
        feed_rounds.pending, others = advance_free(feed_rounds.pending, others)
        feed_rounds.pending, tree_grads = advance_free(feed_rounds.pending, tree_grads)
        feed_rounds.advance(feed_rounds.pending)

        def route_sum(which, part):
            start, height = later_cuts(model)[part]
            more, tall = tree_cuts(tree_height)[part]
            mine, other = later[which][..., start : start + height, :], others[1 - which][..., start : start + height, :]
            more_rows = tree_grads[which][..., more : more + tall, :]
            return spread_dims(jnp.concatenate([mine + other, more_rows], axis=-2), routes_out[part])

        lower = [route_sum(0, part) for part in range(3)]
        upper = [route_sum(1, part) for part in range(3)]
        later_rounds = Rounds(sum_rounds(lower, upper, heights))
        for _ in range(5):
            advance_after(later_rounds, feed_rounds)
            feed_rounds.advance(feed_rounds.pending)
        advance_together([later_rounds])
        feed_done = advance_together([later_rounds], feed_rounds.result[0])
        advance_together([later_rounds])

        def pieces_scratch(sizes):
            return [pltpu.VMEM((2,) * total_bits + (height, half), low) for height in sizes] + [dma((6,))]

        grad_w_outer, grad_w_inner = pl.pallas_call(
            feed_spread_kernel,
            out_shape=(shape(w_outer.shape, f32), shape(w_inner.shape, f32)),
            in_specs=[smem_space] + [any_space] * 6,
            out_specs=(vmem_space,) * 2,
            scratch_shapes=pieces_scratch([height for _, height in feed_cuts(pieces, model)]),
            compiler_params=grown,
            name="feed_spread",
            cost_estimate=cost(7),
        )(early, *feed_done)
        later_done, shares = later_rounds.result
        arrived = [share.reshape(share.shape[-2:])[rows:] for share, rows in zip(shares, heights)]
        tree_grad = jnp.concatenate(arrived, axis=0)
        spread_out = pl.pallas_call(
            later_spread_kernel,
            out_shape=[shape(w_query.shape, f32)] * 4
            + [shape(b_inner.shape, f32)]
            + [shape(b_outer.shape, f32)] * 7
            + [shape(seg_embed.shape, f32), shape(rel_table.shape, f32)],
            in_specs=[smem_space] + [any_space] * 6,
            out_specs=[vmem_space] * 14,
            scratch_shapes=pieces_scratch(heights),
            compiler_params=grown,
            name="later_spread",
            cost_estimate=cost(4),
        )(early, *later_done)
        grad_w_query, grad_w_key, grad_w_value, grad_w_out, grad_b_inner, *narrow, grad_rel_table = spread_out
    else:
        totals = []
        for entry in (*results[6:8], *later[:4]):
            share = lax.psum_scatter(entry, "shard", scatter_dimension=0, tiled=True)
            totals.append(lax.psum(share, "dp").astype(f32))
        grad_w_outer, grad_w_inner, grad_w_query, grad_w_key, grad_w_value, grad_w_out = totals
        tree_grad = scatter_blocks(tree_grads[0], routes_out[0])
        small = lax.psum(later[4], ("shard", "dp"))
        grad_b_inner = lax.dynamic_slice_in_dim(small[:4].reshape(-1), shard * b_inner.shape[0], b_inner.shape[0])
        narrow = lax.dynamic_slice_in_dim(small[4:13], shard * part_width, part_width, axis=1)
        narrow = [*narrow[:7], narrow[7:9]]
        grad_rel_table = lax.dynamic_slice_in_dim(
            small[16 : 16 + bucket_total, :heads], shard * rel_table.shape[0], rel_table.shape[0], axis=0
        )
    halves = tree_grad.astype(f32).reshape(2, micro_count, run, half)
    grad_content = d_content + jnp.concatenate([halves[0], halves[1]], axis=-1)
    return (
        out_content,
        out_query,
        grad_content,
        grad_query,
        grad_w_query,
        grad_w_key,
        grad_w_value,
        grad_w_out,
        grad_w_inner,
        grad_w_outer,
        grad_b_inner,
        narrow[0],
        narrow[1],
        narrow[2],
        narrow[3],
        narrow[4],
        narrow[5],
        narrow[6],
        narrow[7],
        grad_rel_table,
    )


def solution(mesh):
    rows = P(None, ("shard", "dp"), None)
    tokens = P(None, ("shard", "dp"))
    matrix = P("shard", None)
    vector = P("shard")
    return jax.shard_map(
        shards,
        mesh=mesh,
        in_specs=(rows, rows, tokens, tokens, P(None, "shard", None))
        + (matrix,) * 6
        + (vector,) * 8
        + (P(None, "shard"), matrix, rows, rows),
        out_specs=(rows,) * 4 + (matrix,) * 6 + (vector,) * 8 + (P(None, "shard"), matrix),
        check_vma=False,
    )
```

```python
import functools

import jax
import jax.numpy as jnp
from jax import lax
from jax.experimental import pallas as pl
from jax.experimental.pallas import tpu as pltpu
from jax.sharding import PartitionSpec as P

thresholds = (1, 2, 4, 8, 32, 128, 512)
norm_eps = 1e-05
masked_score = -1e30
path_runs = 6
trunk_runs = 4
tree_runs = 16
vmem_bytes = 60 * 1024 * 1024
low = jnp.bfloat16
f32 = jnp.float32
def cost(microseconds):
    return pl.CostEstimate(flops=int(microseconds * 1e9), bytes_accessed=0, transcendentals=0)


any_space = pl.BlockSpec(memory_space=pl.ANY)
smem_space = pl.BlockSpec(memory_space=pltpu.SMEM)
vmem_space = pl.BlockSpec(memory_space=pltpu.VMEM)


def mm(left, right):
    return lax.dot_general(left, right, (((1,), (0,)), ((), ())), preferred_element_type=f32)


def mm_nt(left, right):
    return lax.dot_general(left, right, (((1,), (1,)), ((), ())), preferred_element_type=f32)


def mm_tn(left, right):
    return lax.dot_general(left, right, (((0,), (0,)), ((), ())), preferred_element_type=f32)


def weight_copies(pieces, target, sems, first, shard):
    if len(pieces) == 1:
        return [pltpu.make_async_copy(pieces[0], target, sems.at[first])]
    half = pieces[0].shape[0]
    own = pl.multiple_of(shard * half, 16)
    other = pl.multiple_of((1 - shard) * half, 16)
    return [
        pltpu.make_async_copy(pieces[0], target.at[pl.ds(own, half)], sems.at[first]),
        pltpu.make_async_copy(pieces[1], target.at[pl.ds(other, half)], sems.at[first + 1]),
    ]


def scalar_at(scalars, micro, entry):
    return scalars[2 + 5 * micro + entry]


def block_index(at, total):
    return tuple((at >> (total - 1 - i)) & 1 for i in range(total))


def half_index(bit, which, total):
    everything = [slice(None)] * total
    everything[total - 1 - bit] = pl.ds(which, 1)
    return tuple(everything)


def half_at(bit, which, total):
    everything = [slice(None)] * total
    everything[total - 1 - bit] = which
    return tuple(everything)


def query_kernel(pieces, scalars, rows, vectors, *refs):
    weights = refs[:pieces]
    query_low, query_segment, full, sems = refs[pieces:]
    copies = weight_copies(weights, full, sems, 0, scalars[0])
    for copy in copies:
        copy.start()
    for copy in copies:
        copy.wait()
    raw = mm(rows[...], full[...])
    query_low[...] = (raw + vectors[9:10, :]).astype(low)
    query_segment[...] = (raw + vectors[10:11, :]).astype(low)


def keys_kernel(pieces, columns, lasts, run, slots, scalars, *refs):
    parts = refs[: 2 * len(columns)]
    refs = refs[2 * len(columns) :]
    key_weights, value_weights = refs[:pieces], refs[pieces : 2 * pieces]
    path, keys, values, found, full_key, full_value, tree, sems, tree_sems = refs[2 * pieces :]
    shard = scalars[0]
    total = len(tree.shape) - 2
    moves = []
    for part, (start, width) in enumerate(columns):
        for which in range(2):
            source = parts[2 * part + which]
            target = tree.at[
                (*half_index(lasts[part], which, total), pl.ds(0, source.shape[-2]), pl.ds(start, width))
            ]
            moves.append(pltpu.make_async_copy(source, target, tree_sems.at[2 * part + which]))
    copies = weight_copies(key_weights, full_key, sems, 0, shard)
    copies = copies + weight_copies(value_weights, full_value, sems, pieces, shard)
    for copy in moves + copies:
        copy.start()
    for copy in moves:
        copy.wait()
    micro_count = path.shape[0]
    content_rows = micro_count * run
    facts = [
        tree[(*block_index(block, total), slice(content_rows, content_rows + 16), slice(0, 128))].astype(f32)
        for block in range(1 << total)
    ]
    numbers = lax.broadcasted_iota(jnp.int32, (1 << total, 128), 0)
    for micro in range(micro_count):
        segs = jnp.concatenate([entry[2 * micro : 2 * micro + 1] for entry in facts], axis=0).astype(jnp.int32)
        places = jnp.concatenate([entry[2 * micro + 1 : 2 * micro + 2] for entry in facts], axis=0).astype(jnp.int32)
        for slot in range(slots):
            if slot < slots // path_runs * trunk_runs:
                wanted = 0
            else:
                wanted = scalar_at(scalars, micro, 4 if slot < slots // path_runs * (trunk_runs + 1) else 3)
            shown = (segs == wanted) & (places == slot)
            relative = jnp.max(jnp.where(shown, numbers, 0))
            found[micro * slots + slot] = relative
            at = block_index(relative, total)
            path[micro, slot * run : (slot + 1) * run, :] = tree[(*at, slice(micro * run, (micro + 1) * run), slice(None))]
    for copy in copies:
        copy.wait()
    for micro in range(micro_count):
        rows = path[micro]
        span = slots * run
        keys[micro * span : (micro + 1) * span, :] = mm(rows, full_key[...]).astype(low)
        values[micro * span : (micro + 1) * span, :] = mm(rows, full_value[...]).astype(low)


def head_masks():
    lane = lax.broadcasted_iota(jnp.int32, (1, 128), 1)
    first = lane < 64
    return first, first.astype(f32).astype(low), (1.0 - first.astype(f32)).astype(low)


def stack_query(query_low, query_segment, mask_a, mask_b):
    both = jnp.concatenate([query_low, query_segment], axis=1)
    wide_a = jnp.concatenate([mask_a, mask_a], axis=1)
    wide_b = jnp.concatenate([mask_b, mask_b], axis=1)
    return jnp.concatenate([both * wide_a, both * wide_b], axis=0)


def stack_keys(keys, vectors, lo):
    row = lax.broadcasted_iota(jnp.int32, (keys.shape[0], 1), 0)
    segment = jnp.where(row >= lo, vectors[12:13, :], vectors[11:12, :]).astype(low)
    return jnp.concatenate([keys, segment], axis=1)


def offsets_of(base, run, span):
    row = lax.broadcasted_iota(jnp.int32, (run, span), 0)
    column = lax.broadcasted_iota(jnp.int32, (run, span), 1)
    return base + row - column, column


def attend_kernel(run, slots, scalars, table, query_low, query_segment, keys, values, vectors, probs, attended):
    pair = pl.program_id(0)
    span = slots * run
    first, mask_a, mask_b = head_masks()
    for micro in range(probs.shape[0]):
        base, lo, hi = (scalar_at(scalars, micro, entry) for entry in range(3))
        rows = slice(micro * 2 * run, (micro + 1) * 2 * run)
        columns = slice(micro * span, (micro + 1) * span)
        left = stack_query(query_low[rows, :], query_segment[rows, :], mask_a, mask_b)
        right = stack_keys(keys[columns, :], vectors[...], lo)
        raw = mm_nt(left, right)
        delta, column = offsets_of(base, run, span)
        visible = column < hi
        biases = []
        for head in range(2):
            at = 2 * pair + head
            bias = jnp.full((run, span), table[0, at], f32)
            for step, threshold in enumerate(thresholds):
                if threshold < span:
                    bias = jnp.where(delta >= threshold, table[1 + step, at], bias)
                    bias = jnp.where(delta <= -threshold, table[9 + step, at], bias)
            bias = jnp.where(visible, bias, masked_score)
            biases.append(bias)
            biases.append(jnp.where(delta == 0, masked_score, bias))
        scores = raw * 0.125 + jnp.concatenate(biases, axis=0)
        peak = jnp.max(scores, axis=-1, keepdims=True)
        mass = jnp.exp(scores - peak)
        total = jnp.sum(mass, axis=-1, keepdims=True)
        probs_low = (mass * (1.0 / total)).astype(low)
        probs[micro] = probs_low
        heads = mm(probs_low, values[columns, :])
        attended[rows, :] = jnp.where(first, heads[: 2 * run], heads[2 * run :])


def norm_forward(inputs):
    centred = inputs - jnp.mean(inputs, axis=-1, keepdims=True)
    scale = lax.rsqrt(jnp.mean(centred * centred, axis=-1, keepdims=True) + norm_eps)
    return centred * scale, scale


def norm_backward(gradient, gain, normal, scale):
    d_normal = gradient * gain
    mean_first = jnp.mean(d_normal, axis=-1, keepdims=True)
    mean_second = jnp.mean(d_normal * normal, axis=-1, keepdims=True)
    return scale * (d_normal - mean_first - normal * mean_second)


def column_sum(inputs):
    return jnp.sum(inputs, axis=0, keepdims=True)


def feed_cuts(pieces, model):
    if pieces == 1:
        return ()
    step = model // 6
    return ((0, step), (step, step), (2 * step, step))


def later_cuts(model):
    whole = model // 4 + 16
    step = whole // 40 * 16
    return ((0, step), (step, step), (2 * step, whole - 2 * step))


def tree_cuts(height):
    step = height // 48 * 16 + 16
    return ((0, step), (step, step), (2 * step, height - 2 * step))


def feed_kernel(pieces, run, scalars, rows, attended, cotangent, vectors, inner_bias, *refs):
    out_weights, inner_weights, outer_weights = (refs[i * pieces : (i + 1) * pieces] for i in range(3))
    refs = refs[3 * pieces :]
    out_content, out_query, d_mid_in, d_branch_out, d_att, small = refs[:6]
    routes = feed_cuts(pieces, rows.shape[1])
    outputs = 4 if pieces == 2 else 2
    grads = refs[6 : 6 + outputs]
    full_out, full_inner, full_outer, act_low, slope = refs[6 + outputs : 11 + outputs]
    if pieces == 2:
        held, sems, grad_sems = refs[11 + outputs :]
    else:
        (sems,) = refs[11 + outputs :]
    shard, place = scalars[0], scalars[1]
    copies = [
        weight_copies(out_weights, full_out, sems, 0, shard),
        weight_copies(inner_weights, full_inner, sems, pieces, shard),
        weight_copies(outer_weights, full_outer, sems, 2 * pieces, shard),
    ]
    for group in copies:
        for copy in group:
            copy.start()
    model = rows.shape[1]
    hidden = full_inner.shape[1]
    att_low = attended[...].astype(low)
    for copy in copies[0]:
        copy.wait()
    normal_first, scale_first = norm_forward(mm(att_low, full_out[...]) + rows[...].astype(f32))
    middle = normal_first * vectors[5:6, :] + vectors[6:7, :]
    middle_low = middle.astype(low)
    for copy in copies[1]:
        copy.wait()
    wide = model
    total = None
    for start in range(0, hidden, wide):
        at = slice(start, start + wide)
        pre = mm(middle_low, full_inner[:, at]) + inner_bias[:, at]
        squared = pre * pre
        bent = jnp.tanh(0.7978845608028654 * pre * (1.0 + 0.044715 * squared))
        half = 0.5 * (1.0 + bent)
        act = (pre * half).astype(low)
        act_low[:, at] = act
        slope[:, at] = half + (0.5 * 0.7978845608028654) * pre * (1.0 - bent * bent) * (
            1.0 + (3 * 0.044715) * squared
        )
        if start == 0:
            for copy in copies[2]:
                copy.wait()
        share = mm(act, full_outer[at, :])
        total = share if total is None else total + share
    normal_second, scale_second = norm_forward(total + vectors[4:5, :] + middle)
    final = (normal_second * vectors[7:8, :] + vectors[8:9, :]).astype(low)
    for micro in range(out_content.shape[0]):
        start = 2 * run * micro
        out_content[micro] = final[start : start + run]
        out_query[micro] = final[start + run : start + 2 * run]
    d_final = cotangent[...].astype(f32)
    small[7:8, :] = column_sum(d_final * normal_second)
    small[8:9, :] = column_sum(d_final)
    d_final_in = norm_backward(d_final, vectors[7:8, :], normal_second, scale_second)
    d_outer = d_final_in.astype(low)
    small[4:5, :] = column_sum(d_outer.astype(f32))
    block = model // 2

    def hold_outer(start, value):
        if pieces == 1:
            grads[0][start : start + block, :] = value.astype(low)
            return
        half = hidden // 2
        target = (start // half) ^ shard
        for down in range(2):
            for across in range(2):
                chunk = ((start % half) // (block // 2) + down) * 2 + across
                held[(target, *block_index(chunk ^ place, 4), slice(0, block // 2), slice(None))] = value[
                    down * (block // 2) : (down + 1) * (block // 2), across * block : (across + 1) * block
                ].astype(low)

    def hold_inner(start, value):
        if pieces == 1:
            grads[1][:, start : start + block] = value.astype(low)
            return
        for quarter in range(4):
            chunk = (quarter % 2) * 8 + start // block
            held[
                ((quarter // 2) ^ shard, *block_index(chunk ^ place, 4), slice(block // 2, block), slice(None))
            ] = value[
                quarter * (block // 2) : (quarter + 1) * (block // 2), :
            ].astype(low)

    for start in range(0, hidden, block):
        hold_outer(start, mm_tn(act_low[:, start : start + block], d_outer))
    sent = []
    for part, (start, height) in enumerate(routes):
        for side in range(2):
            for which in range(2):
                rows_at = (pl.ds(start, height), slice(None))
                source = held.at[(side, *half_at(routes_out[part][0], which, 4), *rows_at)]
                target = grads[2 * side + which].at[(*(slice(None),) * 3, *rows_at)]
                sent.append(pltpu.make_async_copy(source, target, grad_sems.at[4 * part + 2 * side + which]))
    for copy in sent[:4]:
        copy.start()
    d_middle = d_final_in
    for start in range(0, hidden, block):
        at = slice(start, start + block)
        d_inner = (mm_nt(d_outer, full_outer[at, :]) * slope[:, at]).astype(low)
        summed = column_sum(d_inner.astype(f32))
        row, lane = start // model, start % model
        small[row : row + 1, lane : lane + block] = summed
        hold_inner(start, mm_tn(middle_low, d_inner))
        d_middle = d_middle + mm_nt(d_inner, full_inner[:, at])
    for copy in sent[4:]:
        copy.start()
    small[5:6, :] = column_sum(d_middle * normal_first)
    small[6:7, :] = column_sum(d_middle)
    small[9:16, :] = jnp.zeros((7, model), f32)
    d_mid = norm_backward(d_middle, vectors[5:6, :], normal_first, scale_first)
    d_mid_in[...] = d_mid
    d_branch = d_mid.astype(low)
    d_branch_out[...] = d_branch
    d_att[...] = mm_nt(d_branch, full_out[...]).astype(low)
    for copy in sent:
        copy.wait()


def back_kernel(
    run,
    slots,
    scalars,
    query_low,
    query_segment,
    keys,
    values,
    probs,
    d_att,
    attended,
    vectors,
    d_query,
    d_keys,
    d_values,
    small,
    buckets,
):
    span = slots * run
    first, mask_a, mask_b = head_masks()
    shares = jnp.zeros((8, 128), f32)
    tallies = [jnp.zeros((16, span), f32)] * 2
    for micro in range(probs.shape[0]):
        base, lo = scalar_at(scalars, micro, 0), scalar_at(scalars, micro, 1)
        rows = slice(micro * 2 * run, (micro + 1) * 2 * run)
        columns = slice(micro * span, (micro + 1) * span)
        gradient = d_att[rows, :]
        stacked = jnp.concatenate([gradient * mask_a, gradient * mask_b], axis=0)
        product = gradient.astype(f32) * attended[rows, :]
        delta_a = jnp.sum(jnp.where(first, product, 0.0), axis=-1, keepdims=True)
        delta_b = jnp.sum(jnp.where(first, 0.0, product), axis=-1, keepdims=True)
        delta_row = jnp.concatenate([delta_a, delta_b], axis=0)
        probs_low = probs[micro]
        d_probs = mm_nt(stacked, values[columns, :])
        d_scores = (probs_low.astype(f32) * (d_probs - delta_row)).astype(low)
        left = stack_query(query_low[rows, :], query_segment[rows, :], mask_a, mask_b)
        right = stack_keys(keys[columns, :], vectors[...], lo)
        d_left = mm(d_scores, right) * 0.125
        mine = jnp.concatenate([first, first], axis=1)
        d_left = jnp.where(mine, d_left[: 2 * run], d_left[2 * run :])
        d_content, d_segment = d_left[:, :128], d_left[:, 128:]
        d_query[rows, :] = (d_content + d_segment).astype(low)
        d_right = mm_tn(d_scores, left) * 0.125
        d_keys[columns, :] = d_right[:, :128].astype(low)
        d_values[columns, :] = mm_tn(probs_low, stacked).astype(low)
        row = lax.broadcasted_iota(jnp.int32, (span, 1), 0)
        d_embed = d_right[:, 128:]
        shares = shares + jnp.concatenate(
            [
                column_sum(d_content),
                column_sum(d_segment),
                column_sum(jnp.where(row >= lo, 0.0, d_embed)),
                column_sum(jnp.where(row >= lo, d_embed, 0.0)),
                jnp.zeros((4, 128), f32),
            ],
            axis=0,
        )
        delta, _ = offsets_of(base, run, span)
        exact = d_scores.astype(f32)
        for head in range(2):
            at = 2 * run * head
            both = exact[at : at + run] + exact[at + run : at + 2 * run]
            lines = [None] * 16
            lines[0] = column_sum(jnp.where(delta == 0, both, 0.0))
            for step, threshold in enumerate(thresholds):
                if threshold < span:
                    later = thresholds[step + 1] if step + 1 < len(thresholds) else span
                    above = (delta >= threshold) & (delta < later)
                    below = (delta <= -threshold) & (delta > -later)
                    lines[1 + step] = column_sum(jnp.where(above, both, 0.0))
                    lines[9 + step] = column_sum(jnp.where(below, both, 0.0))
            blank = jnp.zeros((1, span), f32)
            tallies[head] = tallies[head] + jnp.concatenate(
                [blank if entry is None else entry for entry in lines], axis=0
            )
    small[...] = shares
    for head in range(2):
        buckets[head] = tallies[head]


def columns_of(parts, at):
    pieces, start = [], 0
    for part in parts:
        low_end, high_end = max(at.start, start), min(at.stop, start + part.shape[1])
        if low_end < high_end:
            pieces.append(part[:, low_end - start : high_end - start])
        start += part.shape[1]
    return pieces[0] if len(pieces) == 1 else jnp.concatenate(pieces, axis=1)


def weights_kernel(
    pieces,
    scalars,
    rows,
    path,
    attended,
    d_branch,
    small_first,
    *refs,
):
    d_query, d_keys, d_values, small_second, tallies = (refs[i : 10 : 5] for i in range(5))
    refs = refs[10:]
    model = rows.shape[1]
    block = model // 2
    if pieces == 2:
        kept, sent, held, grad_sems = refs[:2], refs[2:4], *refs[4:]
    else:
        natural, small_out = refs[:4], refs[4]
    shard, place = scalars[0], scalars[1]
    small_rows = block // 8

    def hold(which, across, value):
        if pieces == 1:
            natural[which][:, across * block : (across + 1) * block] = value.astype(low)
            return
        spot = (slice(which * small_rows, (which + 1) * small_rows), slice(None))
        for half in range(2):
            for down in range(8):
                start = half * block + down * small_rows
                held[(half ^ shard, *block_index((down * 2 + across) ^ place, 4), *spot)] = value[
                    start : start + small_rows, :
                ].astype(low)

    for across in range(2):
        at = slice(across * block, (across + 1) * block)
        hold(0, across, mm_tn(rows[...], columns_of(d_query, at)))
        hold(1, across, mm_tn(path[...], columns_of(d_keys, at)))
        hold(2, across, mm_tn(path[...], columns_of(d_values, at)))
        hold(3, across, mm_tn(attended[...].astype(low), d_branch[:, at]))
    buckets = jnp.zeros((16, 16), f32)
    every_head = [part[head] for part in tallies for head in range(part.shape[0])]
    line = lax.broadcasted_iota(jnp.int32, every_head[0].shape, 0)
    for head, tally in enumerate(every_head):
        buckets = buckets + lax.dot_general(
            tally,
            (line == head).astype(f32),
            (((1,), (1,)), ((), ())),
            precision=lax.Precision.HIGHEST,
            preferred_element_type=f32,
        )
    if pieces == 1:
        small_out[:9, :] = small_first[:9, :]
        for across in range(2):
            small_out[9:13, across * block : (across + 1) * block] = columns_of(small_second, slice(across * block, (across + 1) * block))[:4]
        small_out[13:, :] = jnp.zeros((small_out.shape[0] - 13, model), f32)
        small_out[16:32, :16] = buckets
    else:
        last = model // 4
        for half in range(2):
            at = slice(half * block, (half + 1) * block)
            lines = [
                small_first[2 * half + i // 2 : 2 * half + i // 2 + 1, (i % 2) * block : (i % 2 + 1) * block]
                for i in range(4)
            ]
            lines += [small_first[i : i + 1, at] for i in range(4, 9)]
            late_lines = columns_of(small_second, at)
            lines += [late_lines[i : i + 1, :] for i in range(4)]
            for chunk in range(16):
                line = lines[chunk].astype(low) if chunk < 13 else jnp.zeros((1, block), low)
                spread_line = jnp.concatenate([line.astype(f32), jnp.zeros((15, block), f32)], axis=0)
                held[(half ^ shard, *block_index(chunk ^ place, 4), slice(last, last + 16), slice(None))] = spread_line.astype(low)
            wide = jnp.concatenate([buckets[8 * half : 8 * half + 8], jnp.zeros((8, 16), f32)], axis=0)
            wide = jnp.concatenate([wide, jnp.zeros((16, block - 16), f32)], axis=1)
            held[(half ^ shard, *block_index(13 ^ place, 4), slice(last, last + 16), slice(None))] = wide.astype(low)
    leaving = []
    if pieces == 2:
        for part, (start, height) in enumerate(later_cuts(model)):
            for which in range(2):
                at = 2 * part + which
                rows_at = (pl.ds(start, height), slice(None))
                for side in range(2):
                    source = held.at[(side, *half_at(routes_out[part][0], which, 4), *rows_at)]
                    target = (kept, sent)[side][which].at[(*(slice(None),) * 3, *rows_at)]
                    leaving.append(pltpu.make_async_copy(source, target, grad_sems.at[6 * side + at]))
        for copy in leaving:
            copy.start()
    for copy in leaving:
        copy.wait()


def tree_kernel(pieces, run, slots, scalars, found, d_mid_in, *refs):
    d_query, d_keys, d_values = (refs[i : 6 : 3] for i in range(3))
    refs = refs[6:]
    weights = [refs[i * pieces : (i + 1) * pieces] for i in range(3)]
    refs = refs[3 * pieces :]
    d_content, d_state = refs[:2]
    if pieces == 2:
        kept, full, tree, sems, grad_sems = refs[2:4], *refs[4:]
    else:
        tree_out, full, tree, sems, grad_sems = refs[2:]
    copies = [weight_copies(weights[i], full.at[i], sems, i * pieces, scalars[0]) for i in range(3)]
    for group in copies:
        for copy in group:
            copy.start()
    block = d_mid_in.shape[1] // 2
    tree[...] = jnp.zeros(tree.shape, tree.dtype)
    for group in copies[1:]:
        for copy in group:
            copy.wait()
    span = slots * run
    micro_count = d_mid_in.shape[0] // (2 * run)
    for micro in range(micro_count):
        at = slice(micro * span, (micro + 1) * span)
        shares = mm_nt(jnp.concatenate([entry[at, :] for entry in d_keys], axis=1), full[1])
        shares = shares + mm_nt(jnp.concatenate([entry[at, :] for entry in d_values], axis=1), full[2])
        for slot in range(slots):
            relative = found[micro * slots + slot]
            for half in range(2):
                piece = shares[slot * run : (slot + 1) * run, half * block : (half + 1) * block]
                start = (half * micro_count + micro) * run
                spot = (*block_index(relative, len(tree.shape) - 2), slice(start, start + run), slice(None))
                tree[spot] = (tree[spot].astype(f32) + piece).astype(low)
    if pieces == 2:
        last_copies = []
        for part, (start, height) in enumerate(tree_cuts(tree.shape[-2])):
            for which in range(2):
                source = tree.at[(*half_at(routes_out[part][0], which, 4), pl.ds(start, height), slice(None))]
                target = kept[which].at[(*(slice(None),) * 3, pl.ds(start, height), slice(None))]
                last_copies.append(pltpu.make_async_copy(source, target, grad_sems.at[2 * part + which]))
    else:
        last_copies = [pltpu.make_async_copy(tree, tree_out, grad_sems.at[0])]
    for copy in last_copies:
        copy.start()
    for copy in copies[0]:
        copy.wait()
    d_both = d_mid_in[...] + mm_nt(jnp.concatenate([entry[...] for entry in d_query], axis=1), full[0])
    for micro in range(micro_count):
        start = 2 * run * micro
        d_content[micro] = d_both[start : start + run]
        d_state[micro] = d_both[start + run : start + 2 * run]
    for copy in last_copies:
        copy.wait()


def collect_pieces(refs, held, sems):
    copies = []
    for part, route in enumerate(routes_out):
        for which in range(2):
            at = 2 * part + which
            target = held[part].at[(*half_index(route[0], which, 4), slice(None), slice(None))]
            copies.append(pltpu.make_async_copy(refs[at], target, sems.at[at]))
    for copy in copies:
        copy.start()
    for copy in copies:
        copy.wait()


def feed_spread_kernel(scalars, *refs):
    outer, inner, first, second, third, sems = refs[6:]
    collect_pieces(refs[:6], (first, second, third), sems)
    place = scalars[1]
    height, side = first.shape[-2:]
    total = 3 * height // 2
    for chunk in range(16):
        at = block_index(chunk ^ place, 4)
        down, across = (chunk // 2) * total, (chunk % 2) * side
        outer[down : down + height, across : across + side] = first[at].astype(f32)
        middle = second[at].astype(f32)
        outer[down + height : down + total, across : across + side] = middle[: total - height]
        down, across = (chunk // 8) * total, (chunk % 8) * side
        inner[down : down + total - height, across : across + side] = middle[total - height :]
        inner[down + total - height : down + total, across : across + side] = third[at].astype(f32)


def later_spread_kernel(scalars, *refs):
    weights, inner_bias, vectors, embed, table, sources, sems = refs[6:10], refs[10], refs[11:18], *refs[18:20], refs[20:23], refs[23]
    collect_pieces(refs[:6], sources, sems)
    place = scalars[1]
    side = sources[0].shape[-1]
    rows = weights[0].shape[0] // 8
    cuts = later_cuts(2 * side)
    for chunk in range(16):
        at = block_index(chunk ^ place, 4)
        down, across = (chunk // 2) * rows, (chunk % 2) * side
        for source, (start, height) in zip(sources, cuts):
            value = source[at].astype(f32)
            for which in range(4):
                begin, end = max(start, which * rows), min(start + height, (which + 1) * rows)
                if begin < end:
                    top = down + begin - which * rows
                    weights[which][top : top + end - begin, across : across + side] = value[begin - start : end - start]
            begin = 4 * rows
            if start <= begin < start + height:
                line = value[begin - start : begin - start + 1]
                if chunk < 4:
                    inner_bias[chunk * side : (chunk + 1) * side] = line.reshape(side)
                elif chunk < 11:
                    vectors[chunk - 4][...] = line.reshape(side)
                elif chunk < 13:
                    embed[chunk - 11 : chunk - 10, :] = line
                elif chunk == 13:
                    table[...] = value[begin - start : begin - start + table.shape[0], : table.shape[1]]


routes_out = ((0, 1, 2), (1, 2, 0), (2, 0, 1))


def send(inputs, bit):
    count = lax.axis_size("dp")
    return lax.ppermute(inputs, "dp", [(i, i ^ (1 << bit)) for i in range(count)])


def half_dims(bit):
    return tuple(1 if i == bit_total() - 1 - bit else 2 for i in range(bit_total()))


def bit_total():
    return lax.axis_size("dp").bit_length() - 1


def extra_bits():
    return tuple(range(3, bit_total()))


def grow(held, bit):
    return jnp.concatenate([held, send(held, bit)], axis=bit_total() - 1 - bit)


def part_of(held, bit, which):
    total = bit_total()
    if held.ndim == 3:
        held = held.reshape((2,) * total + held.shape[1:])
    return lax.slice_in_dim(held, which, which + 1, axis=total - 1 - bit)


def scatter_rest(held, route):
    for bit in route + extra_bits()[::-1]:
        held = part_of(held, bit, 0) + send(part_of(held, bit, 1), bit)
    return held.reshape(held.shape[-2:])


def scatter_blocks(blocks, route):
    held = part_of(blocks, route[0], 0) + send(part_of(blocks, route[0], 1), route[0])
    return scatter_rest(held, route[1:])


def axis_of(bit):
    return bit_total() - 1 - bit


def sum_rounds(lower, upper, keep):
    ready = yield list(upper)
    held = [own + send(entry, route[0]) for own, entry, route in zip(lower, ready, routes_out)]
    for step in (1, 2):
        ready = yield [part_of(entry, route[step], 1) for entry, route in zip(held, routes_out)]
        held = [
            part_of(entry, route[step], 0) + send(other, route[step])
            for entry, other, route in zip(held, ready, routes_out)
        ]
    (far,) = extra_bits()
    both = [[part_of(entry, far, which) for entry in held] for which in range(2)]
    leaving = [entry[..., :rows, :] for which in range(2) for entry, rows in zip(both[which], keep)]
    leaving += [entry[..., rows:, :] for entry, rows in zip(both[1], keep) if rows < entry.shape[-2]]
    (ready,) = yield [jnp.concatenate(leaving, axis=-2)]
    arrived, start, received = send(ready, far), 0, []
    for entry in leaving:
        received.append(arrived[..., start : start + entry.shape[-2], :])
        start += entry.shape[-2]
    count = len(keep)
    shares = [
        entry[..., rows:, :] + other for entry, rows, other in zip(both[0], keep, received[2 * count :])
    ]
    held = [
        jnp.concatenate(
            [both[0][i][..., :rows, :] + received[count + i], both[1][i][..., :rows, :] + received[i]],
            axis=axis_of(far),
        )
        for i, rows in enumerate(keep)
    ]
    for step in (2, 1):
        ready = yield held
        held = [
            jnp.concatenate([entry, send(entry, route[step])], axis=axis_of(route[step]))
            for entry, route in zip(ready, routes_out)
        ]
    ready = yield held
    arrived = [send(entry, route[0]) for entry, route in zip(ready, routes_out)]
    return [piece for pair in zip(ready, arrived) for piece in pair], shares


class Rounds:
    def __init__(self, steps):
        self.steps = steps
        self.pending = next(steps)
        self.result = None

    def advance(self, ready):
        try:
            self.pending = self.steps.send(ready)
        except StopIteration as stop:
            self.pending, self.result = [], stop.value


def advance_after(group, other):
    joined = lax.optimization_barrier(list(group.pending) + list(other.pending))
    group.advance(joined[: len(group.pending)])


def advance_free(pending, others):
    joined = lax.optimization_barrier(list(pending) + list(others))
    return joined[: len(pending)], joined[len(pending) :]


def spread_dims(held, route):
    return jnp.expand_dims(held, axis_of(route[0]))


def advance_together(groups, others=()):
    joined = [entry for group in groups for entry in group.pending] + list(others)
    joined = lax.optimization_barrier(joined)
    for group in groups:
        count = len(group.pending)
        ready, joined = joined[:count], joined[count:]
        group.advance(ready)
    return joined


def shards(
    content,
    query_state,
    token_seg,
    positions,
    parent,
    w_query,
    w_key,
    w_value,
    w_out,
    w_inner,
    w_outer,
    b_inner,
    b_outer,
    gain_attn,
    bias_attn,
    gain_ffn,
    bias_ffn,
    bias_content,
    bias_segment,
    seg_embed,
    rel_table,
    cot_content,
    cot_query,
):
    micro_count, run, model = content.shape
    shard_count, dp_count = lax.axis_size("shard"), lax.axis_size("dp")
    shard, place = lax.axis_index("shard"), lax.axis_index("dp")
    heads = rel_table.shape[1]
    bucket_total = rel_table.shape[0] * shard_count
    hidden = w_inner.shape[1]
    pairs = heads // 2
    per_run = dp_count // tree_runs
    slots = path_runs * per_run
    span = slots * run
    rows_total = 2 * run * micro_count
    pieces = 2 if shard_count == 2 and dp_count == tree_runs else 1
    part_width = model // shard_count

    def fetch(weight):
        if pieces == 2:
            return [weight, lax.ppermute(weight, "shard", [(0, 1), (1, 0)])]
        return [lax.all_gather(weight, "shard", axis=0, tiled=True)]

    own_seg = token_seg[:, 0]
    own_slot = positions[:, 0] // run
    facts = jnp.stack([own_seg, own_slot], axis=1).reshape(2 * micro_count, 1).astype(low)
    fact_rows = jnp.broadcast_to(jnp.pad(facts, ((0, 16 - 2 * micro_count), (0, 0))), (16, model))
    third = model // 3
    columns = ((0, third), (third, third), (2 * third, third))
    content_rows = micro_count * run
    block = jnp.concatenate([content.reshape(content_rows, model), fact_rows], axis=0)
    total_bits = bit_total()
    block, b_inner, b_outer, parent, seg_embed, w_query, w_key, cot_content = lax.optimization_barrier(
        (block, b_inner, b_outer, parent, seg_embed, w_query, w_key, cot_content)
    )
    held = block.reshape((1,) * total_bits + block.shape)
    for bit in extra_bits():
        held = grow(held, bit)
    query_weights, key_weights = fetch(w_query), fetch(w_key)
    inner_rows = b_inner.shape[0] // part_width
    flat = [b_inner, b_outer, gain_attn, bias_attn, gain_ffn, bias_ffn, bias_content, bias_segment]
    flat += [seg_embed.reshape(-1), rel_table.reshape(-1)]
    fill = 16 * part_width - sum(entry.size for entry in flat)
    small_parts = jnp.concatenate(flat + [jnp.zeros((fill,), low)]).reshape(16, part_width)
    parts = []
    for part, (start, width) in enumerate(columns):
        height = block.shape[0] if part == 0 else content_rows
        parts.append(held[..., :height, start : start + width])
    parts, (query_weights[-1], key_weights[-1], w_value, small_parts, parent, content, cot_query) = advance_free(
        parts, [query_weights[-1], key_weights[-1], w_value, small_parts, parent, content, cot_query]
    )
    value_weights = fetch(w_value)
    first_branch, first_leaf = trunk_runs * per_run, (trunk_runs + 1) * per_run
    mine = own_seg
    above = jnp.sum(jnp.where(jnp.arange(parent.shape[2]) == mine[:, None], parent[:, 0], 0), axis=1)
    trunk, leaf = mine == 0, mine > trunk_runs
    branch = jnp.where(leaf, above, mine)
    lo = jnp.where(trunk, 0, jnp.where(leaf, first_leaf, first_branch)) * run
    hi = jnp.where(trunk, first_branch, jnp.where(leaf, slots, first_leaf)) * run
    early = jnp.stack([shard, place]).astype(jnp.int32)
    facts_own = jnp.stack([own_slot * run, lo, hi, mine, branch], axis=1)
    scalars = jnp.concatenate([early, facts_own.reshape(-1)]).astype(jnp.int32)

    rows = jnp.concatenate([content, query_state], axis=1).reshape(rows_total, model)
    cotangent = jnp.concatenate([cot_content, cot_query], axis=1).reshape(rows_total, model)
    if pieces == 2:
        other = lax.ppermute(small_parts, "shard", [(0, 1), (1, 0)])
        gathered = jnp.where(shard == 0, jnp.stack([small_parts, other]), jnp.stack([other, small_parts]))
    else:
        gathered = lax.all_gather(small_parts, "shard", axis=0, tiled=False)
    gathered = gathered.astype(f32)
    parts = [grow(piece, route[2]) for piece, route in zip(parts, routes_out)]
    parts, (value_weights[-1], w_out, w_inner, gathered, scalars, rows, cotangent) = advance_free(
        parts, [value_weights[-1], w_out, w_inner, gathered, scalars, rows, cotangent]
    )
    inner_weights, out_weights = fetch(w_inner), fetch(w_out)
    inner_bias = gathered[:, :inner_rows].reshape(1, hidden)
    vectors = jnp.transpose(gathered, (1, 0, 2)).reshape(16, model)
    table = gathered[:, 13, : rel_table.size].reshape(bucket_total, heads)

    parts = [grow(piece, route[1]) for piece, route in zip(parts, routes_out)]
    parts, (out_weights[-1], inner_weights[-1], w_outer, vectors, inner_bias, table) = advance_free(
        parts, [out_weights[-1], inner_weights[-1], w_outer, vectors, inner_bias, table]
    )
    outer_weights = fetch(w_outer)
    tree_parts = [entry for piece, route in zip(parts, routes_out) for entry in (piece, send(piece, route[0]))]
    tree_parts, (outer_weights[-1],) = advance_free(tree_parts, [outer_weights[-1]])

    grown = pltpu.CompilerParams(vmem_limit_bytes=vmem_bytes)

    def shape(dims, kind):
        return jax.ShapeDtypeStruct(dims, kind)

    dma = pltpu.SemaphoreType.DMA
    query_low, query_segment = pl.pallas_call(
        functools.partial(query_kernel, pieces),
        out_shape=(shape((rows_total, model), low),) * 2,
        in_specs=[smem_space, vmem_space, vmem_space] + [any_space] * pieces,
        out_specs=(vmem_space,) * 2,
        scratch_shapes=[pltpu.VMEM((model, model), low), dma((pieces,))],
        compiler_params=grown,
        name="query_projection",
        cost_estimate=cost(1),
    )(early, rows, vectors, *query_weights)

    path, keys, values, found = pl.pallas_call(
        functools.partial(keys_kernel, pieces, columns, [route[0] for route in routes_out], run, slots),
        out_shape=(
            shape((micro_count, span, model), low),
            shape((micro_count * span, model), low),
            shape((micro_count * span, model), low),
            shape((micro_count * slots,), jnp.int32),
        ),
        in_specs=[smem_space] + [any_space] * (2 * len(columns) + 2 * pieces),
        out_specs=(vmem_space,) * 3 + (smem_space,),
        scratch_shapes=[
            pltpu.VMEM((model, model), low),
            pltpu.VMEM((model, model), low),
            pltpu.VMEM((2,) * total_bits + (content_rows + 16, model), low),
            dma((2 * pieces,)),
            dma((2 * len(columns),)),
        ],
        compiler_params=grown,
        name="path_keys",
        cost_estimate=cost(6),
    )(scalars, *tree_parts, *key_weights, *value_weights)
    path = path.reshape(micro_count * span, model)

    def blocks_at(first):
        return (
            pl.BlockSpec((rows_total, 128), lambda pair: (0, pair + first)),
            pl.BlockSpec((micro_count * span, 128), lambda pair: (0, pair + first)),
            pl.BlockSpec((micro_count, 4 * run, span), lambda pair: (pair + first, 0, 0)),
            pl.BlockSpec((16, 128), lambda pair: (0, pair + first)),
        )

    row_block, key_block, prob_block, vector_block = blocks_at(0)
    probs, attended = pl.pallas_call(
        functools.partial(attend_kernel, run, slots),
        grid=(pairs,),
        out_shape=(
            shape((pairs * micro_count, 4 * run, span), low),
            shape((rows_total, model), f32),
        ),
        in_specs=[smem_space, smem_space, row_block, row_block, key_block, key_block, vector_block],
        out_specs=(prob_block, row_block),
        compiler_params=grown,
        name="attend",
        cost_estimate=cost(11),
    )(scalars, table, query_low, query_segment, keys, values, vectors)

    half = model // 2
    if pieces == 2:
        grad_shapes = [shape((2,) * (total_bits - 1) + (half, half), low)] * 4
        grad_specs = [any_space] * len(grad_shapes)
        grad_scratch = [pltpu.VMEM((2,) * (1 + total_bits) + (half, half), low)]
    else:
        grad_shapes = [shape((hidden, model), low), shape((model, hidden), low)]
        grad_specs = [vmem_space] * 2
        grad_scratch = []
    results = pl.pallas_call(
        functools.partial(feed_kernel, pieces, run),
        out_shape=[
            shape((micro_count, run, model), low),
            shape((micro_count, run, model), low),
            shape((rows_total, model), f32),
            shape((rows_total, model), low),
            shape((rows_total, model), low),
            shape((16, model), f32),
        ]
        + grad_shapes,
        in_specs=[smem_space] + [vmem_space] * 5 + [any_space] * (3 * pieces),
        out_specs=[vmem_space] * 6 + grad_specs,
        scratch_shapes=[
            pltpu.VMEM((model, model), low),
            pltpu.VMEM((model, hidden), low),
            pltpu.VMEM((hidden, model), low),
            pltpu.VMEM((rows_total, hidden), low),
            pltpu.VMEM((rows_total, hidden), f32),
        ]
        + grad_scratch
        + [dma((3 * pieces,))]
        + ([dma((12,))] if pieces == 2 else []),
        compiler_params=grown,
        name="feed_forward",
        cost_estimate=cost(21),
    )(scalars, rows, attended, cotangent, vectors, inner_bias, *out_weights, *inner_weights, *outer_weights)
    out_content, out_query, d_mid_in, d_branch, d_att, small_first = results[:6]

    swap = [(0, 1), (1, 0)]
    if pieces == 2:
        feed_grads = results[6:]
        feed_other = [lax.ppermute(entry, "shard", swap) for entry in (feed_grads[3], feed_grads[2])]

    def attend_back(first, pair_count, gradient):
        rows_in, keys_in, probs_in, vector_in = blocks_at(first)
        return pl.pallas_call(
            functools.partial(back_kernel, run, slots),
            grid=(pair_count,),
            out_shape=(
                shape((rows_total, 128 * pair_count), low),
                shape((micro_count * span, 128 * pair_count), low),
                shape((micro_count * span, 128 * pair_count), low),
                shape((8, 128 * pair_count), f32),
                shape((2 * pair_count, 16, span), f32),
            ),
            in_specs=[smem_space, rows_in, rows_in, keys_in, keys_in, probs_in, rows_in, rows_in, vector_in],
            out_specs=(
                row_block,
                key_block,
                key_block,
                pl.BlockSpec((8, 128), lambda pair: (0, pair)),
                pl.BlockSpec((2, 16, span), lambda pair: (pair, 0, 0)),
            ),
            compiler_params=grown,
            name="attend_back",
            cost_estimate=cost(3),
        )(scalars, query_low, query_segment, keys, values, probs, gradient, attended, vectors)

    back_first = attend_back(0, pairs // 3, d_att)
    if pieces == 2:
        sizes = [height for _, height in feed_cuts(pieces, model)]
        upper = [
            spread_dims(feed_grads[1][..., start : start + height, :] + feed_other[0][..., start : start + height, :], route)
            for (start, height), route in zip(feed_cuts(pieces, model), routes_out)
        ]
        feed_lower = feed_other[1]
        *upper, feed_lower, d_att, _ = lax.optimization_barrier((*upper, feed_lower, d_att, back_first[0]))
        lower = [
            spread_dims(feed_grads[0][..., start : start + height, :] + feed_lower[..., start : start + height, :], route)
            for (start, height), route in zip(feed_cuts(pieces, model), routes_out)
        ]
        feed_rounds = Rounds(sum_rounds(lower, upper, sizes))
        feed_rounds.advance(feed_rounds.pending)
    back_second = attend_back(pairs // 3, pairs - pairs // 3, d_att)
    tree_height = 2 * micro_count * run
    if pieces == 2:
        whole = later_cuts(model)[-1][0] + later_cuts(model)[-1][1]
        heights = [entry[1] for entry in later_cuts(model)]
        cube = (2,) * (total_bits - 1)
        grad_shapes = [shape(cube + (whole, half), low)] * 4
        grad_specs = [any_space] * 4
        extra = [pltpu.VMEM((2,) * (1 + total_bits) + (whole, half), low), dma((12,))]
        tree_shapes = [shape(cube + (tree_height, half), low)] * 2
    else:
        grad_shapes = [shape((model, model), low)] * 4 + [shape((32, model), f32)]
        grad_specs = [vmem_space] * 5
        extra = []
        tree_shapes = [shape((2,) * total_bits + (tree_height, half), low)]
    later = pl.pallas_call(
        functools.partial(weights_kernel, pieces),
        out_shape=grad_shapes,
        in_specs=[smem_space] + [vmem_space] * 15,
        out_specs=grad_specs,
        scratch_shapes=extra,
        compiler_params=grown,
        name="weight_gradients",
        cost_estimate=cost(3),
    )(scalars, rows, path, attended, d_branch, small_first, *back_first, *back_second)
    if pieces == 2:
        feed_rounds.pending, later = advance_free(feed_rounds.pending, later)
        feed_rounds.pending, (d_mid_in,) = advance_free(feed_rounds.pending, [d_mid_in])
        feed_rounds.advance(feed_rounds.pending)
    d_content, grad_query, *tree_grads = pl.pallas_call(
        functools.partial(tree_kernel, pieces, run, slots),
        out_shape=[shape((micro_count, run, model), f32)] * 2 + tree_shapes,
        in_specs=[smem_space] * 2 + [vmem_space] * 7 + [any_space] * (3 * pieces),
        out_specs=[vmem_space] * 2 + [any_space] * len(tree_shapes),
        scratch_shapes=[
            pltpu.VMEM((3, model, model), low),
            pltpu.VMEM((2,) * total_bits + (tree_height, half), low),
            dma((3 * pieces,)),
            dma((6,)),
        ],
        compiler_params=grown,
        name="tree_gradients",
        cost_estimate=cost(3),
    )(scalars, found, d_mid_in, *back_first[:3], *back_second[:3], *query_weights, *key_weights, *value_weights)

    if pieces == 2:
        others = [lax.ppermute(entry, "shard", swap) for entry in (later[3], later[2])]
        feed_rounds.pending, others = advance_free(feed_rounds.pending, others)
        feed_rounds.pending, tree_grads = advance_free(feed_rounds.pending, tree_grads)
        feed_rounds.advance(feed_rounds.pending)

        def route_sum(which, part):
            start, height = later_cuts(model)[part]
            more, tall = tree_cuts(tree_height)[part]
            mine, other = later[which][..., start : start + height, :], others[1 - which][..., start : start + height, :]
            more_rows = tree_grads[which][..., more : more + tall, :]
            return spread_dims(jnp.concatenate([mine + other, more_rows], axis=-2), routes_out[part])

        lower = [route_sum(0, part) for part in range(3)]
        upper = [route_sum(1, part) for part in range(3)]
        later_rounds = Rounds(sum_rounds(lower, upper, heights))
        for _ in range(4):
            advance_together([feed_rounds, later_rounds])
        advance_together([later_rounds])
        feed_done = advance_together([later_rounds], feed_rounds.result[0])
        advance_together([later_rounds])

        def pieces_scratch(sizes):
            return [pltpu.VMEM((2,) * total_bits + (height, half), low) for height in sizes] + [dma((6,))]

        grad_w_outer, grad_w_inner = pl.pallas_call(
            feed_spread_kernel,
            out_shape=(shape(w_outer.shape, f32), shape(w_inner.shape, f32)),
            in_specs=[smem_space] + [any_space] * 6,
            out_specs=(vmem_space,) * 2,
            scratch_shapes=pieces_scratch([height for _, height in feed_cuts(pieces, model)]),
            compiler_params=grown,
            name="feed_spread",
            cost_estimate=cost(7),
        )(early, *feed_done)
        later_done, shares = later_rounds.result
        arrived = [share.reshape(share.shape[-2:]) for share in shares]
        tree_grad = jnp.concatenate(arrived, axis=0)
        spread_out = pl.pallas_call(
            later_spread_kernel,
            out_shape=[shape(w_query.shape, f32)] * 4
            + [shape(b_inner.shape, f32)]
            + [shape(b_outer.shape, f32)] * 7
            + [shape(seg_embed.shape, f32), shape(rel_table.shape, f32)],
            in_specs=[smem_space] + [any_space] * 6,
            out_specs=[vmem_space] * 14,
            scratch_shapes=pieces_scratch(heights),
            compiler_params=grown,
            name="later_spread",
            cost_estimate=cost(4),
        )(early, *later_done)
        grad_w_query, grad_w_key, grad_w_value, grad_w_out, grad_b_inner, *narrow, grad_rel_table = spread_out
    else:
        totals = []
        for entry in (*results[6:8], *later[:4]):
            share = lax.psum_scatter(entry, "shard", scatter_dimension=0, tiled=True)
            totals.append(lax.psum(share, "dp").astype(f32))
        grad_w_outer, grad_w_inner, grad_w_query, grad_w_key, grad_w_value, grad_w_out = totals
        tree_grad = scatter_blocks(tree_grads[0], routes_out[0])
        small = lax.psum(later[4], ("shard", "dp"))
        grad_b_inner = lax.dynamic_slice_in_dim(small[:4].reshape(-1), shard * b_inner.shape[0], b_inner.shape[0])
        narrow = lax.dynamic_slice_in_dim(small[4:13], shard * part_width, part_width, axis=1)
        narrow = [*narrow[:7], narrow[7:9]]
        grad_rel_table = lax.dynamic_slice_in_dim(
            small[16 : 16 + bucket_total, :heads], shard * rel_table.shape[0], rel_table.shape[0], axis=0
        )
    halves = tree_grad.astype(f32).reshape(2, micro_count, run, half)
    grad_content = d_content + jnp.concatenate([halves[0], halves[1]], axis=-1)
    return (
        out_content,
        out_query,
        grad_content,
        grad_query,
        grad_w_query,
        grad_w_key,
        grad_w_value,
        grad_w_out,
        grad_w_inner,
        grad_w_outer,
        grad_b_inner,
        narrow[0],
        narrow[1],
        narrow[2],
        narrow[3],
        narrow[4],
        narrow[5],
        narrow[6],
        narrow[7],
        grad_rel_table,
    )


def solution(mesh):
    rows = P(None, ("shard", "dp"), None)
    tokens = P(None, ("shard", "dp"))
    matrix = P("shard", None)
    vector = P("shard")
    return jax.shard_map(
        shards,
        mesh=mesh,
        in_specs=(rows, rows, tokens, tokens, P(None, "shard", None))
        + (matrix,) * 6
        + (vector,) * 8
        + (P(None, "shard"), matrix, rows, rows),
        out_specs=(rows,) * 4 + (matrix,) * 6 + (vector,) * 8 + (P(None, "shard"), matrix),
        check_vma=False,
    )
```

```python
import functools

import jax
import jax.numpy as jnp
from jax import lax
from jax.experimental import pallas as pl
from jax.experimental.pallas import tpu as pltpu
from jax.sharding import PartitionSpec as P

thresholds = (1, 2, 4, 8, 32, 128, 512)
norm_eps = 1e-05
masked_score = -1e30
path_runs = 6
trunk_runs = 4
tree_runs = 16
vmem_bytes = 60 * 1024 * 1024
low = jnp.bfloat16
f32 = jnp.float32
def cost(microseconds):
    return pl.CostEstimate(flops=int(microseconds * 1e9), bytes_accessed=0, transcendentals=0)


any_space = pl.BlockSpec(memory_space=pl.ANY)
smem_space = pl.BlockSpec(memory_space=pltpu.SMEM)
vmem_space = pl.BlockSpec(memory_space=pltpu.VMEM)


def mm(left, right):
    return lax.dot_general(left, right, (((1,), (0,)), ((), ())), preferred_element_type=f32)


def mm_nt(left, right):
    return lax.dot_general(left, right, (((1,), (1,)), ((), ())), preferred_element_type=f32)


def mm_tn(left, right):
    return lax.dot_general(left, right, (((0,), (0,)), ((), ())), preferred_element_type=f32)


def weight_copies(pieces, target, sems, first, shard):
    if len(pieces) == 1:
        return [pltpu.make_async_copy(pieces[0], target, sems.at[first])]
    half = pieces[0].shape[0]
    own = pl.multiple_of(shard * half, 16)
    other = pl.multiple_of((1 - shard) * half, 16)
    return [
        pltpu.make_async_copy(pieces[0], target.at[pl.ds(own, half)], sems.at[first]),
        pltpu.make_async_copy(pieces[1], target.at[pl.ds(other, half)], sems.at[first + 1]),
    ]


def scalar_at(scalars, micro, entry):
    return scalars[2 + 5 * micro + entry]


def block_index(at, total):
    return tuple((at >> (total - 1 - i)) & 1 for i in range(total))


def half_index(bit, which, total):
    everything = [slice(None)] * total
    everything[total - 1 - bit] = pl.ds(which, 1)
    return tuple(everything)


def half_at(bit, which, total):
    everything = [slice(None)] * total
    everything[total - 1 - bit] = which
    return tuple(everything)


def query_kernel(pieces, scalars, rows, vectors, *refs):
    weights = refs[:pieces]
    query_low, query_segment, full, sems = refs[pieces:]
    copies = weight_copies(weights, full, sems, 0, scalars[0])
    for copy in copies:
        copy.start()
    for copy in copies:
        copy.wait()
    raw = mm(rows[...], full[...])
    query_low[...] = (raw + vectors[9:10, :]).astype(low)
    query_segment[...] = (raw + vectors[10:11, :]).astype(low)


def keys_kernel(pieces, columns, lasts, run, slots, scalars, *refs):
    parts = refs[: 2 * len(columns)]
    refs = refs[2 * len(columns) :]
    key_weights, value_weights = refs[:pieces], refs[pieces : 2 * pieces]
    path, keys, values, found, full_key, full_value, tree, sems, tree_sems, prefetch = refs[2 * pieces :]
    shard = scalars[0]
    total = len(tree.shape) - 2
    moves = []
    for part, (start, width) in enumerate(columns):
        for which in range(2):
            source = parts[2 * part + which]
            target = tree.at[
                (*half_index(lasts[part], which, total), pl.ds(0, source.shape[-2]), pl.ds(start, width))
            ]
            moves.append(pltpu.make_async_copy(source, target, tree_sems.at[2 * part + which]))
    copies = weight_copies(key_weights, full_key, sems, 0, shard)
    copies = copies + weight_copies(value_weights, full_value, sems, pieces, shard)
    for copy in moves + copies:
        copy.start()
    for copy in moves:
        copy.wait()
    prefetch()
    micro_count = path.shape[0]
    content_rows = micro_count * run
    facts = [
        tree[(*block_index(block, total), slice(content_rows, content_rows + 16), slice(0, 128))].astype(f32)
        for block in range(1 << total)
    ]
    numbers = lax.broadcasted_iota(jnp.int32, (1 << total, 128), 0)
    for micro in range(micro_count):
        segs = jnp.concatenate([entry[2 * micro : 2 * micro + 1] for entry in facts], axis=0).astype(jnp.int32)
        places = jnp.concatenate([entry[2 * micro + 1 : 2 * micro + 2] for entry in facts], axis=0).astype(jnp.int32)
        for slot in range(slots):
            if slot < slots // path_runs * trunk_runs:
                wanted = 0
            else:
                wanted = scalar_at(scalars, micro, 4 if slot < slots // path_runs * (trunk_runs + 1) else 3)
            shown = (segs == wanted) & (places == slot)
            relative = jnp.max(jnp.where(shown, numbers, 0))
            found[micro * slots + slot] = relative
            at = block_index(relative, total)
            path[micro, slot * run : (slot + 1) * run, :] = tree[(*at, slice(micro * run, (micro + 1) * run), slice(None))]
    for copy in copies:
        copy.wait()
    for micro in range(micro_count):
        rows = path[micro]
        span = slots * run
        keys[micro * span : (micro + 1) * span, :] = mm(rows, full_key[...]).astype(low)
        values[micro * span : (micro + 1) * span, :] = mm(rows, full_value[...]).astype(low)


def start_all(groups):
    for group in groups:
        for copy in group:
            copy.start()


def forward_kernel(pieces, columns, lasts, run, slots, scalars, table, *refs):
    query_low, query_segment, rows, cotangent, vectors, inner_bias = refs[:6]
    parts, refs = refs[6 : 6 + 2 * len(columns)], refs[6 + 2 * len(columns) :]
    pair_weights, feed_weights, refs = refs[: 2 * pieces], refs[2 * pieces : 5 * pieces], refs[5 * pieces :]
    path_out, keys_out, values_out, probs_out, found, attended = refs[:6]
    refs = refs[6:]
    feed_outs = refs[: 6 + (4 if pieces == 2 else 2)]
    refs = refs[len(feed_outs) :]
    path, keys, values, probs, full_key, full_value, tree, out_sems, pair_sems, tree_sems = refs[:10]
    feed_scratch = refs[10:]
    sems = feed_scratch[6] if pieces == 2 else feed_scratch[5]
    copies = [
        weight_copies(feed_weights[i * pieces : (i + 1) * pieces], feed_scratch[i], sems, i * pieces, scalars[0])
        for i in range(3)
    ]
    keys_kernel(
        pieces,
        columns,
        lasts,
        run,
        slots,
        scalars,
        *parts,
        *pair_weights,
        path,
        keys,
        values,
        found,
        full_key,
        full_value,
        tree,
        pair_sems,
        tree_sems,
        lambda: start_all(copies),
    )
    leaving = [
        pltpu.make_async_copy(path, path_out, out_sems.at[0]),
        pltpu.make_async_copy(keys, keys_out, out_sems.at[1]),
        pltpu.make_async_copy(values, values_out, out_sems.at[2]),
    ]
    for copy in leaving:
        copy.start()
    micro_count = path.shape[0]

    def attend(pair, carry):
        lanes = pl.ds(pl.multiple_of(pair * 128, 128), 128)
        attend_kernel(
            run,
            slots,
            pair,
            scalars,
            table,
            query_low.at[:, lanes],
            query_segment.at[:, lanes],
            keys.at[:, lanes],
            values.at[:, lanes],
            vectors.at[:, lanes],
            probs.at[pl.ds(pair * micro_count, micro_count)],
            attended.at[:, lanes],
        )
        return carry

    lax.fori_loop(0, rows.shape[1] // 128, attend, 0)
    leaving.append(pltpu.make_async_copy(probs, probs_out, out_sems.at[3]))
    leaving[-1].start()
    feed_kernel(
        pieces, run, copies, scalars, rows, attended, cotangent, vectors, inner_bias, *feed_outs, *feed_scratch
    )
    for copy in leaving:
        copy.wait()


def head_masks():
    lane = lax.broadcasted_iota(jnp.int32, (1, 128), 1)
    first = lane < 64
    return first, first.astype(f32).astype(low), (1.0 - first.astype(f32)).astype(low)


def stack_query(query_low, query_segment, mask_a, mask_b):
    both = jnp.concatenate([query_low, query_segment], axis=1)
    wide_a = jnp.concatenate([mask_a, mask_a], axis=1)
    wide_b = jnp.concatenate([mask_b, mask_b], axis=1)
    return jnp.concatenate([both * wide_a, both * wide_b], axis=0)


def stack_keys(keys, vectors, lo):
    row = lax.broadcasted_iota(jnp.int32, (keys.shape[0], 1), 0)
    segment = jnp.where(row >= lo, vectors[12:13, :], vectors[11:12, :]).astype(low)
    return jnp.concatenate([keys, segment], axis=1)


def offsets_of(base, run, span):
    row = lax.broadcasted_iota(jnp.int32, (run, span), 0)
    column = lax.broadcasted_iota(jnp.int32, (run, span), 1)
    return base + row - column, column


def attend_kernel(run, slots, pair, scalars, table, query_low, query_segment, keys, values, vectors, probs, attended):
    span = slots * run
    first, mask_a, mask_b = head_masks()
    for micro in range(probs.shape[0]):
        base, lo, hi = (scalar_at(scalars, micro, entry) for entry in range(3))
        rows = slice(micro * 2 * run, (micro + 1) * 2 * run)
        columns = slice(micro * span, (micro + 1) * span)
        left = stack_query(query_low[rows, :], query_segment[rows, :], mask_a, mask_b)
        right = stack_keys(keys[columns, :], vectors[...], lo)
        raw = mm_nt(left, right)
        delta, column = offsets_of(base, run, span)
        visible = column < hi
        biases = []
        for head in range(2):
            at = 2 * pair + head
            bias = jnp.full((run, span), table[0, at], f32)
            for step, threshold in enumerate(thresholds):
                if threshold < span:
                    bias = jnp.where(delta >= threshold, table[1 + step, at], bias)
                    bias = jnp.where(delta <= -threshold, table[9 + step, at], bias)
            bias = jnp.where(visible, bias, masked_score)
            biases.append(bias)
            biases.append(jnp.where(delta == 0, masked_score, bias))
        scores = raw * 0.125 + jnp.concatenate(biases, axis=0)
        peak = jnp.max(scores, axis=-1, keepdims=True)
        mass = jnp.exp(scores - peak)
        total = jnp.sum(mass, axis=-1, keepdims=True)
        probs_low = (mass * (1.0 / total)).astype(low)
        probs[micro] = probs_low
        heads = mm(probs_low, values[columns, :])
        attended[rows, :] = jnp.where(first, heads[: 2 * run], heads[2 * run :])


def norm_forward(inputs):
    centred = inputs - jnp.mean(inputs, axis=-1, keepdims=True)
    scale = lax.rsqrt(jnp.mean(centred * centred, axis=-1, keepdims=True) + norm_eps)
    return centred * scale, scale


def norm_backward(gradient, gain, normal, scale):
    d_normal = gradient * gain
    mean_first = jnp.mean(d_normal, axis=-1, keepdims=True)
    mean_second = jnp.mean(d_normal * normal, axis=-1, keepdims=True)
    return scale * (d_normal - mean_first - normal * mean_second)


def column_sum(inputs):
    return jnp.sum(inputs, axis=0, keepdims=True)


def feed_cuts(pieces, model):
    if pieces == 1:
        return ()
    step = model // 6
    return ((0, step), (step, step), (2 * step, step))


def later_cuts(model):
    whole = model // 4 + 16
    step = whole // 40 * 16
    return ((0, step), (step, step), (2 * step, whole - 2 * step))


def tree_cuts(height):
    step = height // 48 * 16 + 16
    return ((0, step), (step, step), (2 * step, height - 2 * step))


def feed_kernel(pieces, run, copies, scalars, rows, attended, cotangent, vectors, inner_bias, *refs):
    out_content, out_query, d_mid_in, d_branch_out, d_att, small = refs[:6]
    routes = feed_cuts(pieces, rows.shape[1])
    outputs = 4 if pieces == 2 else 2
    grads = refs[6 : 6 + outputs]
    full_out, full_inner, full_outer, act_low, slope = refs[6 + outputs : 11 + outputs]
    if pieces == 2:
        held, sems, grad_sems = refs[11 + outputs :]
    shard, place = scalars[0], scalars[1]
    model = rows.shape[1]
    hidden = full_inner.shape[1]
    att_low = attended[...].astype(low)
    for copy in copies[0]:
        copy.wait()
    normal_first, scale_first = norm_forward(mm(att_low, full_out[...]) + rows[...].astype(f32))
    middle = normal_first * vectors[5:6, :] + vectors[6:7, :]
    middle_low = middle.astype(low)
    for copy in copies[1]:
        copy.wait()
    wide = model
    total = None
    for start in range(0, hidden, wide):
        at = slice(start, start + wide)
        pre = mm(middle_low, full_inner[:, at]) + inner_bias[:, at]
        squared = pre * pre
        bent = jnp.tanh(0.7978845608028654 * pre * (1.0 + 0.044715 * squared))
        half = 0.5 * (1.0 + bent)
        act = (pre * half).astype(low)
        act_low[:, at] = act
        slope[:, at] = half + (0.5 * 0.7978845608028654) * pre * (1.0 - bent * bent) * (
            1.0 + (3 * 0.044715) * squared
        )
        if start == 0:
            for copy in copies[2]:
                copy.wait()
        share = mm(act, full_outer[at, :])
        total = share if total is None else total + share
    normal_second, scale_second = norm_forward(total + vectors[4:5, :] + middle)
    final = (normal_second * vectors[7:8, :] + vectors[8:9, :]).astype(low)
    for micro in range(out_content.shape[0]):
        start = 2 * run * micro
        out_content[micro] = final[start : start + run]
        out_query[micro] = final[start + run : start + 2 * run]
    d_final = cotangent[...].astype(f32)
    small[7:8, :] = column_sum(d_final * normal_second)
    small[8:9, :] = column_sum(d_final)
    d_final_in = norm_backward(d_final, vectors[7:8, :], normal_second, scale_second)
    d_outer = d_final_in.astype(low)
    small[4:5, :] = column_sum(d_outer.astype(f32))
    block = model // 2

    def hold_outer(start, value):
        if pieces == 1:
            grads[0][start : start + block, :] = value.astype(low)
            return
        half = hidden // 2
        target = (start // half) ^ shard
        for down in range(2):
            for across in range(2):
                chunk = ((start % half) // (block // 2) + down) * 2 + across
                held[(target, *block_index(chunk ^ place, 4), slice(0, block // 2), slice(None))] = value[
                    down * (block // 2) : (down + 1) * (block // 2), across * block : (across + 1) * block
                ].astype(low)

    def hold_inner(start, value):
        if pieces == 1:
            grads[1][:, start : start + block] = value.astype(low)
            return
        for quarter in range(4):
            chunk = (quarter % 2) * 8 + start // block
            held[
                ((quarter // 2) ^ shard, *block_index(chunk ^ place, 4), slice(block // 2, block), slice(None))
            ] = value[
                quarter * (block // 2) : (quarter + 1) * (block // 2), :
            ].astype(low)

    for start in range(0, hidden, block):
        hold_outer(start, mm_tn(act_low[:, start : start + block], d_outer))
    sent = []
    for part, (start, height) in enumerate(routes):
        for side in range(2):
            for which in range(2):
                rows_at = (pl.ds(start, height), slice(None))
                source = held.at[(side, *half_at(routes_out[part][0], which, 4), *rows_at)]
                target = grads[2 * side + which].at[(*(slice(None),) * 3, *rows_at)]
                sent.append(pltpu.make_async_copy(source, target, grad_sems.at[4 * part + 2 * side + which]))
    for copy in sent[:4]:
        copy.start()
    d_middle = d_final_in
    for start in range(0, hidden, block):
        at = slice(start, start + block)
        d_inner = (mm_nt(d_outer, full_outer[at, :]) * slope[:, at]).astype(low)
        summed = column_sum(d_inner.astype(f32))
        row, lane = start // model, start % model
        small[row : row + 1, lane : lane + block] = summed
        hold_inner(start, mm_tn(middle_low, d_inner))
        d_middle = d_middle + mm_nt(d_inner, full_inner[:, at])
    for copy in sent[4:]:
        copy.start()
    small[5:6, :] = column_sum(d_middle * normal_first)
    small[6:7, :] = column_sum(d_middle)
    small[9:16, :] = jnp.zeros((7, model), f32)
    d_mid = norm_backward(d_middle, vectors[5:6, :], normal_first, scale_first)
    d_mid_in[...] = d_mid
    d_branch = d_mid.astype(low)
    d_branch_out[...] = d_branch
    d_att[...] = mm_nt(d_branch, full_out[...]).astype(low)
    for copy in sent:
        copy.wait()


def back_kernel(
    run,
    slots,
    scalars,
    query_low,
    query_segment,
    keys,
    values,
    probs,
    d_att,
    attended,
    vectors,
    d_query,
    d_keys,
    d_values,
    small,
    buckets,
):
    span = slots * run
    first, mask_a, mask_b = head_masks()
    shares = jnp.zeros((8, 128), f32)
    tallies = [jnp.zeros((16, span), f32)] * 2
    for micro in range(probs.shape[0]):
        base, lo = scalar_at(scalars, micro, 0), scalar_at(scalars, micro, 1)
        rows = slice(micro * 2 * run, (micro + 1) * 2 * run)
        columns = slice(micro * span, (micro + 1) * span)
        gradient = d_att[rows, :]
        stacked = jnp.concatenate([gradient * mask_a, gradient * mask_b], axis=0)
        product = gradient.astype(f32) * attended[rows, :]
        delta_a = jnp.sum(jnp.where(first, product, 0.0), axis=-1, keepdims=True)
        delta_b = jnp.sum(jnp.where(first, 0.0, product), axis=-1, keepdims=True)
        delta_row = jnp.concatenate([delta_a, delta_b], axis=0)
        probs_low = probs[micro]
        d_probs = mm_nt(stacked, values[columns, :])
        d_scores = (probs_low.astype(f32) * (d_probs - delta_row)).astype(low)
        left = stack_query(query_low[rows, :], query_segment[rows, :], mask_a, mask_b)
        right = stack_keys(keys[columns, :], vectors[...], lo)
        d_left = mm(d_scores, right) * 0.125
        mine = jnp.concatenate([first, first], axis=1)
        d_left = jnp.where(mine, d_left[: 2 * run], d_left[2 * run :])
        d_content, d_segment = d_left[:, :128], d_left[:, 128:]
        d_query[rows, :] = (d_content + d_segment).astype(low)
        d_right = mm_tn(d_scores, left) * 0.125
        d_keys[columns, :] = d_right[:, :128].astype(low)
        d_values[columns, :] = mm_tn(probs_low, stacked).astype(low)
        row = lax.broadcasted_iota(jnp.int32, (span, 1), 0)
        d_embed = d_right[:, 128:]
        shares = shares + jnp.concatenate(
            [
                column_sum(d_content),
                column_sum(d_segment),
                column_sum(jnp.where(row >= lo, 0.0, d_embed)),
                column_sum(jnp.where(row >= lo, d_embed, 0.0)),
                jnp.zeros((4, 128), f32),
            ],
            axis=0,
        )
        delta, _ = offsets_of(base, run, span)
        exact = d_scores.astype(f32)
        for head in range(2):
            at = 2 * run * head
            both = exact[at : at + run] + exact[at + run : at + 2 * run]
            lines = [None] * 16
            lines[0] = column_sum(jnp.where(delta == 0, both, 0.0))
            for step, threshold in enumerate(thresholds):
                if threshold < span:
                    later = thresholds[step + 1] if step + 1 < len(thresholds) else span
                    above = (delta >= threshold) & (delta < later)
                    below = (delta <= -threshold) & (delta > -later)
                    lines[1 + step] = column_sum(jnp.where(above, both, 0.0))
                    lines[9 + step] = column_sum(jnp.where(below, both, 0.0))
            blank = jnp.zeros((1, span), f32)
            tallies[head] = tallies[head] + jnp.concatenate(
                [blank if entry is None else entry for entry in lines], axis=0
            )
    small[...] = shares
    for head in range(2):
        buckets[head] = tallies[head]


def columns_of(parts, at):
    pieces, start = [], 0
    for part in parts:
        low_end, high_end = max(at.start, start), min(at.stop, start + part.shape[1])
        if low_end < high_end:
            pieces.append(part[:, low_end - start : high_end - start])
        start += part.shape[1]
    return pieces[0] if len(pieces) == 1 else jnp.concatenate(pieces, axis=1)


def weights_kernel(
    pieces,
    scalars,
    rows,
    path,
    attended,
    d_branch,
    small_first,
    *refs,
):
    d_query, d_keys, d_values, small_second, tallies = (refs[i : 10 : 5] for i in range(5))
    refs = refs[10:]
    model = rows.shape[1]
    block = model // 2
    if pieces == 2:
        kept, sent, held, grad_sems = refs[:2], refs[2:4], *refs[4:]
    else:
        natural, small_out = refs[:4], refs[4]
    shard, place = scalars[0], scalars[1]
    small_rows = block // 8

    def hold(which, across, value):
        if pieces == 1:
            natural[which][:, across * block : (across + 1) * block] = value.astype(low)
            return
        spot = (slice(which * small_rows, (which + 1) * small_rows), slice(None))
        for half in range(2):
            for down in range(8):
                start = half * block + down * small_rows
                held[(half ^ shard, *block_index((down * 2 + across) ^ place, 4), *spot)] = value[
                    start : start + small_rows, :
                ].astype(low)

    for across in range(2):
        at = slice(across * block, (across + 1) * block)
        hold(0, across, mm_tn(rows[...], columns_of(d_query, at)))
        hold(1, across, mm_tn(path[...], columns_of(d_keys, at)))
        hold(2, across, mm_tn(path[...], columns_of(d_values, at)))
        hold(3, across, mm_tn(attended[...].astype(low), d_branch[:, at]))
    buckets = jnp.zeros((16, 16), f32)
    every_head = [part[head] for part in tallies for head in range(part.shape[0])]
    line = lax.broadcasted_iota(jnp.int32, every_head[0].shape, 0)
    for head, tally in enumerate(every_head):
        buckets = buckets + lax.dot_general(
            tally,
            (line == head).astype(f32),
            (((1,), (1,)), ((), ())),
            precision=lax.Precision.HIGHEST,
            preferred_element_type=f32,
        )
    if pieces == 1:
        small_out[:9, :] = small_first[:9, :]
        for across in range(2):
            small_out[9:13, across * block : (across + 1) * block] = columns_of(small_second, slice(across * block, (across + 1) * block))[:4]
        small_out[13:, :] = jnp.zeros((small_out.shape[0] - 13, model), f32)
        small_out[16:32, :16] = buckets
    else:
        last = model // 4
        for half in range(2):
            at = slice(half * block, (half + 1) * block)
            lines = [
                small_first[2 * half + i // 2 : 2 * half + i // 2 + 1, (i % 2) * block : (i % 2 + 1) * block]
                for i in range(4)
            ]
            lines += [small_first[i : i + 1, at] for i in range(4, 9)]
            late_lines = columns_of(small_second, at)
            lines += [late_lines[i : i + 1, :] for i in range(4)]
            for chunk in range(16):
                line = lines[chunk].astype(low) if chunk < 13 else jnp.zeros((1, block), low)
                spread_line = jnp.concatenate([line.astype(f32), jnp.zeros((15, block), f32)], axis=0)
                held[(half ^ shard, *block_index(chunk ^ place, 4), slice(last, last + 16), slice(None))] = spread_line.astype(low)
            wide = jnp.concatenate([buckets[8 * half : 8 * half + 8], jnp.zeros((8, 16), f32)], axis=0)
            wide = jnp.concatenate([wide, jnp.zeros((16, block - 16), f32)], axis=1)
            held[(half ^ shard, *block_index(13 ^ place, 4), slice(last, last + 16), slice(None))] = wide.astype(low)
    leaving = []
    if pieces == 2:
        for part, (start, height) in enumerate(later_cuts(model)):
            for which in range(2):
                at = 2 * part + which
                rows_at = (pl.ds(start, height), slice(None))
                for side in range(2):
                    source = held.at[(side, *half_at(routes_out[part][0], which, 4), *rows_at)]
                    target = (kept, sent)[side][which].at[(*(slice(None),) * 3, *rows_at)]
                    leaving.append(pltpu.make_async_copy(source, target, grad_sems.at[6 * side + at]))
        for copy in leaving:
            copy.start()
    for copy in leaving:
        copy.wait()


def tree_kernel(pieces, run, slots, scalars, found, d_mid_in, *refs):
    d_query, d_keys, d_values = (refs[i : 6 : 3] for i in range(3))
    refs = refs[6:]
    weights = [refs[i * pieces : (i + 1) * pieces] for i in range(3)]
    refs = refs[3 * pieces :]
    d_content, d_state = refs[:2]
    if pieces == 2:
        kept, full, tree, sems, grad_sems = refs[2:4], *refs[4:]
    else:
        tree_out, full, tree, sems, grad_sems = refs[2:]
    copies = [weight_copies(weights[i], full.at[i], sems, i * pieces, scalars[0]) for i in range(3)]
    for group in copies:
        for copy in group:
            copy.start()
    block = d_mid_in.shape[1] // 2
    tree[...] = jnp.zeros(tree.shape, tree.dtype)
    for group in copies[1:]:
        for copy in group:
            copy.wait()
    span = slots * run
    micro_count = d_mid_in.shape[0] // (2 * run)
    for micro in range(micro_count):
        at = slice(micro * span, (micro + 1) * span)
        shares = mm_nt(jnp.concatenate([entry[at, :] for entry in d_keys], axis=1), full[1])
        shares = shares + mm_nt(jnp.concatenate([entry[at, :] for entry in d_values], axis=1), full[2])
        for slot in range(slots):
            relative = found[micro * slots + slot]
            for half in range(2):
                piece = shares[slot * run : (slot + 1) * run, half * block : (half + 1) * block]
                start = (half * micro_count + micro) * run
                spot = (*block_index(relative, len(tree.shape) - 2), slice(start, start + run), slice(None))
                tree[spot] = (tree[spot].astype(f32) + piece).astype(low)
    if pieces == 2:
        last_copies = []
        for part, (start, height) in enumerate(tree_cuts(tree.shape[-2])):
            for which in range(2):
                source = tree.at[(*half_at(routes_out[part][0], which, 4), pl.ds(start, height), slice(None))]
                target = kept[which].at[(*(slice(None),) * 3, pl.ds(start, height), slice(None))]
                last_copies.append(pltpu.make_async_copy(source, target, grad_sems.at[2 * part + which]))
    else:
        last_copies = [pltpu.make_async_copy(tree, tree_out, grad_sems.at[0])]
    for copy in last_copies:
        copy.start()
    for copy in copies[0]:
        copy.wait()
    d_both = d_mid_in[...] + mm_nt(jnp.concatenate([entry[...] for entry in d_query], axis=1), full[0])
    for micro in range(micro_count):
        start = 2 * run * micro
        d_content[micro] = d_both[start : start + run]
        d_state[micro] = d_both[start + run : start + 2 * run]
    for copy in last_copies:
        copy.wait()


def collect_pieces(refs, held, sems):
    copies = []
    for part, route in enumerate(routes_out):
        for which in range(2):
            at = 2 * part + which
            target = held[part].at[(*half_index(route[0], which, 4), slice(None), slice(None))]
            copies.append(pltpu.make_async_copy(refs[at], target, sems.at[at]))
    for copy in copies:
        copy.start()
    for copy in copies:
        copy.wait()


def feed_spread_kernel(scalars, *refs):
    outer, inner, first, second, third, sems = refs[6:]
    collect_pieces(refs[:6], (first, second, third), sems)
    place = scalars[1]
    height, side = first.shape[-2:]
    total = 3 * height // 2
    for chunk in range(16):
        at = block_index(chunk ^ place, 4)
        down, across = (chunk // 2) * total, (chunk % 2) * side
        outer[down : down + height, across : across + side] = first[at].astype(f32)
        middle = second[at].astype(f32)
        outer[down + height : down + total, across : across + side] = middle[: total - height]
        down, across = (chunk // 8) * total, (chunk % 8) * side
        inner[down : down + total - height, across : across + side] = middle[total - height :]
        inner[down + total - height : down + total, across : across + side] = third[at].astype(f32)


def later_spread_kernel(scalars, *refs):
    weights, inner_bias, vectors, embed, table, sources, sems = refs[6:10], refs[10], refs[11:18], *refs[18:20], refs[20:23], refs[23]
    collect_pieces(refs[:6], sources, sems)
    place = scalars[1]
    side = sources[0].shape[-1]
    rows = weights[0].shape[0] // 8
    cuts = later_cuts(2 * side)
    for chunk in range(16):
        at = block_index(chunk ^ place, 4)
        down, across = (chunk // 2) * rows, (chunk % 2) * side
        for source, (start, height) in zip(sources, cuts):
            value = source[at].astype(f32)
            for which in range(4):
                begin, end = max(start, which * rows), min(start + height, (which + 1) * rows)
                if begin < end:
                    top = down + begin - which * rows
                    weights[which][top : top + end - begin, across : across + side] = value[begin - start : end - start]
            begin = 4 * rows
            if start <= begin < start + height:
                line = value[begin - start : begin - start + 1]
                if chunk < 4:
                    inner_bias[chunk * side : (chunk + 1) * side] = line.reshape(side)
                elif chunk < 11:
                    vectors[chunk - 4][...] = line.reshape(side)
                elif chunk < 13:
                    embed[chunk - 11 : chunk - 10, :] = line
                elif chunk == 13:
                    table[...] = value[begin - start : begin - start + table.shape[0], : table.shape[1]]


routes_out = ((0, 1, 2), (1, 2, 0), (2, 0, 1))


def send(inputs, bit):
    count = lax.axis_size("dp")
    return lax.ppermute(inputs, "dp", [(i, i ^ (1 << bit)) for i in range(count)])


def half_dims(bit):
    return tuple(1 if i == bit_total() - 1 - bit else 2 for i in range(bit_total()))


def bit_total():
    return lax.axis_size("dp").bit_length() - 1


def extra_bits():
    return tuple(range(3, bit_total()))


def grow(held, bit):
    return jnp.concatenate([held, send(held, bit)], axis=bit_total() - 1 - bit)


def part_of(held, bit, which):
    total = bit_total()
    if held.ndim == 3:
        held = held.reshape((2,) * total + held.shape[1:])
    return lax.slice_in_dim(held, which, which + 1, axis=total - 1 - bit)


def scatter_rest(held, route):
    for bit in route + extra_bits()[::-1]:
        held = part_of(held, bit, 0) + send(part_of(held, bit, 1), bit)
    return held.reshape(held.shape[-2:])


def scatter_blocks(blocks, route):
    held = part_of(blocks, route[0], 0) + send(part_of(blocks, route[0], 1), route[0])
    return scatter_rest(held, route[1:])


def axis_of(bit):
    return bit_total() - 1 - bit


def sum_rounds(lower, upper, keep):
    ready = yield list(upper)
    held = [own + send(entry, route[0]) for own, entry, route in zip(lower, ready, routes_out)]
    for step in (1, 2):
        ready = yield [part_of(entry, route[step], 1) for entry, route in zip(held, routes_out)]
        held = [
            part_of(entry, route[step], 0) + send(other, route[step])
            for entry, other, route in zip(held, ready, routes_out)
        ]
    (far,) = extra_bits()
    both = [[part_of(entry, far, which) for entry in held] for which in range(2)]
    leaving = [entry[..., :rows, :] for which in range(2) for entry, rows in zip(both[which], keep)]
    leaving += [entry[..., rows:, :] for entry, rows in zip(both[1], keep) if rows < entry.shape[-2]]
    (ready,) = yield [jnp.concatenate(leaving, axis=-2)]
    arrived, start, received = send(ready, far), 0, []
    for entry in leaving:
        received.append(arrived[..., start : start + entry.shape[-2], :])
        start += entry.shape[-2]
    count = len(keep)
    shares = [
        entry[..., rows:, :] + other for entry, rows, other in zip(both[0], keep, received[2 * count :])
    ]
    held = [
        jnp.concatenate(
            [both[0][i][..., :rows, :] + received[count + i], both[1][i][..., :rows, :] + received[i]],
            axis=axis_of(far),
        )
        for i, rows in enumerate(keep)
    ]
    for step in (2, 1):
        ready = yield held
        held = [
            jnp.concatenate([entry, send(entry, route[step])], axis=axis_of(route[step]))
            for entry, route in zip(ready, routes_out)
        ]
    ready = yield held
    arrived = [send(entry, route[0]) for entry, route in zip(ready, routes_out)]
    return [piece for pair in zip(ready, arrived) for piece in pair], shares


class Rounds:
    def __init__(self, steps):
        self.steps = steps
        self.pending = next(steps)
        self.result = None

    def advance(self, ready):
        try:
            self.pending = self.steps.send(ready)
        except StopIteration as stop:
            self.pending, self.result = [], stop.value


def advance_after(group, other):
    joined = lax.optimization_barrier(list(group.pending) + list(other.pending))
    group.advance(joined[: len(group.pending)])


def advance_free(pending, others):
    joined = lax.optimization_barrier(list(pending) + list(others))
    return joined[: len(pending)], joined[len(pending) :]


def spread_dims(held, route):
    return jnp.expand_dims(held, axis_of(route[0]))


def advance_together(groups, others=()):
    joined = [entry for group in groups for entry in group.pending] + list(others)
    joined = lax.optimization_barrier(joined)
    for group in groups:
        count = len(group.pending)
        ready, joined = joined[:count], joined[count:]
        group.advance(ready)
    return joined


def shards(
    content,
    query_state,
    token_seg,
    positions,
    parent,
    w_query,
    w_key,
    w_value,
    w_out,
    w_inner,
    w_outer,
    b_inner,
    b_outer,
    gain_attn,
    bias_attn,
    gain_ffn,
    bias_ffn,
    bias_content,
    bias_segment,
    seg_embed,
    rel_table,
    cot_content,
    cot_query,
):
    micro_count, run, model = content.shape
    shard_count, dp_count = lax.axis_size("shard"), lax.axis_size("dp")
    shard, place = lax.axis_index("shard"), lax.axis_index("dp")
    heads = rel_table.shape[1]
    bucket_total = rel_table.shape[0] * shard_count
    hidden = w_inner.shape[1]
    pairs = heads // 2
    per_run = dp_count // tree_runs
    slots = path_runs * per_run
    span = slots * run
    rows_total = 2 * run * micro_count
    pieces = 2 if shard_count == 2 and dp_count == tree_runs else 1
    part_width = model // shard_count

    def fetch(weight):
        if pieces == 2:
            return [weight, lax.ppermute(weight, "shard", [(0, 1), (1, 0)])]
        return [lax.all_gather(weight, "shard", axis=0, tiled=True)]

    own_seg = token_seg[:, 0]
    own_slot = positions[:, 0] // run
    facts = jnp.stack([own_seg, own_slot], axis=1).reshape(2 * micro_count, 1).astype(low)
    fact_rows = jnp.broadcast_to(jnp.pad(facts, ((0, 16 - 2 * micro_count), (0, 0))), (16, model))
    third = model // 3
    columns = ((0, third), (third, third), (2 * third, third))
    content_rows = micro_count * run
    block = jnp.concatenate([content.reshape(content_rows, model), fact_rows], axis=0)
    total_bits = bit_total()
    block, b_inner, b_outer, parent, seg_embed, w_query, w_key, cot_content = lax.optimization_barrier(
        (block, b_inner, b_outer, parent, seg_embed, w_query, w_key, cot_content)
    )
    held = block.reshape((1,) * total_bits + block.shape)
    for bit in extra_bits():
        held = grow(held, bit)
    query_weights, key_weights = fetch(w_query), fetch(w_key)
    inner_rows = b_inner.shape[0] // part_width
    flat = [b_inner, b_outer, gain_attn, bias_attn, gain_ffn, bias_ffn, bias_content, bias_segment]
    flat += [seg_embed.reshape(-1), rel_table.reshape(-1)]
    fill = 16 * part_width - sum(entry.size for entry in flat)
    small_parts = jnp.concatenate(flat + [jnp.zeros((fill,), low)]).reshape(16, part_width)
    parts = []
    for part, (start, width) in enumerate(columns):
        height = block.shape[0] if part == 0 else content_rows
        parts.append(held[..., :height, start : start + width])
    parts, (query_weights[-1], key_weights[-1], w_value, small_parts, parent, content, cot_query) = advance_free(
        parts, [query_weights[-1], key_weights[-1], w_value, small_parts, parent, content, cot_query]
    )
    value_weights = fetch(w_value)
    first_branch, first_leaf = trunk_runs * per_run, (trunk_runs + 1) * per_run
    mine = own_seg
    above = jnp.sum(jnp.where(jnp.arange(parent.shape[2]) == mine[:, None], parent[:, 0], 0), axis=1)
    trunk, leaf = mine == 0, mine > trunk_runs
    branch = jnp.where(leaf, above, mine)
    lo = jnp.where(trunk, 0, jnp.where(leaf, first_leaf, first_branch)) * run
    hi = jnp.where(trunk, first_branch, jnp.where(leaf, slots, first_leaf)) * run
    early = jnp.stack([shard, place]).astype(jnp.int32)
    facts_own = jnp.stack([own_slot * run, lo, hi, mine, branch], axis=1)
    scalars = jnp.concatenate([early, facts_own.reshape(-1)]).astype(jnp.int32)

    rows = jnp.concatenate([content, query_state], axis=1).reshape(rows_total, model)
    cotangent = jnp.concatenate([cot_content, cot_query], axis=1).reshape(rows_total, model)
    if pieces == 2:
        other = lax.ppermute(small_parts, "shard", [(0, 1), (1, 0)])
        gathered = jnp.where(shard == 0, jnp.stack([small_parts, other]), jnp.stack([other, small_parts]))
    else:
        gathered = lax.all_gather(small_parts, "shard", axis=0, tiled=False)
    gathered = gathered.astype(f32)
    parts = [grow(piece, route[2]) for piece, route in zip(parts, routes_out)]
    parts, (value_weights[-1], w_out, w_inner, gathered, scalars, rows, cotangent) = advance_free(
        parts, [value_weights[-1], w_out, w_inner, gathered, scalars, rows, cotangent]
    )
    inner_weights, out_weights = fetch(w_inner), fetch(w_out)
    inner_bias = gathered[:, :inner_rows].reshape(1, hidden)
    vectors = jnp.transpose(gathered, (1, 0, 2)).reshape(16, model)
    table = gathered[:, 13, : rel_table.size].reshape(bucket_total, heads)

    parts = [grow(piece, route[1]) for piece, route in zip(parts, routes_out)]
    parts, (out_weights[-1], inner_weights[-1], w_outer, vectors, inner_bias, table) = advance_free(
        parts, [out_weights[-1], inner_weights[-1], w_outer, vectors, inner_bias, table]
    )
    outer_weights = fetch(w_outer)
    tree_parts = [entry for piece, route in zip(parts, routes_out) for entry in (piece, send(piece, route[0]))]
    tree_parts, (outer_weights[-1],) = advance_free(tree_parts, [outer_weights[-1]])

    grown = pltpu.CompilerParams(vmem_limit_bytes=vmem_bytes)

    def shape(dims, kind):
        return jax.ShapeDtypeStruct(dims, kind)

    dma = pltpu.SemaphoreType.DMA
    query_low, query_segment = pl.pallas_call(
        functools.partial(query_kernel, pieces),
        out_shape=(shape((rows_total, model), low),) * 2,
        in_specs=[smem_space, vmem_space, vmem_space] + [any_space] * pieces,
        out_specs=(vmem_space,) * 2,
        scratch_shapes=[pltpu.VMEM((model, model), low), dma((pieces,))],
        compiler_params=grown,
        name="query_projection",
        cost_estimate=cost(1),
    )(early, rows, vectors, *query_weights)

    def blocks_at(first):
        return (
            pl.BlockSpec((rows_total, 128), lambda pair: (0, pair + first)),
            pl.BlockSpec((micro_count * span, 128), lambda pair: (0, pair + first)),
            pl.BlockSpec((micro_count, 4 * run, span), lambda pair: (pair + first, 0, 0)),
            pl.BlockSpec((16, 128), lambda pair: (0, pair + first)),
        )

    row_block, key_block, prob_block, vector_block = blocks_at(0)
    half = model // 2
    if pieces == 2:
        grad_shapes = [shape((2,) * (total_bits - 1) + (half, half), low)] * 4
        grad_specs = [any_space] * len(grad_shapes)
        grad_scratch = [pltpu.VMEM((2,) * (1 + total_bits) + (half, half), low)]
    else:
        grad_shapes = [shape((hidden, model), low), shape((model, hidden), low)]
        grad_specs = [vmem_space] * 2
        grad_scratch = []
    path, keys, values, probs, found, attended, *results = pl.pallas_call(
        functools.partial(forward_kernel, pieces, columns, [route[0] for route in routes_out], run, slots),
        out_shape=[
            shape((micro_count, span, model), low),
            shape((micro_count * span, model), low),
            shape((micro_count * span, model), low),
            shape((pairs * micro_count, 4 * run, span), low),
            shape((micro_count * slots,), jnp.int32),
            shape((rows_total, model), f32),
            shape((micro_count, run, model), low),
            shape((micro_count, run, model), low),
            shape((rows_total, model), f32),
            shape((rows_total, model), low),
            shape((rows_total, model), low),
            shape((16, model), f32),
        ]
        + grad_shapes,
        in_specs=[smem_space] * 2 + [vmem_space] * 6 + [any_space] * (2 * len(columns) + 5 * pieces),
        out_specs=[any_space] * 4 + [smem_space] + [vmem_space] * 7 + grad_specs,
        scratch_shapes=[
            pltpu.VMEM((micro_count, span, model), low),
            pltpu.VMEM((micro_count * span, model), low),
            pltpu.VMEM((micro_count * span, model), low),
            pltpu.VMEM((pairs * micro_count, 4 * run, span), low),
            pltpu.VMEM((model, model), low),
            pltpu.VMEM((model, model), low),
            pltpu.VMEM((2,) * total_bits + (content_rows + 16, model), low),
            dma((4,)),
            dma((2 * pieces,)),
            dma((2 * len(columns),)),
            pltpu.VMEM((model, model), low),
            pltpu.VMEM((model, hidden), low),
            pltpu.VMEM((hidden, model), low),
            pltpu.VMEM((rows_total, hidden), low),
            pltpu.VMEM((rows_total, hidden), f32),
        ]
        + grad_scratch
        + [dma((3 * pieces,))]
        + ([dma((12,))] if pieces == 2 else []),
        compiler_params=grown,
        name="forward",
        cost_estimate=cost(36),
    )(
        scalars,
        table,
        query_low,
        query_segment,
        rows,
        cotangent,
        vectors,
        inner_bias,
        *tree_parts,
        *key_weights,
        *value_weights,
        *out_weights,
        *inner_weights,
        *outer_weights,
    )
    path = path.reshape(micro_count * span, model)
    out_content, out_query, d_mid_in, d_branch, d_att, small_first = results[:6]

    swap = [(0, 1), (1, 0)]
    if pieces == 2:
        feed_grads = results[6:]
        feed_other = [lax.ppermute(entry, "shard", swap) for entry in (feed_grads[3], feed_grads[2])]

    def attend_back(first, pair_count, gradient):
        rows_in, keys_in, probs_in, vector_in = blocks_at(first)
        return pl.pallas_call(
            functools.partial(back_kernel, run, slots),
            grid=(pair_count,),
            out_shape=(
                shape((rows_total, 128 * pair_count), low),
                shape((micro_count * span, 128 * pair_count), low),
                shape((micro_count * span, 128 * pair_count), low),
                shape((8, 128 * pair_count), f32),
                shape((2 * pair_count, 16, span), f32),
            ),
            in_specs=[smem_space, rows_in, rows_in, keys_in, keys_in, probs_in, rows_in, rows_in, vector_in],
            out_specs=(
                row_block,
                key_block,
                key_block,
                pl.BlockSpec((8, 128), lambda pair: (0, pair)),
                pl.BlockSpec((2, 16, span), lambda pair: (pair, 0, 0)),
            ),
            compiler_params=grown,
            name="attend_back",
            cost_estimate=cost(3),
        )(scalars, query_low, query_segment, keys, values, probs, gradient, attended, vectors)

    back_first = attend_back(0, pairs // 3, d_att)
    if pieces == 2:
        sizes = [height for _, height in feed_cuts(pieces, model)]
        upper = [
            spread_dims(feed_grads[1][..., start : start + height, :] + feed_other[0][..., start : start + height, :], route)
            for (start, height), route in zip(feed_cuts(pieces, model), routes_out)
        ]
        feed_lower = feed_other[1]
        *upper, feed_lower, d_att, _ = lax.optimization_barrier((*upper, feed_lower, d_att, back_first[0]))
        lower = [
            spread_dims(feed_grads[0][..., start : start + height, :] + feed_lower[..., start : start + height, :], route)
            for (start, height), route in zip(feed_cuts(pieces, model), routes_out)
        ]
        feed_rounds = Rounds(sum_rounds(lower, upper, sizes))
        feed_rounds.advance(feed_rounds.pending)
    back_second = attend_back(pairs // 3, pairs - pairs // 3, d_att)
    tree_height = 2 * micro_count * run
    if pieces == 2:
        whole = later_cuts(model)[-1][0] + later_cuts(model)[-1][1]
        heights = [entry[1] for entry in later_cuts(model)]
        cube = (2,) * (total_bits - 1)
        grad_shapes = [shape(cube + (whole, half), low)] * 4
        grad_specs = [any_space] * 4
        extra = [pltpu.VMEM((2,) * (1 + total_bits) + (whole, half), low), dma((12,))]
        tree_shapes = [shape(cube + (tree_height, half), low)] * 2
    else:
        grad_shapes = [shape((model, model), low)] * 4 + [shape((32, model), f32)]
        grad_specs = [vmem_space] * 5
        extra = []
        tree_shapes = [shape((2,) * total_bits + (tree_height, half), low)]
    later = pl.pallas_call(
        functools.partial(weights_kernel, pieces),
        out_shape=grad_shapes,
        in_specs=[smem_space] + [vmem_space] * 15,
        out_specs=grad_specs,
        scratch_shapes=extra,
        compiler_params=grown,
        name="weight_gradients",
        cost_estimate=cost(3),
    )(scalars, rows, path, attended, d_branch, small_first, *back_first, *back_second)
    if pieces == 2:
        feed_rounds.pending, later = advance_free(feed_rounds.pending, later)
        feed_rounds.pending, (d_mid_in,) = advance_free(feed_rounds.pending, [d_mid_in])
        feed_rounds.advance(feed_rounds.pending)
    d_content, grad_query, *tree_grads = pl.pallas_call(
        functools.partial(tree_kernel, pieces, run, slots),
        out_shape=[shape((micro_count, run, model), f32)] * 2 + tree_shapes,
        in_specs=[smem_space] * 2 + [vmem_space] * 7 + [any_space] * (3 * pieces),
        out_specs=[vmem_space] * 2 + [any_space] * len(tree_shapes),
        scratch_shapes=[
            pltpu.VMEM((3, model, model), low),
            pltpu.VMEM((2,) * total_bits + (tree_height, half), low),
            dma((3 * pieces,)),
            dma((6,)),
        ],
        compiler_params=grown,
        name="tree_gradients",
        cost_estimate=cost(3),
    )(scalars, found, d_mid_in, *back_first[:3], *back_second[:3], *query_weights, *key_weights, *value_weights)

    if pieces == 2:
        others = [lax.ppermute(entry, "shard", swap) for entry in (later[3], later[2])]
        feed_rounds.pending, others = advance_free(feed_rounds.pending, others)
        feed_rounds.pending, tree_grads = advance_free(feed_rounds.pending, tree_grads)
        feed_rounds.advance(feed_rounds.pending)

        def route_sum(which, part):
            start, height = later_cuts(model)[part]
            more, tall = tree_cuts(tree_height)[part]
            mine, other = later[which][..., start : start + height, :], others[1 - which][..., start : start + height, :]
            more_rows = tree_grads[which][..., more : more + tall, :]
            return spread_dims(jnp.concatenate([mine + other, more_rows], axis=-2), routes_out[part])

        lower = [route_sum(0, part) for part in range(3)]
        upper = [route_sum(1, part) for part in range(3)]
        later_rounds = Rounds(sum_rounds(lower, upper, heights))
        for _ in range(4):
            advance_together([feed_rounds, later_rounds])
        advance_together([later_rounds])
        feed_done = advance_together([later_rounds], feed_rounds.result[0])
        advance_together([later_rounds])

        def pieces_scratch(sizes):
            return [pltpu.VMEM((2,) * total_bits + (height, half), low) for height in sizes] + [dma((6,))]

        grad_w_outer, grad_w_inner = pl.pallas_call(
            feed_spread_kernel,
            out_shape=(shape(w_outer.shape, f32), shape(w_inner.shape, f32)),
            in_specs=[smem_space] + [any_space] * 6,
            out_specs=(vmem_space,) * 2,
            scratch_shapes=pieces_scratch([height for _, height in feed_cuts(pieces, model)]),
            compiler_params=grown,
            name="feed_spread",
            cost_estimate=cost(7),
        )(early, *feed_done)
        later_done, shares = later_rounds.result
        arrived = [share.reshape(share.shape[-2:]) for share in shares]
        tree_grad = jnp.concatenate(arrived, axis=0)
        spread_out = pl.pallas_call(
            later_spread_kernel,
            out_shape=[shape(w_query.shape, f32)] * 4
            + [shape(b_inner.shape, f32)]
            + [shape(b_outer.shape, f32)] * 7
            + [shape(seg_embed.shape, f32), shape(rel_table.shape, f32)],
            in_specs=[smem_space] + [any_space] * 6,
            out_specs=[vmem_space] * 14,
            scratch_shapes=pieces_scratch(heights),
            compiler_params=grown,
            name="later_spread",
            cost_estimate=cost(4),
        )(early, *later_done)
        grad_w_query, grad_w_key, grad_w_value, grad_w_out, grad_b_inner, *narrow, grad_rel_table = spread_out
    else:
        totals = []
        for entry in (*results[6:8], *later[:4]):
            share = lax.psum_scatter(entry, "shard", scatter_dimension=0, tiled=True)
            totals.append(lax.psum(share, "dp").astype(f32))
        grad_w_outer, grad_w_inner, grad_w_query, grad_w_key, grad_w_value, grad_w_out = totals
        tree_grad = scatter_blocks(tree_grads[0], routes_out[0])
        small = lax.psum(later[4], ("shard", "dp"))
        grad_b_inner = lax.dynamic_slice_in_dim(small[:4].reshape(-1), shard * b_inner.shape[0], b_inner.shape[0])
        narrow = lax.dynamic_slice_in_dim(small[4:13], shard * part_width, part_width, axis=1)
        narrow = [*narrow[:7], narrow[7:9]]
        grad_rel_table = lax.dynamic_slice_in_dim(
            small[16 : 16 + bucket_total, :heads], shard * rel_table.shape[0], rel_table.shape[0], axis=0
        )
    halves = tree_grad.astype(f32).reshape(2, micro_count, run, half)
    grad_content = d_content + jnp.concatenate([halves[0], halves[1]], axis=-1)
    return (
        out_content,
        out_query,
        grad_content,
        grad_query,
        grad_w_query,
        grad_w_key,
        grad_w_value,
        grad_w_out,
        grad_w_inner,
        grad_w_outer,
        grad_b_inner,
        narrow[0],
        narrow[1],
        narrow[2],
        narrow[3],
        narrow[4],
        narrow[5],
        narrow[6],
        narrow[7],
        grad_rel_table,
    )


def solution(mesh):
    rows = P(None, ("shard", "dp"), None)
    tokens = P(None, ("shard", "dp"))
    matrix = P("shard", None)
    vector = P("shard")
    return jax.shard_map(
        shards,
        mesh=mesh,
        in_specs=(rows, rows, tokens, tokens, P(None, "shard", None))
        + (matrix,) * 6
        + (vector,) * 8
        + (P(None, "shard"), matrix, rows, rows),
        out_specs=(rows,) * 4 + (matrix,) * 6 + (vector,) * 8 + (P(None, "shard"), matrix),
        check_vma=False,
    )
```

```python
import functools

import jax
import jax.numpy as jnp
from jax import lax
from jax.experimental import pallas as pl
from jax.experimental.pallas import tpu as pltpu
from jax.sharding import PartitionSpec as P

thresholds = (1, 2, 4, 8, 32, 128, 512)
norm_eps = 1e-05
masked_score = -1e30
path_runs = 6
trunk_runs = 4
tree_runs = 16
vmem_bytes = 60 * 1024 * 1024
low = jnp.bfloat16
f32 = jnp.float32
def cost(microseconds):
    return pl.CostEstimate(flops=int(microseconds * 1e9), bytes_accessed=0, transcendentals=0)


any_space = pl.BlockSpec(memory_space=pl.ANY)
smem_space = pl.BlockSpec(memory_space=pltpu.SMEM)
vmem_space = pl.BlockSpec(memory_space=pltpu.VMEM)


def mm(left, right):
    return lax.dot_general(left, right, (((1,), (0,)), ((), ())), preferred_element_type=f32)


def mm_nt(left, right):
    return lax.dot_general(left, right, (((1,), (1,)), ((), ())), preferred_element_type=f32)


def mm_tn(left, right):
    return lax.dot_general(left, right, (((0,), (0,)), ((), ())), preferred_element_type=f32)


def weight_copies(pieces, target, sems, first, shard):
    if len(pieces) == 1:
        return [pltpu.make_async_copy(pieces[0], target, sems.at[first])]
    half = pieces[0].shape[0]
    own = pl.multiple_of(shard * half, 16)
    other = pl.multiple_of((1 - shard) * half, 16)
    return [
        pltpu.make_async_copy(pieces[0], target.at[pl.ds(own, half)], sems.at[first]),
        pltpu.make_async_copy(pieces[1], target.at[pl.ds(other, half)], sems.at[first + 1]),
    ]


def scalar_at(scalars, micro, entry):
    return scalars[2 + 5 * micro + entry]


def block_index(at, total):
    return tuple((at >> (total - 1 - i)) & 1 for i in range(total))


def half_index(bit, which, total):
    everything = [slice(None)] * total
    everything[total - 1 - bit] = pl.ds(which, 1)
    return tuple(everything)


def half_at(bit, which, total):
    everything = [slice(None)] * total
    everything[total - 1 - bit] = which
    return tuple(everything)


def query_kernel(pieces, scalars, rows, vectors, *refs):
    weights = refs[:pieces]
    query_low, query_segment, full, sems = refs[pieces:]
    copies = weight_copies(weights, full, sems, 0, scalars[0])
    for copy in copies:
        copy.start()
    for copy in copies:
        copy.wait()
    raw = mm(rows[...], full[...])
    query_low[...] = (raw + vectors[9:10, :]).astype(low)
    query_segment[...] = (raw + vectors[10:11, :]).astype(low)


def keys_kernel(pieces, columns, lasts, run, slots, scalars, *refs):
    parts = refs[: 2 * len(columns)]
    refs = refs[2 * len(columns) :]
    key_weights, value_weights = refs[:pieces], refs[pieces : 2 * pieces]
    path, keys, values, found, full_key, full_value, tree, sems, tree_sems, prefetch = refs[2 * pieces :]
    shard = scalars[0]
    total = len(tree.shape) - 2
    moves = []
    for part, (start, width) in enumerate(columns):
        for which in range(2):
            source = parts[2 * part + which]
            target = tree.at[
                (*half_index(lasts[part], which, total), pl.ds(0, source.shape[-2]), pl.ds(start, width))
            ]
            moves.append(pltpu.make_async_copy(source, target, tree_sems.at[2 * part + which]))
    copies = weight_copies(key_weights, full_key, sems, 0, shard)
    copies = copies + weight_copies(value_weights, full_value, sems, pieces, shard)
    for copy in moves + copies:
        copy.start()
    for copy in moves:
        copy.wait()
    prefetch()
    micro_count = path.shape[0]
    content_rows = micro_count * run
    facts = [
        tree[(*block_index(block, total), slice(content_rows, content_rows + 16), slice(0, 128))].astype(f32)
        for block in range(1 << total)
    ]
    numbers = lax.broadcasted_iota(jnp.int32, (1 << total, 128), 0)
    for micro in range(micro_count):
        segs = jnp.concatenate([entry[2 * micro : 2 * micro + 1] for entry in facts], axis=0).astype(jnp.int32)
        places = jnp.concatenate([entry[2 * micro + 1 : 2 * micro + 2] for entry in facts], axis=0).astype(jnp.int32)
        for slot in range(slots):
            if slot < slots // path_runs * trunk_runs:
                wanted = 0
            else:
                wanted = scalar_at(scalars, micro, 4 if slot < slots // path_runs * (trunk_runs + 1) else 3)
            shown = (segs == wanted) & (places == slot)
            relative = jnp.max(jnp.where(shown, numbers, 0))
            found[micro * slots + slot] = relative
            at = block_index(relative, total)
            path[micro, slot * run : (slot + 1) * run, :] = tree[(*at, slice(micro * run, (micro + 1) * run), slice(None))]
    for copy in copies:
        copy.wait()
    for micro in range(micro_count):
        rows = path[micro]
        span = slots * run
        keys[micro * span : (micro + 1) * span, :] = mm(rows, full_key[...]).astype(low)
        values[micro * span : (micro + 1) * span, :] = mm(rows, full_value[...]).astype(low)


def start_all(groups):
    for group in groups:
        for copy in group:
            copy.start()


def forward_kernel(pieces, columns, lasts, run, slots, scalars, table, *refs):
    query_low, query_segment, rows, cotangent, vectors, inner_bias = refs[:6]
    parts, refs = refs[6 : 6 + 2 * len(columns)], refs[6 + 2 * len(columns) :]
    pair_weights, feed_weights, refs = refs[: 2 * pieces], refs[2 * pieces : 5 * pieces], refs[5 * pieces :]
    path_out, keys_out, values_out, probs_out, found, attended = refs[:6]
    refs = refs[6:]
    feed_outs = refs[: 6 + (4 if pieces == 2 else 2)]
    refs = refs[len(feed_outs) :]
    path, keys, values, probs, full_key, full_value, tree, out_sems, pair_sems, tree_sems = refs[:10]
    feed_scratch = refs[10:]
    sems = feed_scratch[6] if pieces == 2 else feed_scratch[5]
    copies = [
        weight_copies(feed_weights[i * pieces : (i + 1) * pieces], feed_scratch[i], sems, i * pieces, scalars[0])
        for i in range(3)
    ]
    keys_kernel(
        pieces,
        columns,
        lasts,
        run,
        slots,
        scalars,
        *parts,
        *pair_weights,
        path,
        keys,
        values,
        found,
        full_key,
        full_value,
        tree,
        pair_sems,
        tree_sems,
        lambda: start_all(copies),
    )
    leaving = [
        pltpu.make_async_copy(path, path_out, out_sems.at[0]),
        pltpu.make_async_copy(keys, keys_out, out_sems.at[1]),
        pltpu.make_async_copy(values, values_out, out_sems.at[2]),
    ]
    for copy in leaving:
        copy.start()
    micro_count = path.shape[0]

    def attend(pair, carry):
        lanes = pl.ds(pair * 128, 128)
        attend_kernel(
            run,
            slots,
            pair,
            scalars,
            table,
            query_low.at[:, lanes],
            query_segment.at[:, lanes],
            keys.at[:, lanes],
            values.at[:, lanes],
            vectors.at[:, lanes],
            probs.at[pl.ds(pair * micro_count, micro_count)],
            attended.at[:, lanes],
        )
        return carry

    for pair in range(rows.shape[1] // 128):
        attend(pair, 0)
    leaving.append(pltpu.make_async_copy(probs, probs_out, out_sems.at[3]))
    leaving[-1].start()
    feed_kernel(
        pieces, run, copies, scalars, rows, attended, cotangent, vectors, inner_bias, *feed_outs, *feed_scratch
    )
    for copy in leaving:
        copy.wait()


def head_masks():
    lane = lax.broadcasted_iota(jnp.int32, (1, 128), 1)
    first = lane < 64
    return first, first.astype(f32).astype(low), (1.0 - first.astype(f32)).astype(low)


def stack_query(query_low, query_segment, mask_a, mask_b):
    both = jnp.concatenate([query_low, query_segment], axis=1)
    wide_a = jnp.concatenate([mask_a, mask_a], axis=1)
    wide_b = jnp.concatenate([mask_b, mask_b], axis=1)
    return jnp.concatenate([both * wide_a, both * wide_b], axis=0)


def stack_keys(keys, vectors, lo):
    row = lax.broadcasted_iota(jnp.int32, (keys.shape[0], 1), 0)
    segment = jnp.where(row >= lo, vectors[12:13, :], vectors[11:12, :]).astype(low)
    return jnp.concatenate([keys, segment], axis=1)


def offsets_of(base, run, span):
    row = lax.broadcasted_iota(jnp.int32, (run, span), 0)
    column = lax.broadcasted_iota(jnp.int32, (run, span), 1)
    return base + row - column, column


def attend_kernel(run, slots, pair, scalars, table, query_low, query_segment, keys, values, vectors, probs, attended):
    span = slots * run
    first, mask_a, mask_b = head_masks()
    for micro in range(probs.shape[0]):
        base, lo, hi = (scalar_at(scalars, micro, entry) for entry in range(3))
        rows = slice(micro * 2 * run, (micro + 1) * 2 * run)
        columns = slice(micro * span, (micro + 1) * span)
        left = stack_query(query_low[rows, :], query_segment[rows, :], mask_a, mask_b)
        right = stack_keys(keys[columns, :], vectors[...], lo)
        raw = mm_nt(left, right)
        delta, column = offsets_of(base, run, span)
        visible = column < hi
        biases = []
        for head in range(2):
            at = 2 * pair + head
            bias = jnp.full((run, span), table[0, at], f32)
            for step, threshold in enumerate(thresholds):
                if threshold < span:
                    bias = jnp.where(delta >= threshold, table[1 + step, at], bias)
                    bias = jnp.where(delta <= -threshold, table[9 + step, at], bias)
            bias = jnp.where(visible, bias, masked_score)
            biases.append(bias)
            biases.append(jnp.where(delta == 0, masked_score, bias))
        scores = raw * 0.125 + jnp.concatenate(biases, axis=0)
        peak = jnp.max(scores, axis=-1, keepdims=True)
        mass = jnp.exp(scores - peak)
        total = jnp.sum(mass, axis=-1, keepdims=True)
        probs_low = (mass * (1.0 / total)).astype(low)
        probs[micro] = probs_low
        heads = mm(probs_low, values[columns, :])
        attended[rows, :] = jnp.where(first, heads[: 2 * run], heads[2 * run :])


def norm_forward(inputs):
    centred = inputs - jnp.mean(inputs, axis=-1, keepdims=True)
    scale = lax.rsqrt(jnp.mean(centred * centred, axis=-1, keepdims=True) + norm_eps)
    return centred * scale, scale


def norm_backward(gradient, gain, normal, scale):
    d_normal = gradient * gain
    mean_first = jnp.mean(d_normal, axis=-1, keepdims=True)
    mean_second = jnp.mean(d_normal * normal, axis=-1, keepdims=True)
    return scale * (d_normal - mean_first - normal * mean_second)


def column_sum(inputs):
    return jnp.sum(inputs, axis=0, keepdims=True)


def feed_cuts(pieces, model):
    if pieces == 1:
        return ()
    step = model // 6
    return ((0, step), (step, step), (2 * step, step))


def later_cuts(model):
    whole = model // 4 + 16
    step = whole // 40 * 16
    return ((0, step), (step, step), (2 * step, whole - 2 * step))


def tree_cuts(height):
    step = height // 48 * 16 + 16
    return ((0, step), (step, step), (2 * step, height - 2 * step))


def feed_kernel(pieces, run, copies, scalars, rows, attended, cotangent, vectors, inner_bias, *refs):
    out_content, out_query, d_mid_in, d_branch_out, d_att, small = refs[:6]
    routes = feed_cuts(pieces, rows.shape[1])
    outputs = 4 if pieces == 2 else 2
    grads = refs[6 : 6 + outputs]
    full_out, full_inner, full_outer, act_low, slope = refs[6 + outputs : 11 + outputs]
    if pieces == 2:
        held, sems, grad_sems = refs[11 + outputs :]
    shard, place = scalars[0], scalars[1]
    model = rows.shape[1]
    hidden = full_inner.shape[1]
    att_low = attended[...].astype(low)
    for copy in copies[0]:
        copy.wait()
    normal_first, scale_first = norm_forward(mm(att_low, full_out[...]) + rows[...].astype(f32))
    middle = normal_first * vectors[5:6, :] + vectors[6:7, :]
    middle_low = middle.astype(low)
    for copy in copies[1]:
        copy.wait()
    wide = model
    total = None
    for start in range(0, hidden, wide):
        at = slice(start, start + wide)
        pre = mm(middle_low, full_inner[:, at]) + inner_bias[:, at]
        squared = pre * pre
        bent = jnp.tanh(0.7978845608028654 * pre * (1.0 + 0.044715 * squared))
        half = 0.5 * (1.0 + bent)
        act = (pre * half).astype(low)
        act_low[:, at] = act
        slope[:, at] = half + (0.5 * 0.7978845608028654) * pre * (1.0 - bent * bent) * (
            1.0 + (3 * 0.044715) * squared
        )
        if start == 0:
            for copy in copies[2]:
                copy.wait()
        share = mm(act, full_outer[at, :])
        total = share if total is None else total + share
    normal_second, scale_second = norm_forward(total + vectors[4:5, :] + middle)
    final = (normal_second * vectors[7:8, :] + vectors[8:9, :]).astype(low)
    for micro in range(out_content.shape[0]):
        start = 2 * run * micro
        out_content[micro] = final[start : start + run]
        out_query[micro] = final[start + run : start + 2 * run]
    d_final = cotangent[...].astype(f32)
    small[7:8, :] = column_sum(d_final * normal_second)
    small[8:9, :] = column_sum(d_final)
    d_final_in = norm_backward(d_final, vectors[7:8, :], normal_second, scale_second)
    d_outer = d_final_in.astype(low)
    small[4:5, :] = column_sum(d_outer.astype(f32))
    block = model // 2

    def hold_outer(start, value):
        if pieces == 1:
            grads[0][start : start + block, :] = value.astype(low)
            return
        half = hidden // 2
        target = (start // half) ^ shard
        for down in range(2):
            for across in range(2):
                chunk = ((start % half) // (block // 2) + down) * 2 + across
                held[(target, *block_index(chunk ^ place, 4), slice(0, block // 2), slice(None))] = value[
                    down * (block // 2) : (down + 1) * (block // 2), across * block : (across + 1) * block
                ].astype(low)

    def hold_inner(start, value):
        if pieces == 1:
            grads[1][:, start : start + block] = value.astype(low)
            return
        for quarter in range(4):
            chunk = (quarter % 2) * 8 + start // block
            held[
                ((quarter // 2) ^ shard, *block_index(chunk ^ place, 4), slice(block // 2, block), slice(None))
            ] = value[
                quarter * (block // 2) : (quarter + 1) * (block // 2), :
            ].astype(low)

    for start in range(0, hidden, block):
        hold_outer(start, mm_tn(act_low[:, start : start + block], d_outer))
    sent = []
    for part, (start, height) in enumerate(routes):
        for side in range(2):
            for which in range(2):
                rows_at = (pl.ds(start, height), slice(None))
                source = held.at[(side, *half_at(routes_out[part][0], which, 4), *rows_at)]
                target = grads[2 * side + which].at[(*(slice(None),) * 3, *rows_at)]
                sent.append(pltpu.make_async_copy(source, target, grad_sems.at[4 * part + 2 * side + which]))
    for copy in sent[:4]:
        copy.start()
    d_middle = d_final_in
    for start in range(0, hidden, block):
        at = slice(start, start + block)
        d_inner = (mm_nt(d_outer, full_outer[at, :]) * slope[:, at]).astype(low)
        summed = column_sum(d_inner.astype(f32))
        row, lane = start // model, start % model
        small[row : row + 1, lane : lane + block] = summed
        hold_inner(start, mm_tn(middle_low, d_inner))
        d_middle = d_middle + mm_nt(d_inner, full_inner[:, at])
    for copy in sent[4:]:
        copy.start()
    small[5:6, :] = column_sum(d_middle * normal_first)
    small[6:7, :] = column_sum(d_middle)
    small[9:16, :] = jnp.zeros((7, model), f32)
    d_mid = norm_backward(d_middle, vectors[5:6, :], normal_first, scale_first)
    d_mid_in[...] = d_mid
    d_branch = d_mid.astype(low)
    d_branch_out[...] = d_branch
    d_att[...] = mm_nt(d_branch, full_out[...]).astype(low)
    for copy in sent:
        copy.wait()


def back_kernel(
    run,
    slots,
    scalars,
    query_low,
    query_segment,
    keys,
    values,
    probs,
    d_att,
    attended,
    vectors,
    d_query,
    d_keys,
    d_values,
    small,
    buckets,
):
    span = slots * run
    first, mask_a, mask_b = head_masks()
    shares = jnp.zeros((8, 128), f32)
    tallies = [jnp.zeros((16, span), f32)] * 2
    for micro in range(probs.shape[0]):
        base, lo = scalar_at(scalars, micro, 0), scalar_at(scalars, micro, 1)
        rows = slice(micro * 2 * run, (micro + 1) * 2 * run)
        columns = slice(micro * span, (micro + 1) * span)
        gradient = d_att[rows, :]
        stacked = jnp.concatenate([gradient * mask_a, gradient * mask_b], axis=0)
        product = gradient.astype(f32) * attended[rows, :]
        delta_a = jnp.sum(jnp.where(first, product, 0.0), axis=-1, keepdims=True)
        delta_b = jnp.sum(jnp.where(first, 0.0, product), axis=-1, keepdims=True)
        delta_row = jnp.concatenate([delta_a, delta_b], axis=0)
        probs_low = probs[micro]
        d_probs = mm_nt(stacked, values[columns, :])
        d_scores = (probs_low.astype(f32) * (d_probs - delta_row)).astype(low)
        left = stack_query(query_low[rows, :], query_segment[rows, :], mask_a, mask_b)
        right = stack_keys(keys[columns, :], vectors[...], lo)
        d_left = mm(d_scores, right) * 0.125
        mine = jnp.concatenate([first, first], axis=1)
        d_left = jnp.where(mine, d_left[: 2 * run], d_left[2 * run :])
        d_content, d_segment = d_left[:, :128], d_left[:, 128:]
        d_query[rows, :] = (d_content + d_segment).astype(low)
        d_right = mm_tn(d_scores, left) * 0.125
        d_keys[columns, :] = d_right[:, :128].astype(low)
        d_values[columns, :] = mm_tn(probs_low, stacked).astype(low)
        row = lax.broadcasted_iota(jnp.int32, (span, 1), 0)
        d_embed = d_right[:, 128:]
        shares = shares + jnp.concatenate(
            [
                column_sum(d_content),
                column_sum(d_segment),
                column_sum(jnp.where(row >= lo, 0.0, d_embed)),
                column_sum(jnp.where(row >= lo, d_embed, 0.0)),
                jnp.zeros((4, 128), f32),
            ],
            axis=0,
        )
        delta, _ = offsets_of(base, run, span)
        exact = d_scores.astype(f32)
        for head in range(2):
            at = 2 * run * head
            both = exact[at : at + run] + exact[at + run : at + 2 * run]
            lines = [None] * 16
            lines[0] = column_sum(jnp.where(delta == 0, both, 0.0))
            for step, threshold in enumerate(thresholds):
                if threshold < span:
                    later = thresholds[step + 1] if step + 1 < len(thresholds) else span
                    above = (delta >= threshold) & (delta < later)
                    below = (delta <= -threshold) & (delta > -later)
                    lines[1 + step] = column_sum(jnp.where(above, both, 0.0))
                    lines[9 + step] = column_sum(jnp.where(below, both, 0.0))
            blank = jnp.zeros((1, span), f32)
            tallies[head] = tallies[head] + jnp.concatenate(
                [blank if entry is None else entry for entry in lines], axis=0
            )
    small[...] = shares
    for head in range(2):
        buckets[head] = tallies[head]


def columns_of(parts, at):
    pieces, start = [], 0
    for part in parts:
        low_end, high_end = max(at.start, start), min(at.stop, start + part.shape[1])
        if low_end < high_end:
            pieces.append(part[:, low_end - start : high_end - start])
        start += part.shape[1]
    return pieces[0] if len(pieces) == 1 else jnp.concatenate(pieces, axis=1)


def weights_kernel(
    pieces,
    scalars,
    rows,
    path,
    attended,
    d_branch,
    small_first,
    *refs,
):
    d_query, d_keys, d_values, small_second, tallies = (refs[i : 10 : 5] for i in range(5))
    refs = refs[10:]
    model = rows.shape[1]
    block = model // 2
    if pieces == 2:
        kept, sent, held, grad_sems = refs[:2], refs[2:4], *refs[4:]
    else:
        natural, small_out = refs[:4], refs[4]
    shard, place = scalars[0], scalars[1]
    small_rows = block // 8

    def hold(which, across, value):
        if pieces == 1:
            natural[which][:, across * block : (across + 1) * block] = value.astype(low)
            return
        spot = (slice(which * small_rows, (which + 1) * small_rows), slice(None))
        for half in range(2):
            for down in range(8):
                start = half * block + down * small_rows
                held[(half ^ shard, *block_index((down * 2 + across) ^ place, 4), *spot)] = value[
                    start : start + small_rows, :
                ].astype(low)

    for across in range(2):
        at = slice(across * block, (across + 1) * block)
        hold(0, across, mm_tn(rows[...], columns_of(d_query, at)))
        hold(1, across, mm_tn(path[...], columns_of(d_keys, at)))
        hold(2, across, mm_tn(path[...], columns_of(d_values, at)))
        hold(3, across, mm_tn(attended[...].astype(low), d_branch[:, at]))
    buckets = jnp.zeros((16, 16), f32)
    every_head = [part[head] for part in tallies for head in range(part.shape[0])]
    line = lax.broadcasted_iota(jnp.int32, every_head[0].shape, 0)
    for head, tally in enumerate(every_head):
        buckets = buckets + lax.dot_general(
            tally,
            (line == head).astype(f32),
            (((1,), (1,)), ((), ())),
            precision=lax.Precision.HIGHEST,
            preferred_element_type=f32,
        )
    if pieces == 1:
        small_out[:9, :] = small_first[:9, :]
        for across in range(2):
            small_out[9:13, across * block : (across + 1) * block] = columns_of(small_second, slice(across * block, (across + 1) * block))[:4]
        small_out[13:, :] = jnp.zeros((small_out.shape[0] - 13, model), f32)
        small_out[16:32, :16] = buckets
    else:
        last = model // 4
        for half in range(2):
            at = slice(half * block, (half + 1) * block)
            lines = [
                small_first[2 * half + i // 2 : 2 * half + i // 2 + 1, (i % 2) * block : (i % 2 + 1) * block]
                for i in range(4)
            ]
            lines += [small_first[i : i + 1, at] for i in range(4, 9)]
            late_lines = columns_of(small_second, at)
            lines += [late_lines[i : i + 1, :] for i in range(4)]
            for chunk in range(16):
                line = lines[chunk].astype(low) if chunk < 13 else jnp.zeros((1, block), low)
                spread_line = jnp.concatenate([line.astype(f32), jnp.zeros((15, block), f32)], axis=0)
                held[(half ^ shard, *block_index(chunk ^ place, 4), slice(last, last + 16), slice(None))] = spread_line.astype(low)
            wide = jnp.concatenate([buckets[8 * half : 8 * half + 8], jnp.zeros((8, 16), f32)], axis=0)
            wide = jnp.concatenate([wide, jnp.zeros((16, block - 16), f32)], axis=1)
            held[(half ^ shard, *block_index(13 ^ place, 4), slice(last, last + 16), slice(None))] = wide.astype(low)
    leaving = []
    if pieces == 2:
        for part, (start, height) in enumerate(later_cuts(model)):
            for which in range(2):
                at = 2 * part + which
                rows_at = (pl.ds(start, height), slice(None))
                for side in range(2):
                    source = held.at[(side, *half_at(routes_out[part][0], which, 4), *rows_at)]
                    target = (kept, sent)[side][which].at[(*(slice(None),) * 3, *rows_at)]
                    leaving.append(pltpu.make_async_copy(source, target, grad_sems.at[6 * side + at]))
        for copy in leaving:
            copy.start()
    for copy in leaving:
        copy.wait()


def tree_kernel(pieces, run, slots, scalars, found, d_mid_in, *refs):
    d_query, d_keys, d_values = (refs[i : 6 : 3] for i in range(3))
    refs = refs[6:]
    weights = [refs[i * pieces : (i + 1) * pieces] for i in range(3)]
    refs = refs[3 * pieces :]
    d_content, d_state = refs[:2]
    if pieces == 2:
        kept, full, tree, sems, grad_sems = refs[2:4], *refs[4:]
    else:
        tree_out, full, tree, sems, grad_sems = refs[2:]
    copies = [weight_copies(weights[i], full.at[i], sems, i * pieces, scalars[0]) for i in range(3)]
    for group in copies:
        for copy in group:
            copy.start()
    block = d_mid_in.shape[1] // 2
    tree[...] = jnp.zeros(tree.shape, tree.dtype)
    for group in copies[1:]:
        for copy in group:
            copy.wait()
    span = slots * run
    micro_count = d_mid_in.shape[0] // (2 * run)
    for micro in range(micro_count):
        at = slice(micro * span, (micro + 1) * span)
        shares = mm_nt(jnp.concatenate([entry[at, :] for entry in d_keys], axis=1), full[1])
        shares = shares + mm_nt(jnp.concatenate([entry[at, :] for entry in d_values], axis=1), full[2])
        for slot in range(slots):
            relative = found[micro * slots + slot]
            for half in range(2):
                piece = shares[slot * run : (slot + 1) * run, half * block : (half + 1) * block]
                start = (half * micro_count + micro) * run
                spot = (*block_index(relative, len(tree.shape) - 2), slice(start, start + run), slice(None))
                tree[spot] = (tree[spot].astype(f32) + piece).astype(low)
    if pieces == 2:
        last_copies = []
        for part, (start, height) in enumerate(tree_cuts(tree.shape[-2])):
            for which in range(2):
                source = tree.at[(*half_at(routes_out[part][0], which, 4), pl.ds(start, height), slice(None))]
                target = kept[which].at[(*(slice(None),) * 3, pl.ds(start, height), slice(None))]
                last_copies.append(pltpu.make_async_copy(source, target, grad_sems.at[2 * part + which]))
    else:
        last_copies = [pltpu.make_async_copy(tree, tree_out, grad_sems.at[0])]
    for copy in last_copies:
        copy.start()
    for copy in copies[0]:
        copy.wait()
    d_both = d_mid_in[...] + mm_nt(jnp.concatenate([entry[...] for entry in d_query], axis=1), full[0])
    for micro in range(micro_count):
        start = 2 * run * micro
        d_content[micro] = d_both[start : start + run]
        d_state[micro] = d_both[start + run : start + 2 * run]
    for copy in last_copies:
        copy.wait()


def collect_pieces(refs, held, sems):
    copies = []
    for part, route in enumerate(routes_out):
        for which in range(2):
            at = 2 * part + which
            target = held[part].at[(*half_index(route[0], which, 4), slice(None), slice(None))]
            copies.append(pltpu.make_async_copy(refs[at], target, sems.at[at]))
    for copy in copies:
        copy.start()
    for copy in copies:
        copy.wait()


def feed_spread_kernel(scalars, *refs):
    outer, inner, first, second, third, sems = refs[6:]
    collect_pieces(refs[:6], (first, second, third), sems)
    place = scalars[1]
    height, side = first.shape[-2:]
    total = 3 * height // 2
    for chunk in range(16):
        at = block_index(chunk ^ place, 4)
        down, across = (chunk // 2) * total, (chunk % 2) * side
        outer[down : down + height, across : across + side] = first[at].astype(f32)
        middle = second[at].astype(f32)
        outer[down + height : down + total, across : across + side] = middle[: total - height]
        down, across = (chunk // 8) * total, (chunk % 8) * side
        inner[down : down + total - height, across : across + side] = middle[total - height :]
        inner[down + total - height : down + total, across : across + side] = third[at].astype(f32)


def later_spread_kernel(scalars, *refs):
    weights, inner_bias, vectors, embed, table, small = refs[6:10], refs[10], refs[11:18], *refs[18:21]
    place = scalars[1]
    side = refs[0].shape[-1]
    rows = weights[0].shape[0] // 8
    cuts = later_cuts(2 * side)
    for relative in range(16):
        chunk = relative ^ place
        down = pl.multiple_of((chunk // 2) * rows, 16)
        across = pl.ds(pl.multiple_of((chunk % 2) * side, 128), side)
        at = block_index(relative, 4)
        for part, (start, height) in enumerate(cuts):
            axis = 3 - routes_out[part][0]
            inside = tuple(0 if i == axis else bit for i, bit in enumerate(at))
            value = refs[2 * part + at[axis]][inside].astype(f32)
            for which in range(4):
                begin, end = max(start, which * rows), min(start + height, (which + 1) * rows)
                if begin < end:
                    here = pl.ds(pl.multiple_of(down + begin - which * rows, 16), end - begin)
                    weights[which][here, across] = value[begin - start : end - start]
            begin = 4 * rows
            if start <= begin < start + height:
                small[chunk] = value[begin - start : begin - start + 16]
    for chunk in range(14):
        line = small[chunk, :1]
        if chunk < 4:
            inner_bias[chunk * side : (chunk + 1) * side] = line.reshape(side)
        elif chunk < 11:
            vectors[chunk - 4][...] = line.reshape(side)
        elif chunk < 13:
            embed[chunk - 11 : chunk - 10, :] = line
        else:
            table[...] = small[chunk, : table.shape[0], : table.shape[1]]


routes_out = ((0, 1, 2), (1, 2, 0), (2, 0, 1))


def send(inputs, bit):
    count = lax.axis_size("dp")
    return lax.ppermute(inputs, "dp", [(i, i ^ (1 << bit)) for i in range(count)])


def half_dims(bit):
    return tuple(1 if i == bit_total() - 1 - bit else 2 for i in range(bit_total()))


def bit_total():
    return lax.axis_size("dp").bit_length() - 1


def extra_bits():
    return tuple(range(3, bit_total()))


def grow(held, bit):
    return jnp.concatenate([held, send(held, bit)], axis=bit_total() - 1 - bit)


def part_of(held, bit, which):
    total = bit_total()
    if held.ndim == 3:
        held = held.reshape((2,) * total + held.shape[1:])
    return lax.slice_in_dim(held, which, which + 1, axis=total - 1 - bit)


def scatter_rest(held, route):
    for bit in route + extra_bits()[::-1]:
        held = part_of(held, bit, 0) + send(part_of(held, bit, 1), bit)
    return held.reshape(held.shape[-2:])


def scatter_blocks(blocks, route):
    held = part_of(blocks, route[0], 0) + send(part_of(blocks, route[0], 1), route[0])
    return scatter_rest(held, route[1:])


def axis_of(bit):
    return bit_total() - 1 - bit


def sum_rounds(lower, upper, keep):
    ready = yield list(upper)
    held = [own + send(entry, route[0]) for own, entry, route in zip(lower, ready, routes_out)]
    for step in (1, 2):
        ready = yield [part_of(entry, route[step], 1) for entry, route in zip(held, routes_out)]
        held = [
            part_of(entry, route[step], 0) + send(other, route[step])
            for entry, other, route in zip(held, ready, routes_out)
        ]
    (far,) = extra_bits()
    both = [[part_of(entry, far, which) for entry in held] for which in range(2)]
    leaving = [entry[..., :rows, :] for which in range(2) for entry, rows in zip(both[which], keep)]
    leaving += [entry[..., rows:, :] for entry, rows in zip(both[1], keep) if rows < entry.shape[-2]]
    (ready,) = yield [jnp.concatenate(leaving, axis=-2)]
    arrived, start, received = send(ready, far), 0, []
    for entry in leaving:
        received.append(arrived[..., start : start + entry.shape[-2], :])
        start += entry.shape[-2]
    count = len(keep)
    shares = [
        entry[..., rows:, :] + other for entry, rows, other in zip(both[0], keep, received[2 * count :])
    ]
    held = [
        jnp.concatenate(
            [both[0][i][..., :rows, :] + received[count + i], both[1][i][..., :rows, :] + received[i]],
            axis=axis_of(far),
        )
        for i, rows in enumerate(keep)
    ]
    for step in (2, 1):
        ready = yield held
        held = [
            jnp.concatenate([entry, send(entry, route[step])], axis=axis_of(route[step]))
            for entry, route in zip(ready, routes_out)
        ]
    ready = yield held
    arrived = [send(entry, route[0]) for entry, route in zip(ready, routes_out)]
    return [piece for pair in zip(ready, arrived) for piece in pair], shares


class Rounds:
    def __init__(self, steps):
        self.steps = steps
        self.pending = next(steps)
        self.result = None

    def advance(self, ready):
        try:
            self.pending = self.steps.send(ready)
        except StopIteration as stop:
            self.pending, self.result = [], stop.value


def advance_after(group, other):
    joined = lax.optimization_barrier(list(group.pending) + list(other.pending))
    group.advance(joined[: len(group.pending)])


def advance_free(pending, others):
    joined = lax.optimization_barrier(list(pending) + list(others))
    return joined[: len(pending)], joined[len(pending) :]


def spread_dims(held, route):
    return jnp.expand_dims(held, axis_of(route[0]))


def advance_together(groups, others=()):
    joined = [entry for group in groups for entry in group.pending] + list(others)
    joined = lax.optimization_barrier(joined)
    for group in groups:
        count = len(group.pending)
        ready, joined = joined[:count], joined[count:]
        group.advance(ready)
    return joined


def shards(
    content,
    query_state,
    token_seg,
    positions,
    parent,
    w_query,
    w_key,
    w_value,
    w_out,
    w_inner,
    w_outer,
    b_inner,
    b_outer,
    gain_attn,
    bias_attn,
    gain_ffn,
    bias_ffn,
    bias_content,
    bias_segment,
    seg_embed,
    rel_table,
    cot_content,
    cot_query,
):
    micro_count, run, model = content.shape
    shard_count, dp_count = lax.axis_size("shard"), lax.axis_size("dp")
    shard, place = lax.axis_index("shard"), lax.axis_index("dp")
    heads = rel_table.shape[1]
    bucket_total = rel_table.shape[0] * shard_count
    hidden = w_inner.shape[1]
    pairs = heads // 2
    per_run = dp_count // tree_runs
    slots = path_runs * per_run
    span = slots * run
    rows_total = 2 * run * micro_count
    pieces = 2 if shard_count == 2 and dp_count == tree_runs else 1
    part_width = model // shard_count

    def fetch(weight):
        if pieces == 2:
            return [weight, lax.ppermute(weight, "shard", [(0, 1), (1, 0)])]
        return [lax.all_gather(weight, "shard", axis=0, tiled=True)]

    own_seg = token_seg[:, 0]
    own_slot = positions[:, 0] // run
    facts = jnp.stack([own_seg, own_slot], axis=1).reshape(2 * micro_count, 1).astype(low)
    fact_rows = jnp.broadcast_to(jnp.pad(facts, ((0, 16 - 2 * micro_count), (0, 0))), (16, model))
    third = model // 3
    columns = ((0, third), (third, third), (2 * third, third))
    content_rows = micro_count * run
    block = jnp.concatenate([content.reshape(content_rows, model), fact_rows], axis=0)
    total_bits = bit_total()
    block, b_inner, b_outer, parent, seg_embed, w_query, w_key, cot_content = lax.optimization_barrier(
        (block, b_inner, b_outer, parent, seg_embed, w_query, w_key, cot_content)
    )
    held = block.reshape((1,) * total_bits + block.shape)
    for bit in extra_bits():
        held = grow(held, bit)
    query_weights, key_weights = fetch(w_query), fetch(w_key)
    inner_rows = b_inner.shape[0] // part_width
    flat = [b_inner, b_outer, gain_attn, bias_attn, gain_ffn, bias_ffn, bias_content, bias_segment]
    flat += [seg_embed.reshape(-1), rel_table.reshape(-1)]
    fill = 16 * part_width - sum(entry.size for entry in flat)
    small_parts = jnp.concatenate(flat + [jnp.zeros((fill,), low)]).reshape(16, part_width)
    parts = []
    for part, (start, width) in enumerate(columns):
        height = block.shape[0] if part == 0 else content_rows
        parts.append(held[..., :height, start : start + width])
    parts, (query_weights[-1], key_weights[-1], w_value, small_parts, parent, content, cot_query) = advance_free(
        parts, [query_weights[-1], key_weights[-1], w_value, small_parts, parent, content, cot_query]
    )
    value_weights = fetch(w_value)
    first_branch, first_leaf = trunk_runs * per_run, (trunk_runs + 1) * per_run
    mine = own_seg
    above = jnp.sum(jnp.where(jnp.arange(parent.shape[2]) == mine[:, None], parent[:, 0], 0), axis=1)
    trunk, leaf = mine == 0, mine > trunk_runs
    branch = jnp.where(leaf, above, mine)
    lo = jnp.where(trunk, 0, jnp.where(leaf, first_leaf, first_branch)) * run
    hi = jnp.where(trunk, first_branch, jnp.where(leaf, slots, first_leaf)) * run
    early = jnp.stack([shard, place]).astype(jnp.int32)
    facts_own = jnp.stack([own_slot * run, lo, hi, mine, branch], axis=1)
    scalars = jnp.concatenate([early, facts_own.reshape(-1)]).astype(jnp.int32)

    rows = jnp.concatenate([content, query_state], axis=1).reshape(rows_total, model)
    cotangent = jnp.concatenate([cot_content, cot_query], axis=1).reshape(rows_total, model)
    if pieces == 2:
        other = lax.ppermute(small_parts, "shard", [(0, 1), (1, 0)])
        gathered = jnp.where(shard == 0, jnp.stack([small_parts, other]), jnp.stack([other, small_parts]))
    else:
        gathered = lax.all_gather(small_parts, "shard", axis=0, tiled=False)
    gathered = gathered.astype(f32)
    parts = [grow(piece, route[2]) for piece, route in zip(parts, routes_out)]
    parts, (value_weights[-1], w_out, w_inner, gathered, scalars, rows, cotangent) = advance_free(
        parts, [value_weights[-1], w_out, w_inner, gathered, scalars, rows, cotangent]
    )
    inner_weights, out_weights = fetch(w_inner), fetch(w_out)
    inner_bias = gathered[:, :inner_rows].reshape(1, hidden)
    vectors = jnp.transpose(gathered, (1, 0, 2)).reshape(16, model)
    table = gathered[:, 13, : rel_table.size].reshape(bucket_total, heads)

    parts = [grow(piece, route[1]) for piece, route in zip(parts, routes_out)]
    parts, (out_weights[-1], inner_weights[-1], w_outer, vectors, inner_bias, table) = advance_free(
        parts, [out_weights[-1], inner_weights[-1], w_outer, vectors, inner_bias, table]
    )
    outer_weights = fetch(w_outer)
    tree_parts = [entry for piece, route in zip(parts, routes_out) for entry in (piece, send(piece, route[0]))]
    tree_parts, (outer_weights[-1],) = advance_free(tree_parts, [outer_weights[-1]])

    grown = pltpu.CompilerParams(vmem_limit_bytes=vmem_bytes)

    def granted(mebibytes):
        return pltpu.CompilerParams(vmem_limit_bytes=mebibytes * 1024 * 1024)


    def shape(dims, kind):
        return jax.ShapeDtypeStruct(dims, kind)

    dma = pltpu.SemaphoreType.DMA
    query_low, query_segment = pl.pallas_call(
        functools.partial(query_kernel, pieces),
        out_shape=(shape((rows_total, model), low),) * 2,
        in_specs=[smem_space, vmem_space, vmem_space] + [any_space] * pieces,
        out_specs=(vmem_space,) * 2,
        scratch_shapes=[pltpu.VMEM((model, model), low), dma((pieces,))],
        compiler_params=granted(16),
        name="query_projection",
        cost_estimate=cost(1),
    )(early, rows, vectors, *query_weights)

    def blocks_at(first):
        return (
            pl.BlockSpec((rows_total, 128), lambda pair: (0, pair + first)),
            pl.BlockSpec((micro_count * span, 128), lambda pair: (0, pair + first)),
            pl.BlockSpec((micro_count, 4 * run, span), lambda pair: (pair + first, 0, 0)),
            pl.BlockSpec((16, 128), lambda pair: (0, pair + first)),
        )

    row_block, key_block, prob_block, vector_block = blocks_at(0)
    half = model // 2
    if pieces == 2:
        grad_shapes = [shape((2,) * (total_bits - 1) + (half, half), low)] * 4
        grad_specs = [any_space] * len(grad_shapes)
        grad_scratch = [pltpu.VMEM((2,) * (1 + total_bits) + (half, half), low)]
    else:
        grad_shapes = [shape((hidden, model), low), shape((model, hidden), low)]
        grad_specs = [vmem_space] * 2
        grad_scratch = []
    path, keys, values, probs, found, attended, *results = pl.pallas_call(
        functools.partial(forward_kernel, pieces, columns, [route[0] for route in routes_out], run, slots),
        out_shape=[
            shape((micro_count, span, model), low),
            shape((micro_count * span, model), low),
            shape((micro_count * span, model), low),
            shape((pairs * micro_count, 4 * run, span), low),
            shape((micro_count * slots,), jnp.int32),
            shape((rows_total, model), f32),
            shape((micro_count, run, model), low),
            shape((micro_count, run, model), low),
            shape((rows_total, model), f32),
            shape((rows_total, model), low),
            shape((rows_total, model), low),
            shape((16, model), f32),
        ]
        + grad_shapes,
        in_specs=[smem_space] * 2 + [vmem_space] * 6 + [any_space] * (2 * len(columns) + 5 * pieces),
        out_specs=[any_space] * 4 + [smem_space] + [vmem_space] * 7 + grad_specs,
        scratch_shapes=[
            pltpu.VMEM((micro_count, span, model), low),
            pltpu.VMEM((micro_count * span, model), low),
            pltpu.VMEM((micro_count * span, model), low),
            pltpu.VMEM((pairs * micro_count, 4 * run, span), low),
            pltpu.VMEM((model, model), low),
            pltpu.VMEM((model, model), low),
            pltpu.VMEM((2,) * total_bits + (content_rows + 16, model), low),
            dma((4,)),
            dma((2 * pieces,)),
            dma((2 * len(columns),)),
            pltpu.VMEM((model, model), low),
            pltpu.VMEM((model, hidden), low),
            pltpu.VMEM((hidden, model), low),
            pltpu.VMEM((rows_total, hidden), low),
            pltpu.VMEM((rows_total, hidden), f32),
        ]
        + grad_scratch
        + [dma((3 * pieces,))]
        + ([dma((12,))] if pieces == 2 else []),
        compiler_params=grown,
        name="forward",
        cost_estimate=cost(36),
    )(
        scalars,
        table,
        query_low,
        query_segment,
        rows,
        cotangent,
        vectors,
        inner_bias,
        *tree_parts,
        *key_weights,
        *value_weights,
        *out_weights,
        *inner_weights,
        *outer_weights,
    )
    path = path.reshape(micro_count * span, model)
    out_content, out_query, d_mid_in, d_branch, d_att, small_first = results[:6]

    swap = [(0, 1), (1, 0)]
    if pieces == 2:
        feed_grads = results[6:]
        feed_other = [lax.ppermute(entry, "shard", swap) for entry in (feed_grads[3], feed_grads[2])]

    def attend_back(first, pair_count, gradient):
        rows_in, keys_in, probs_in, vector_in = blocks_at(first)
        return pl.pallas_call(
            functools.partial(back_kernel, run, slots),
            grid=(pair_count,),
            out_shape=(
                shape((rows_total, 128 * pair_count), low),
                shape((micro_count * span, 128 * pair_count), low),
                shape((micro_count * span, 128 * pair_count), low),
                shape((8, 128 * pair_count), f32),
                shape((2 * pair_count, 16, span), f32),
            ),
            in_specs=[smem_space, rows_in, rows_in, keys_in, keys_in, probs_in, rows_in, rows_in, vector_in],
            out_specs=(
                row_block,
                key_block,
                key_block,
                pl.BlockSpec((8, 128), lambda pair: (0, pair)),
                pl.BlockSpec((2, 16, span), lambda pair: (pair, 0, 0)),
            ),
            compiler_params=granted(24),
            name="attend_back",
            cost_estimate=cost(3),
        )(scalars, query_low, query_segment, keys, values, probs, gradient, attended, vectors)

    back_first = attend_back(0, pairs // 3, d_att)
    if pieces == 2:
        sizes = [height for _, height in feed_cuts(pieces, model)]
        upper = [
            spread_dims(feed_grads[1][..., start : start + height, :] + feed_other[0][..., start : start + height, :], route)
            for (start, height), route in zip(feed_cuts(pieces, model), routes_out)
        ]
        feed_lower = feed_other[1]
        *upper, feed_lower, d_att, _ = lax.optimization_barrier((*upper, feed_lower, d_att, back_first[0]))
        lower = [
            spread_dims(feed_grads[0][..., start : start + height, :] + feed_lower[..., start : start + height, :], route)
            for (start, height), route in zip(feed_cuts(pieces, model), routes_out)
        ]
        feed_rounds = Rounds(sum_rounds(lower, upper, sizes))
        feed_rounds.advance(feed_rounds.pending)
    back_second = attend_back(pairs // 3, pairs - pairs // 3, d_att)
    tree_height = 2 * micro_count * run
    if pieces == 2:
        whole = later_cuts(model)[-1][0] + later_cuts(model)[-1][1]
        heights = [entry[1] for entry in later_cuts(model)]
        cube = (2,) * (total_bits - 1)
        grad_shapes = [shape(cube + (whole, half), low)] * 4
        grad_specs = [any_space] * 4
        extra = [pltpu.VMEM((2,) * (1 + total_bits) + (whole, half), low), dma((12,))]
        tree_shapes = [shape(cube + (tree_height, half), low)] * 2
    else:
        grad_shapes = [shape((model, model), low)] * 4 + [shape((32, model), f32)]
        grad_specs = [vmem_space] * 5
        extra = []
        tree_shapes = [shape((2,) * total_bits + (tree_height, half), low)]
    later = pl.pallas_call(
        functools.partial(weights_kernel, pieces),
        out_shape=grad_shapes,
        in_specs=[smem_space] + [vmem_space] * 15,
        out_specs=grad_specs,
        scratch_shapes=extra,
        compiler_params=granted(40),
        name="weight_gradients",
        cost_estimate=cost(3),
    )(scalars, rows, path, attended, d_branch, small_first, *back_first, *back_second)
    if pieces == 2:
        feed_rounds.pending, later = advance_free(feed_rounds.pending, later)
        feed_rounds.pending, (d_mid_in,) = advance_free(feed_rounds.pending, [d_mid_in])
        feed_rounds.advance(feed_rounds.pending)
    d_content, grad_query, *tree_grads = pl.pallas_call(
        functools.partial(tree_kernel, pieces, run, slots),
        out_shape=[shape((micro_count, run, model), f32)] * 2 + tree_shapes,
        in_specs=[smem_space] * 2 + [vmem_space] * 7 + [any_space] * (3 * pieces),
        out_specs=[vmem_space] * 2 + [any_space] * len(tree_shapes),
        scratch_shapes=[
            pltpu.VMEM((3, model, model), low),
            pltpu.VMEM((2,) * total_bits + (tree_height, half), low),
            dma((3 * pieces,)),
            dma((6,)),
        ],
        compiler_params=granted(40),
        name="tree_gradients",
        cost_estimate=cost(3),
    )(scalars, found, d_mid_in, *back_first[:3], *back_second[:3], *query_weights, *key_weights, *value_weights)

    if pieces == 2:
        others = [lax.ppermute(entry, "shard", swap) for entry in (later[3], later[2])]
        feed_rounds.pending, others = advance_free(feed_rounds.pending, others)
        feed_rounds.pending, tree_grads = advance_free(feed_rounds.pending, tree_grads)
        feed_rounds.advance(feed_rounds.pending)

        def route_sum(which, part):
            start, height = later_cuts(model)[part]
            more, tall = tree_cuts(tree_height)[part]
            mine, other = later[which][..., start : start + height, :], others[1 - which][..., start : start + height, :]
            more_rows = tree_grads[which][..., more : more + tall, :]
            return spread_dims(jnp.concatenate([mine + other, more_rows], axis=-2), routes_out[part])

        lower = [route_sum(0, part) for part in range(3)]
        upper = [route_sum(1, part) for part in range(3)]
        later_rounds = Rounds(sum_rounds(lower, upper, heights))
        for _ in range(4):
            advance_together([feed_rounds, later_rounds])
        advance_together([later_rounds])
        feed_done = advance_together([later_rounds], feed_rounds.result[0])
        advance_together([later_rounds])

        def pieces_scratch(sizes):
            return [pltpu.VMEM((2,) * total_bits + (height, half), low) for height in sizes] + [dma((6,))]

        grad_w_outer, grad_w_inner = pl.pallas_call(
            feed_spread_kernel,
            out_shape=(shape(w_outer.shape, f32), shape(w_inner.shape, f32)),
            in_specs=[smem_space] + [any_space] * 6,
            out_specs=(vmem_space,) * 2,
            scratch_shapes=pieces_scratch([height for _, height in feed_cuts(pieces, model)]),
            compiler_params=granted(32),
            name="feed_spread",
            cost_estimate=cost(7),
        )(early, *feed_done)
        later_done, shares = later_rounds.result
        arrived = [share.reshape(share.shape[-2:]) for share in shares]
        tree_grad = jnp.concatenate(arrived, axis=0)
        spread_out = pl.pallas_call(
            later_spread_kernel,
            out_shape=[shape(w_query.shape, f32)] * 4
            + [shape(b_inner.shape, f32)]
            + [shape(b_outer.shape, f32)] * 7
            + [shape(seg_embed.shape, f32), shape(rel_table.shape, f32)],
            in_specs=[smem_space] + [vmem_space] * 6,
            out_specs=[vmem_space] * 14,
            scratch_shapes=[pltpu.VMEM((dp_count, 16, half), f32)],
            compiler_params=granted(20),
            name="later_spread",
            cost_estimate=cost(4),
        )(early, *later_done)
        grad_w_query, grad_w_key, grad_w_value, grad_w_out, grad_b_inner, *narrow, grad_rel_table = spread_out
    else:
        totals = []
        for entry in (*results[6:8], *later[:4]):
            share = lax.psum_scatter(entry, "shard", scatter_dimension=0, tiled=True)
            totals.append(lax.psum(share, "dp").astype(f32))
        grad_w_outer, grad_w_inner, grad_w_query, grad_w_key, grad_w_value, grad_w_out = totals
        tree_grad = scatter_blocks(tree_grads[0], routes_out[0])
        small = lax.psum(later[4], ("shard", "dp"))
        grad_b_inner = lax.dynamic_slice_in_dim(small[:4].reshape(-1), shard * b_inner.shape[0], b_inner.shape[0])
        narrow = lax.dynamic_slice_in_dim(small[4:13], shard * part_width, part_width, axis=1)
        narrow = [*narrow[:7], narrow[7:9]]
        grad_rel_table = lax.dynamic_slice_in_dim(
            small[16 : 16 + bucket_total, :heads], shard * rel_table.shape[0], rel_table.shape[0], axis=0
        )
    halves = tree_grad.astype(f32).reshape(2, micro_count, run, half)
    grad_content = d_content + jnp.concatenate([halves[0], halves[1]], axis=-1)
    return (
        out_content,
        out_query,
        grad_content,
        grad_query,
        grad_w_query,
        grad_w_key,
        grad_w_value,
        grad_w_out,
        grad_w_inner,
        grad_w_outer,
        grad_b_inner,
        narrow[0],
        narrow[1],
        narrow[2],
        narrow[3],
        narrow[4],
        narrow[5],
        narrow[6],
        narrow[7],
        grad_rel_table,
    )


def solution(mesh):
    rows = P(None, ("shard", "dp"), None)
    tokens = P(None, ("shard", "dp"))
    matrix = P("shard", None)
    vector = P("shard")
    return jax.shard_map(
        shards,
        mesh=mesh,
        in_specs=(rows, rows, tokens, tokens, P(None, "shard", None))
        + (matrix,) * 6
        + (vector,) * 8
        + (P(None, "shard"), matrix, rows, rows),
        out_specs=(rows,) * 4 + (matrix,) * 6 + (vector,) * 8 + (P(None, "shard"), matrix),
        check_vma=False,
    )
```
